32 devices in a mesh: rep: 16 (over z, y, core), shard: 2 (over x).
Axes of the slice: x: 2, y: 2, z: 4, core: 2. Of those that a mesh axis runs over, the one named last changes fastest.
Arguments:
- tokens: bfloat16 [2, 4096, 768], P('shard', 'rep'), may hold values from -6 to 6
- doc_ids: int32 [2, 4096], P('shard'), may hold values from 0 to 1, never falling along the last dimension, each value on 1 to 4095 neighbouring positions
- qkv_weight: bfloat16 [768, 2304], P('shard'), may hold values from -0.21875 to 0.21875
- qv_bias: bfloat16 [1536], P('shard'), may hold values from -1.796875 to 1.796875
- out_weight: bfloat16 [768, 768], P('shard'), may hold values from -2.5 to 2.5
- out_bias: bfloat16 [768], P('shard'), may hold values from -1.796875 to 1.796875
- mid_gain: bfloat16 [768], P('shard'), may hold values from 0.5 to 1.5
- mid_shift: bfloat16 [768], P('shard'), may hold values from -1.796875 to 1.796875
- up_weight: bfloat16 [768, 3072], P('shard'), may hold values from -0.21875 to 0.21875
- up_bias: bfloat16 [3072], P('shard'), may hold values from -3 to 3
- down_weight: bfloat16 [3072, 768], P('shard'), may hold values from -0.109375 to 0.109375
- down_bias: bfloat16 [768], P('shard'), may hold values from -1.796875 to 1.796875
- end_gain: bfloat16 [768], P('shard'), may hold values from 0.5 to 1.5
- end_shift: bfloat16 [768], P('shard'), may hold values from -1.796875 to 1.796875
- out_grad: bfloat16 [2, 4096, 768], P('shard', 'rep'), may hold values from -6 to 6
Outputs:
- layer_out: bfloat16 [2, 4096, 768], P('shard', 'rep')
- input_grad: bfloat16 [2, 4096, 768], P('shard', 'rep')
- grad_qkv_weight: float32 [768, 2304], P('shard')
- grad_qv_bias: float32 [1536], P('shard')
- grad_out_weight: float32 [768, 768], P('shard')
- grad_out_bias: float32 [768], P('shard')
- grad_mid_gain: float32 [768], P('shard')
- grad_mid_shift: float32 [768], P('shard')
- grad_up_weight: float32 [768, 3072], P('shard')
- grad_up_bias: float32 [3072], P('shard')
- grad_down_weight: float32 [3072, 768], P('shard')
- grad_down_bias: float32 [768], P('shard')
- grad_end_gain: float32 [768], P('shard')
- grad_end_shift: float32 [768], P('shard')
The draws below stay inside these ranges and needn't reach their ends.
Inputs may be any that keep to these rules, and one draw needn't show every extreme that they name: `doc_ids`: within a stream the document numbers never fall; each document has 1 to 4095 positions.
All inputs are finite; a program needn't handle non-finite values.
Results may differ from the reference program's by a relative error of at most 0.02.
Values may be sent and summed in bfloat16 or wider, within the bound.
A program may use at most 128 MiB of HBM per device.

```python
import math
import jax
import jax.numpy as jnp
import numpy as np
from jax import lax

D = 768
HEADS = 12
HEAD_DIM = 64
FF = 3072
BLOCK = 256
LENGTH = 4096
STREAMS = 2


def levels(key, shape, shards, least, largest):
    def one(position, parts):
        heights = jax.random.uniform(jax.random.fold_in(jax.random.fold_in(key, 6), position), (parts,), jnp.float32, least / len(shards), largest / len(shards))
        return jnp.repeat(jnp.exp(heights), shape[position] // parts).reshape((-1,) + (1,) * (len(shape) - position - 1))

    level = one(*shards[0])
    for cut in shards[1:]:
        level = level * one(*cut)
    return level


def length_profile(amount, total, most, lean):
    loads = [(1 << 20) // math.isqrt(standing ** lean) + 1 for standing in range(2, amount + 1)]
    rest, counts = total - most - (amount - 1), [1] * (amount - 1)
    while rest > 0:
        free = [i for i in range(amount - 1) if counts[i] < most]
        whole, remaining = sum([loads[i] for i in free]), rest
        for i in free:
            more = min(most - counts[i], max(1, remaining * loads[i] // whole), rest)
            counts[i] = counts[i] + more
            rest = rest - more
    return np.array([most] + counts)


def uneven_parts(rng, number_of, total, most, skew):
    if number_of == 2:
        one = jax.random.randint(rng, (), max(1, total - most), min(most, total - 1) + 1)
        return jnp.stack([one, total - one])
    tallies = jnp.asarray(length_profile(number_of, total, most, skew), jnp.int32)
    twos = (number_of - 1) // 2
    donor, sink = tallies[1:1 + 2 * twos:2], tallies[2:2 + 2 * twos:2]
    slack = jnp.minimum(donor - 1, most - sink)
    moved = jax.random.randint(jax.random.fold_in(rng, 1), (twos,), 0, 1 << 20) % (slack + 1)
    tallies = tallies.at[1:1 + 2 * twos:2].set(donor - moved).at[2:2 + 2 * twos:2].set(sink + moved)
    return tallies[jax.random.permutation(jax.random.fold_in(rng, 2), number_of)]


def gaussian(own_key, extent, deviation, limit, cuts=(), held_as=jnp.bfloat16):
    entries = deviation * jax.random.normal(own_key, extent, jnp.float32)
    if cuts:
        entries = entries * levels(own_key, extent, cuts, -0.22, 0.18)
    return jnp.clip(entries, -limit, limit).astype(held_as)


def setup_inputs(seed: int = 0) -> dict:
    seeds = jax.random.split(jax.random.key(seed), 16)
    return {
        "tokens": gaussian(seeds[0], (STREAMS, LENGTH, D), 1.0, 6.0, ((0, 2), (1, 16))),
        "doc_ids": jax.vmap(lambda own: jnp.searchsorted(jnp.cumsum(uneven_parts(own, 2, LENGTH, LENGTH - 1, 2)), jnp.arange(LENGTH), side="right"))(jax.random.split(seeds[1], STREAMS)).reshape((STREAMS, LENGTH)).astype(jnp.int32),
        "qkv_weight": gaussian(seeds[2], (D, 3 * D), D ** -0.5, 0.21875, ((0, 2),)),
        "qv_bias": gaussian(seeds[3], (2 * D,), 0.3, 1.796875, ((0, 2),)),
        "out_weight": gaussian(seeds[4], (D, D), (max(1, D * 32 // LENGTH)) ** -0.5, 2.5, ((0, 2),)),
        "out_bias": gaussian(seeds[5], (D,), 0.3, 1.796875, ((0, 2),)),
        "mid_gain": jnp.clip(1.0 + 0.1 * jax.random.normal(seeds[6], (D,), jnp.float32), 0.5, 1.5).astype(jnp.bfloat16),
        "mid_shift": gaussian(seeds[7], (D,), 0.3, 1.796875, ((0, 2),)),
        "up_weight": gaussian(seeds[8], (D, FF), D ** -0.5, 0.21875, ((0, 2),)),
        "up_bias": gaussian(seeds[9], (FF,), 0.5, 3.0, ((0, 2),)),
        "down_weight": gaussian(seeds[10], (FF, D), FF ** -0.5, 0.109375, ((0, 2),)),
        "down_bias": gaussian(seeds[11], (D,), 0.3, 1.796875, ((0, 2),)),
        "end_gain": jnp.clip(1.0 + 0.1 * jax.random.normal(seeds[12], (D,), jnp.float32), 0.5, 1.5).astype(jnp.bfloat16),
        "end_shift": gaussian(seeds[13], (D,), 0.3, 1.796875, ((0, 2),)),
        "out_grad": gaussian(seeds[14], (STREAMS, LENGTH, D), 1.0, 6.0, ((0, 2), (1, 16))),
    }


EPSILON = 1e-05
HIGH = lax.Precision.HIGHEST

@jax.custom_vjp
def low(v):
    return lax.optimization_barrier(v.astype(jnp.bfloat16)).astype(jnp.float32)

@jax.custom_vjp
def low_back(v):
    return v

def low_keep(v):
    return (low(v), None)

def low_pass(kept, grad):
    return (grad,)

def back_keep(v):
    return (v, None)

def back_low(kept, grad):
    return (low(grad),)
low.defvjp(low_keep, low_pass)
low_back.defvjp(back_keep, back_low)

def rounded_both(value):
    return low_back(low(value))

def layer_norm(hidden, gain, shift):
    centre = hidden - lax.optimization_barrier(jnp.mean(hidden, axis=-1, keepdims=True))
    inverse = lax.rsqrt(lax.optimization_barrier(jnp.mean(centre * centre, axis=-1, keepdims=True)) + EPSILON)
    return centre * inverse * gain + shift

def attention(queries, keys, values, documents):
    block_rows = math.gcd(LENGTH, 512)
    places = jnp.arange(LENGTH, dtype=jnp.int32)
    scale = HEAD_DIM ** (-0.5)

    def one_block(start):
        query_block = lax.dynamic_slice_in_dim(queries, start, block_rows, 0)
        block_pos = start + jnp.arange(block_rows, dtype=jnp.int32)
        block_docs = lax.dynamic_slice_in_dim(documents, start, block_rows, 0)
        score = jnp.einsum('qhd,khd->qhk', query_block, keys, precision=HIGH) * scale
        score = low_back(score)
        allow = jnp.logical_and(places[None, :] // BLOCK <= block_pos[:, None] // BLOCK, block_docs[:, None] == documents[None, :])
        score = jnp.where(allow[:, None, :], score, -1e+30)
        probs = low(jax.nn.softmax(score, axis=-1))
        return jnp.einsum('qhk,khd->qhd', probs, values, precision=HIGH)
    starts = jnp.arange(LENGTH // block_rows, dtype=jnp.int32) * block_rows
    return lax.map(jax.checkpoint(one_block), starts).reshape(LENGTH, D)

def forward(documents, inputs, qkv_w, qv_b, out_w, out_b, mid_g, mid_s, up_w, up_b, down_w, down_b, end_g, end_s):
    projected = jnp.dot(inputs, qkv_w, precision=HIGH)
    queries = rounded_both(projected[:, :D] + qv_b[:D])
    keys = rounded_both(projected[:, D:2 * D])
    values = rounded_both(projected[:, 2 * D:] + qv_b[D:])
    shape_heads = (LENGTH, HEADS, HEAD_DIM)
    attended = attention(queries.reshape(shape_heads), keys.reshape(shape_heads), values.reshape(shape_heads), documents)
    attended = rounded_both(attended)
    branch = low_back(jnp.dot(attended, out_w, precision=HIGH) + out_b)
    mid_out = layer_norm(inputs + branch, mid_g, mid_s)
    pre_act = low_back(jnp.dot(low(mid_out), up_w, precision=HIGH) + up_b)
    activated = low(jax.nn.gelu(pre_act, approximate=False))
    ffn_out = low_back(jnp.dot(activated, down_w, precision=HIGH) + down_b)
    return layer_norm(mid_out + ffn_out, end_g, end_s)

def reference(tokens, doc_ids, qkv_weight, qv_bias, out_weight, out_bias, mid_gain, mid_shift, up_weight, up_bias, down_weight, down_bias, end_gain, end_shift, out_grad):
    weights = tuple((member.astype(jnp.float32) for member in (qkv_weight, qv_bias, out_weight, out_bias, mid_gain, mid_shift, up_weight, up_bias, down_weight, down_bias, end_gain, end_shift)))

    def one_stream(totals, stream_data):
        inputs, documents, cotangent = stream_data

        def closed(*operands):
            return forward(documents, *operands)
        result, pullback = jax.vjp(closed, inputs.astype(jnp.float32), *weights)
        grads = pullback(cotangent.astype(jnp.float32))
        totals = tuple((total + grad for total, grad in zip(totals, grads[1:])))
        return (totals, (result.astype(jnp.bfloat16), grads[0].astype(jnp.bfloat16)))
    zeros = tuple((jnp.zeros(member.shape, jnp.float32) for member in weights))
    totals, (layer_out, input_grad) = lax.scan(one_stream, zeros, (tokens, doc_ids, out_grad))
    return (layer_out, input_grad, totals[0], totals[1], totals[2], totals[3], totals[4], totals[5], totals[6], totals[7], totals[8], totals[9], totals[10], totals[11])
```

```python
import jax
import jax.numpy as jnp
from jax import lax
from jax.experimental import pallas as pl
from jax.experimental.pallas import tpu as pltpu
from jax.sharding import PartitionSpec as P

HEADS = 12
HEAD_DIM = 64
BLOCK = 256
GROUPS = 4
PER = HEADS // GROUPS
SLAB = PER * HEAD_DIM
EPSILON = 1e-05
FAR = 2.0**100
F32 = jnp.float32
BF16 = jnp.bfloat16
NN = (((1,), (0,)), ((), ()))
NT = (((1,), (1,)), ((), ()))
VMEM_SPEC = pl.BlockSpec(memory_space=pltpu.VMEM)
VMEM_LIMIT = 67043328


def mm(left, right, dims=NN):
    return lax.dot_general(left, right, dims, preferred_element_type=F32)


def forward_kernel(
    members, x_ref, w_ref, bias_ref, docs_ref,
    o_ref, low_ref, lse_ref, q_ref, k_ref, kt_ref, vt_ref,
    top_ref, sum_ref,
):
    blocks = docs_ref.shape[0]
    m = lax.rem(lax.axis_index("rep"), members)

    def project(b, carry):
        rows = pl.ds(pl.multiple_of(b * BLOCK, BLOCK), BLOCK)
        both = mm(w_ref[SLAB:, :], x_ref[rows, :], NT)
        kt = both[:SLAB].astype(BF16)
        kt_ref[b] = kt
        vt_ref[b] = (both[SLAB:] + bias_ref[SLAB:, :]).astype(BF16)
        docs = docs_ref[b]
        extra = jnp.concatenate(
            [docs * FAR - FAR, docs * (-FAR), jnp.zeros((HEAD_DIM - 2, BLOCK), F32)], axis=0
        )
        for h in range(PER):
            part = kt[h * HEAD_DIM : (h + 1) * HEAD_DIM].astype(F32)
            k_ref[h, rows, :] = jnp.concatenate([part, extra], axis=0).T.astype(BF16)
        return carry

    lax.fori_loop(0, blocks, project, 0)
    for i in range(GROUPS):
        b = i * members + m
        rows = pl.ds(pl.multiple_of(b * BLOCK, BLOCK), BLOCK)
        qt = (mm(w_ref[:SLAB, :], x_ref[rows, :], NT) + bias_ref[:SLAB, :]).astype(BF16)
        qt = qt.astype(F32) * HEAD_DIM ** (-0.5)
        docs = docs_ref[b]
        extra = jnp.concatenate(
            [docs, 1.0 - docs, jnp.zeros((HEAD_DIM - 2, BLOCK), F32)], axis=0
        )
        for h in range(PER):
            part = qt[h * HEAD_DIM : (h + 1) * HEAD_DIM]
            q_ref[i, h] = jnp.concatenate([part, extra], axis=0).astype(BF16)
        top_ref[...] = jnp.full(top_ref.shape, -jnp.inf, F32)
        sum_ref[...] = jnp.zeros(sum_ref.shape, F32)
        o_ref[i] = jnp.zeros((SLAB, BLOCK), F32)

        def attend(step, carry):
            kb = b - step
            keys = pl.ds(pl.multiple_of(kb * BLOCK, BLOCK), BLOCK)
            for h in range(PER):
                head = pl.ds(h * HEAD_DIM, HEAD_DIM)
                score = mm(k_ref[h, keys, :], q_ref[i, h])
                old = top_ref[h]
                new = jnp.maximum(old, jnp.max(score, axis=0, keepdims=True))
                probs = jnp.exp(score - new)
                shrink = jnp.exp(old - new)
                top_ref[h] = new
                sum_ref[h] = sum_ref[h] * shrink + jnp.sum(probs, axis=0, keepdims=True)
                o_ref[i, head, :] = o_ref[i, head, :] * shrink + mm(
                    vt_ref[kb, head, :], probs.astype(BF16)
                )
            return carry

        lax.fori_loop(0, b + 1, attend, 0)
        for h in range(PER):
            head = pl.ds(h * HEAD_DIM, HEAD_DIM)
            out = o_ref[i, head, :] / sum_ref[h]
            o_ref[i, head, :] = out
            low_ref[i, head, :] = out.astype(BF16)
            lse_ref[i, h] = top_ref[h] + jnp.log(sum_ref[h])


def attention_forward(x_all, w_group, bias, docs, members):
    blocks = docs.shape[0]
    shape = jax.ShapeDtypeStruct
    return pl.pallas_call(
        lambda *refs: forward_kernel(members, *refs),
        out_shape=(
            shape((GROUPS, SLAB, BLOCK), F32),
            shape((GROUPS, SLAB, BLOCK), BF16),
            shape((GROUPS, PER, 1, BLOCK), F32),
            shape((GROUPS, PER, 2 * HEAD_DIM, BLOCK), BF16),
            shape((PER, blocks * BLOCK, 2 * HEAD_DIM), BF16),
            shape((blocks, SLAB, BLOCK), BF16),
            shape((blocks, SLAB, BLOCK), BF16),
        ),
        in_specs=[VMEM_SPEC] * 4,
        out_specs=(VMEM_SPEC,) * 7,
        scratch_shapes=[pltpu.VMEM((PER, 1, BLOCK), F32), pltpu.VMEM((PER, 1, BLOCK), F32)],
        compiler_params=pltpu.CompilerParams(vmem_limit_bytes=VMEM_LIMIT),
    )(x_all, w_group, bias, docs)


def remote(src, dst, send, recv, rep, shard):
    return pltpu.make_async_remote_copy(
        src_ref=src, dst_ref=dst, send_sem=send, recv_sem=recv,
        device_id=(rep, shard), device_id_type=pl.DeviceIdType.MESH,
    )


def hello(partners):
    barrier = pltpu.get_barrier_semaphore()
    total = 0
    for rep, shard, there in partners:
        if there is True:
            pl.semaphore_signal(
                barrier, inc=1, device_id=(rep, shard), device_id_type=pl.DeviceIdType.MESH
            )
            total = total + 1
        else:

            @pl.when(there)
            def _():
                pl.semaphore_signal(
                    barrier, inc=1, device_id=(rep, shard), device_id_type=pl.DeviceIdType.MESH
                )

            total = total + there.astype(jnp.int32)
    pl.semaphore_wait(barrier, total)


def gather_kernel(
    ring, shards, parts, x_ref, *refs,
):
    n = len(parts)
    own, (xa_ref, *full) = refs[:n], refs[n : 2 * n + 1]
    send, recv, wsend, wrecv, fsend, frecv, lsem = refs[2 * n + 1 :]
    r, s = lax.axis_index("rep"), lax.axis_index("shard")
    levels = ring // 4
    z, c = r // 4, lax.rem(r, 2)
    sib = r + 1 - 2 * c
    yn = r + 2 - 4 * lax.rem(r // 2, 2)
    above, below = z < levels - 1, z > 0
    others = [lax.rem(s + d, shards) for d in range(1, shards)]
    hello(
        [(sib, s, True), (yn, s, True), (r + 4, s, above), (r - 4, s, below)]
        + [(r, t, True) for t in others]
    )

    def move(b, kind):
        src = xa_ref.at[b]
        target = (r + 4, r - 4, yn, sib)[kind]
        return remote(src, xa_ref.at[b], send.at[kind, b], recv.at[b], target, s)

    def first(kind):
        target = (r + 4, r - 4, yn, sib)[kind]
        return remote(x_ref, xa_ref.at[r], send.at[kind, r], recv.at[r], target, s)

    keep = pltpu.make_async_copy(x_ref, xa_ref.at[r], lsem)
    keep.start()
    pl.when(above)(lambda: first(0).start())
    pl.when(below)(lambda: first(1).start())
    first(2).start()
    first(3).start()

    pieces = []
    for w, count in enumerate(parts):
        size = own[w].shape[0] // 2 // count
        for j in range(count):
            pieces.append((w, j, count, size, len(pieces)))

    def across(piece, d):
        w, j, count, size, at = piece
        rows = pl.ds(pl.multiple_of((c * count + j) * size, size), size)
        return remote(
            own[w].at[rows], full[w].at[s, rows], wsend.at[at, d - 1], wrecv.at[at, d - 1],
            r, others[d - 1],
        )

    def along(piece, d, core):
        w, j, count, size, at = piece
        rows = pl.ds(pl.multiple_of((core * count + j) * size, size), size)
        place = full[w].at[lax.rem(s + shards - d, shards), rows]
        return remote(place, place, fsend.at[at, d - 1], frecv.at[at, d - 1], sib, s)

    for piece in pieces:
        for d in range(1, shards):
            across(piece, d).start()

    def pass_on(b, there, kinds):
        def go():
            move(b, 3).wait_recv()
            for kind, also in kinds:
                if also is True:
                    move(b, kind).start()
                else:
                    pl.when(also)(lambda kind=kind: move(b, kind).start())

        if there is True:
            go()
        else:
            pl.when(there)(go)

    for k in range(levels):
        low, high = z >= k, z + k < levels
        if k:
            pass_on(r - 4 * k, low, [(0, above), (2, True), (3, True)])
            pass_on(r + 4 * k, high, [(1, below), (2, True), (3, True)])
            pass_on(yn - 4 * k, low, [(3, True)])
            pass_on(yn + 4 * k, high, [(3, True)])
        else:
            pass_on(yn, True, [(3, True)])
    for piece in pieces:
        for d in range(1, shards):
            across(piece, d).wait_recv()
            along(piece, d, c).start()
    keep.wait()
    for b in range(0, ring, 2):
        move(b + 1 - c, 3).wait_recv()
    for piece in pieces:
        for d in range(1, shards):
            along(piece, d, 1 - c).wait_recv()
    pl.when(above)(lambda: first(0).wait_send())
    pl.when(below)(lambda: first(1).wait_send())
    first(2).wait_send()
    first(3).wait_send()
    for k in range(levels):
        low, high = z >= k, z + k < levels
        if k:
            for b, there, kind, also in (
                (r - 4 * k, low, 0, above), (r + 4 * k, high, 1, below),
            ):

                @pl.when(there)
                def _():
                    pl.when(also)(lambda: move(b, kind).wait_send())
                    move(b, 2).wait_send()
                    move(b, 3).wait_send()

            pl.when(low)(lambda: move(yn - 4 * k, 3).wait_send())
            pl.when(high)(lambda: move(yn + 4 * k, 3).wait_send())
        else:
            move(yn, 3).wait_send()
    for piece in pieces:
        for d in range(1, shards):
            across(piece, d).wait_send()
            along(piece, d, c).wait_send()


ANY_SPEC = pl.BlockSpec(memory_space=pl.ANY)


def gather_all(x, weights, parts, ring, shards):
    shape = jax.ShapeDtypeStruct
    dma = pltpu.SemaphoreType.DMA
    n = sum(parts)
    return pl.pallas_call(
        lambda *refs: gather_kernel(ring, shards, parts, *refs),
        out_shape=(shape((ring,) + x.shape, x.dtype),)
        + tuple(shape((shards,) + w.shape, w.dtype) for w in weights),
        in_specs=[ANY_SPEC] * (1 + len(weights)),
        out_specs=(ANY_SPEC,) * (1 + len(weights)),
        scratch_shapes=[
            dma((4, ring)), dma((ring,)), dma((n, shards - 1)), dma((n, shards - 1)),
            dma((n, shards - 1)), dma((n, shards - 1)), dma(()),
        ],
        compiler_params=pltpu.CompilerParams(collective_id=0, has_side_effects=True),
    )(x, *weights)


def exchange_kernel(ring, in_ref, out_ref, send, recv, lsem):
    r, s = lax.axis_index("rep"), lax.axis_index("shard")
    members = ring // GROUPS
    g, m = r // members, lax.rem(r, members)
    peers = [lax.rem(g + d, GROUPS) for d in range(1, GROUPS)]
    hello([(p * members + m, s, True) for p in peers])
    copies = [
        remote(
            in_ref.at[p], out_ref.at[g], send.at[d], recv.at[d], p * members + m, s
        )
        for d, p in enumerate(peers)
    ]
    for copy in copies:
        copy.start()
    keep = pltpu.make_async_copy(in_ref.at[g], out_ref.at[g], lsem)
    keep.start()
    keep.wait()
    for copy in copies:
        copy.wait()


def exchange_slabs(slabs, ring, ident):
    dma = pltpu.SemaphoreType.DMA
    return pl.pallas_call(
        lambda *refs: exchange_kernel(ring, *refs),
        out_shape=jax.ShapeDtypeStruct(slabs.shape, slabs.dtype),
        in_specs=[VMEM_SPEC],
        out_specs=VMEM_SPEC,
        scratch_shapes=[dma((GROUPS - 1,)), dma((GROUPS - 1,)), dma(())],
        compiler_params=pltpu.CompilerParams(collective_id=ident, has_side_effects=True),
    )(slabs)


def backward_kernel(
    ring, go_ref, q_ref, k_ref, kt_ref, vt_ref, o_ref, lse_ref, xa_ref, w_ref, mid_ref,
    out_ref, dw_ref, db_ref,
    g_ref, x_ref, v_ref, delta_ref, acc_ref, dk_ref, dv_ref, pq_ref, stage_ref, got_ref,
    total_ref, dx_ref, near_ref, far_ref, gsend, grecv, ksend, krecv, xsend, xrecv, lsem,
):
    r, s = lax.axis_index("rep"), lax.axis_index("shard")
    members = ring // GROUPS
    g, m = r // members, lax.rem(r, members)
    peers = [lax.rem(g + d, GROUPS) for d in range(1, GROUPS)]
    mates = [lax.rem(m + d, members) for d in range(1, members)]
    hello(
        [(p * members + m, s, True) for p in peers] + [(g * members + t, s, True) for t in mates]
    )
    loads = [
        pltpu.make_async_copy(xa_ref.at[j * members + m], x_ref.at[j], lsem.at[j])
        for j in range(GROUPS)
    ]
    for load in loads:
        load.start()

    def give(p):
        return remote(go_ref.at[p], g_ref.at[g], gsend.at[p], grecv.at[g], p * members + m, s)

    def take(p):
        return remote(go_ref.at[p], g_ref.at[p], gsend.at[p], grecv.at[p], p * members + m, s)

    for p in peers:
        give(p).start()
    g_ref[g] = go_ref[g]

    def turn(b, carry):
        rows = pl.ds(pl.multiple_of(b * BLOCK, BLOCK), BLOCK)
        for h in range(PER):
            v_ref[h, rows, :] = (
                vt_ref[b, h * HEAD_DIM : (h + 1) * HEAD_DIM, :].astype(F32).T.astype(BF16)
            )
        dk_ref[b] = jnp.zeros((SLAB, BLOCK), F32)
        dv_ref[b] = jnp.zeros((SLAB, BLOCK), F32)
        return carry

    lax.fori_loop(0, ring, turn, 0)
    total_ref[...] = jnp.zeros(total_ref.shape, F32)
    db_ref[...] = jnp.zeros(db_ref.shape, F32)

    def share(j, d):
        return remote(
            stage_ref.at[j, mates[d - 1]], got_ref.at[j, d - 1],
            ksend.at[j, d - 1], krecv.at[j, d - 1], g * members + mates[d - 1], s,
        )

    def attend_block(i):
        b = i * members + m
        pl.when(g != i)(lambda: take(i).wait_recv())
        for h in range(PER):
            head = pl.ds(h * HEAD_DIM, HEAD_DIM)
            delta_ref[h] = jnp.sum(
                g_ref[i, head, :].astype(F32) * o_ref[i, head, :], axis=0, keepdims=True
            )
        acc_ref[...] = jnp.zeros(acc_ref.shape, F32)

        def attend(kb, carry):
            keys = pl.ds(pl.multiple_of(kb * BLOCK, BLOCK), BLOCK)
            for h in range(PER):
                head = pl.ds(h * HEAD_DIM, HEAD_DIM)
                score = mm(k_ref[h, keys, :], q_ref[i, h])
                probs = jnp.exp(score - lse_ref[i, h])
                grad = g_ref[i, head, :]
                moved = (probs * (mm(v_ref[h, keys, :], grad) - delta_ref[h])).astype(BF16)
                acc_ref[h] += mm(kt_ref[kb, head, :], moved)
                dk_ref[kb, head, :] += mm(q_ref[i, h, :HEAD_DIM, :], moved, NT)
                dv_ref[kb, head, :] += mm(grad, probs.astype(BF16), NT)
            return carry

        lax.fori_loop(0, b + 1, attend, 0)
        for h in range(PER):
            pq_ref[i, pl.ds(h * HEAD_DIM, HEAD_DIM), :] = (
                acc_ref[h] * HEAD_DIM ** (-0.5)
            ).astype(BF16)
        for t in range(members):
            stage_ref[i, t, :SLAB, :] = dk_ref[i * members + t].astype(BF16)
            stage_ref[i, t, SLAB:, :] = dv_ref[i * members + t].astype(BF16)
        for d in range(1, members):
            share(i, d).start()

    def send_dx(j):
        return remote(
            dx_ref.at[j], far_ref.at[g], xsend.at[j], xrecv.at[g], j * members + m, s
        )

    def finish_block(j):
        b = j * members + m
        for d in range(1, members):
            share(j, d).wait_recv()
        dk, dv = dk_ref[b], dv_ref[b]
        for d in range(1, members):
            dk = dk + got_ref[j, d - 1, :SLAB, :].astype(F32)
            dv = dv + got_ref[j, d - 1, SLAB:, :].astype(F32)
        proj = jnp.concatenate([pq_ref[j], dk.astype(BF16), dv.astype(BF16)], axis=0)
        db_ref[...] += jnp.sum(proj.astype(F32), axis=1, keepdims=True)
        loads[j].wait()
        total_ref[...] += mm(x_ref[j], proj.T, (((0,), (0,)), ((), ())))
        dx = mm(proj, w_ref[...], (((0,), (0,)), ((), ())))

        @pl.when(g == j)
        def _():
            near_ref[...] = dx

        @pl.when(g != j)
        def _():
            dx_ref[j] = dx.astype(BF16)
            send_dx(j).start()

    order = list(range(GROUPS))[::-1]
    for at, i in enumerate(order):
        attend_block(i)
        if at:
            finish_block(order[at - 1])
    finish_block(order[-1])
    dw_ref[...] = total_ref[...].astype(BF16)
    result = near_ref[...] + mid_ref[...]
    for p in peers:
        remote(dx_ref.at[0], far_ref.at[p], xsend.at[0], xrecv.at[p], r, s).wait_recv()
        result = result + far_ref[p].astype(F32)
    out_ref[...] = result.astype(BF16)
    for p in peers:
        give(p).wait_send()
    for j in range(GROUPS):
        for d in range(1, members):
            share(j, d).wait_send()
        pl.when(g != j)(lambda: send_dx(j).wait_send())


def attention_backward(ring, grads, q, k, kt, vt, o, lse, x_all, w_group, mid, ident):
    members = ring // GROUPS
    width = x_all.shape[-1]
    shape = jax.ShapeDtypeStruct
    dma = pltpu.SemaphoreType.DMA
    vmem = pltpu.VMEM
    return pl.pallas_call(
        lambda *refs: backward_kernel(ring, *refs),
        out_shape=(
            shape((BLOCK, width), BF16), shape((width, 3 * SLAB), BF16), shape((3 * SLAB, 1), F32),
        ),
        in_specs=[VMEM_SPEC] * 7 + [ANY_SPEC] + [VMEM_SPEC] * 2,
        out_specs=(VMEM_SPEC,) * 3,
        scratch_shapes=[
            vmem((GROUPS, SLAB, BLOCK), BF16),
            vmem((GROUPS, BLOCK, width), BF16),
            vmem((PER, ring * BLOCK, HEAD_DIM), BF16),
            vmem((PER, 1, BLOCK), F32),
            vmem((PER, HEAD_DIM, BLOCK), F32),
            vmem((ring, SLAB, BLOCK), F32),
            vmem((ring, SLAB, BLOCK), F32),
            vmem((GROUPS, SLAB, BLOCK), BF16),
            vmem((GROUPS, members, 2 * SLAB, BLOCK), BF16),
            vmem((GROUPS, members - 1, 2 * SLAB, BLOCK), BF16),
            vmem((width, 3 * SLAB), F32),
            vmem((GROUPS, BLOCK, width), BF16),
            vmem((BLOCK, width), F32),
            vmem((GROUPS, BLOCK, width), BF16),
            dma((GROUPS,)), dma((GROUPS,)),
            dma((GROUPS, members - 1)), dma((GROUPS, members - 1)),
            dma((GROUPS,)), dma((GROUPS,)), dma((GROUPS,)),
        ],
        compiler_params=pltpu.CompilerParams(
            collective_id=ident, has_side_effects=True, vmem_limit_bytes=VMEM_LIMIT
        ),
    )(grads, q, k, kt, vt, o, lse, x_all, w_group, mid)


def layer_norm(hidden, gain, shift):
    centre = hidden - jnp.mean(hidden, axis=-1, keepdims=True)
    inverse = lax.rsqrt(jnp.mean(centre * centre, axis=-1, keepdims=True) + EPSILON)
    normed = centre * inverse
    return (normed * gain + shift, normed, inverse)


def norm_back(grad_output, normed, inverse, gain):
    grad_normed = grad_output * gain
    centred = grad_normed - jnp.mean(grad_normed, axis=-1, keepdims=True)
    return inverse * (centred - normed * jnp.mean(grad_normed * normed, axis=-1, keepdims=True))


def gelu_slope(value):
    return (
        0.5 * (1.0 + lax.erf(value * 0.7071067811865476))
        + value * jnp.exp(-0.5 * value * value) * 0.3989422804014327
    )


def on_device(
    tokens, doc_ids, qkv_weight, qv_bias, out_weight, out_bias, mid_gain, mid_shift,
    up_weight, up_bias, down_weight, down_bias, end_gain, end_shift, out_grad,
):
    width = tokens.shape[2]
    ring = lax.axis_size("rep")
    members = ring // GROUPS
    r = lax.axis_index("rep")
    g = r // members
    m = lax.rem(r, members)

    shards = lax.axis_size("shard")
    x = tokens[0]
    local = jnp.concatenate(
        [lax.dynamic_slice_in_dim(qkv_weight, t * width + g * SLAB, SLAB, 1) for t in range(3)], 1
    )
    small = (qv_bias, out_bias, mid_gain, mid_shift, up_bias, down_bias, end_gain, end_shift)
    sizes = [v.shape[0] for v in small]
    flat = jnp.concatenate(small)
    lanes = 128
    flat = jnp.pad(flat, (0, -flat.shape[0] % (32 * lanes))).reshape(-1, lanes)
    x_all, w_group, flat, full_out, full_up, full_down = gather_all(
        x, (local, flat, out_weight, up_weight, down_weight), (1, 1, 1, 2, 2), ring, shards
    )

    def whole(gathered, mine):
        put = lax.dynamic_update_index_in_dim(gathered, mine, lax.axis_index("shard"), 0)
        return put.reshape(shards * mine.shape[0], *mine.shape[1:])

    x_all = x_all.reshape(ring * BLOCK, width)
    w_group = whole(w_group, local).T
    flat_own = jnp.pad(jnp.concatenate(small), (0, -sum(sizes) % (32 * lanes)))
    flat = whole(flat.reshape(shards, -1), flat_own).reshape(shards, -1).astype(F32)
    vectors = []
    at = 0
    for size in sizes:
        vectors.append(flat[:, at : at + size].reshape(-1))
        at += size
    vec_qv, vec_out, gain_mid, shift_mid, vec_up, vec_down, gain_end, shift_end = vectors
    full_out, full_up, full_down = (
        whole(full_out, out_weight), whole(full_up, up_weight), whole(full_down, down_weight)
    )
    bias = jnp.concatenate(
        [
            lax.dynamic_slice_in_dim(vec_qv, g * SLAB, SLAB, 0),
            jnp.zeros((SLAB,), F32),
            lax.dynamic_slice_in_dim(vec_qv, width + g * SLAB, SLAB, 0),
        ]
    )
    bias = jnp.concatenate([bias[:SLAB], bias[2 * SLAB :]]).reshape(2 * SLAB, 1)
    docs = doc_ids.reshape(ring, 1, BLOCK).astype(F32)
    o, o_low, lse, q, k, kt, vt = attention_forward(x_all, w_group, bias, docs, members)
    attended_t = exchange_slabs(o_low, ring, 1).reshape(width, BLOCK)

    attended_low = attended_t.T
    branch = mm(attended_low, full_out) + vec_out
    mid_out, mid_norm, mid_inv = layer_norm(x.astype(F32) + branch, gain_mid, shift_mid)
    mid_low = mid_out.astype(BF16)
    pre_act = mm(mid_low, full_up) + vec_up
    activated = jax.nn.gelu(pre_act, approximate=False).astype(BF16)
    ffn_out = mm(activated, full_down) + vec_down
    end_out, end_norm, end_inv = layer_norm(mid_out + ffn_out, gain_end, shift_end)
    layer_out = end_out.astype(BF16)
    grad_top = out_grad[0].astype(F32)
    grad_end_gain = jnp.sum(grad_top * end_norm, axis=0)
    grad_end_shift = jnp.sum(grad_top, axis=0)
    grad_end_in = norm_back(grad_top, end_norm, end_inv, gain_end)
    grad_ffn = grad_end_in.astype(BF16)
    grad_down_bias = jnp.sum(grad_ffn.astype(F32), axis=0)
    grad_down_weight = mm(activated.T, grad_ffn)
    grad_act = mm(grad_ffn, full_down, NT)
    grad_pre = (grad_act * gelu_slope(pre_act)).astype(BF16)
    grad_up_bias = jnp.sum(grad_pre.astype(F32), axis=0)
    grad_up_weight = mm(mid_low.T, grad_pre)
    grad_mid_out = mm(grad_pre, full_up, NT) + grad_end_in
    grad_mid_gain = jnp.sum(grad_mid_out * mid_norm, axis=0)
    grad_mid_shift = jnp.sum(grad_mid_out, axis=0)
    grad_mid_in = norm_back(grad_mid_out, mid_norm, mid_inv, gain_mid)
    grad_branch = grad_mid_in.astype(BF16)
    grad_out_bias = jnp.sum(grad_branch.astype(F32), axis=0)
    grad_out_weight = mm(attended_t, grad_branch)
    grad_attended_t = mm(full_out, grad_branch, NT).astype(BF16)
    input_grad, dw_group, dbias = attention_backward(
        ring, grad_attended_t.reshape(GROUPS, SLAB, BLOCK), q, k, kt, vt, o, lse,
        x_all.reshape(ring, BLOCK, width), w_group, grad_mid_in, 2,
    )
    dw_group = dw_group.astype(F32)

    place = jnp.zeros((width, 3, GROUPS, SLAB), F32)
    grad_qkv = lax.dynamic_update_slice_in_dim(
        place, dw_group.reshape(width, 3, 1, SLAB), g, 2
    ).reshape(width, 3 * width)
    qv = dbias.reshape(3, SLAB)[jnp.array([0, 2])]
    grad_qv_bias = lax.dynamic_update_slice_in_dim(
        jnp.zeros((2, GROUPS, SLAB), F32), qv.reshape(2, 1, SLAB), g, 1
    ).reshape(2 * width)

    def total(value):
        part = lax.psum_scatter(value.astype(BF16), "shard", scatter_dimension=0, tiled=True)
        return lax.psum(part, "rep").astype(F32)

    return (
        layer_out[None],
        input_grad[None],
        total(grad_qkv),
        total(grad_qv_bias),
        total(grad_out_weight),
        total(grad_out_bias),
        total(grad_mid_gain),
        total(grad_mid_shift),
        total(grad_up_weight),
        total(grad_up_bias),
        total(grad_down_weight),
        total(grad_down_bias),
        total(grad_end_gain),
        total(grad_end_shift),
    )


def solution(mesh):
    rows = P("shard", None)
    flat = P("shard")
    acts = P("shard", "rep", None)
    in_specs = (
        acts, rows, rows, flat, rows, flat, flat, flat, rows, flat, rows, flat, flat, flat, acts
    )
    out_specs = (acts, acts, rows, flat, rows, flat, flat, flat, rows, flat, rows, flat, flat, flat)
    return jax.shard_map(
        on_device, mesh=mesh, in_specs=in_specs, out_specs=out_specs, check_vma=False
    )
```

```python
import jax
import jax.numpy as jnp
from jax import lax
from jax.experimental import pallas as pl
from jax.experimental.pallas import tpu as pltpu
from jax.sharding import PartitionSpec as P

HEADS = 12
HEAD_DIM = 64
BLOCK = 256
GROUPS = 4
PER = HEADS // GROUPS
SLAB = PER * HEAD_DIM
EPSILON = 1e-05
FAR = 2.0**100
F32 = jnp.float32
BF16 = jnp.bfloat16
LANES = 128
NN = (((1,), (0,)), ((), ()))
NT = (((1,), (1,)), ((), ()))
VMEM_SPEC = pl.BlockSpec(memory_space=pltpu.VMEM)
VMEM_LIMIT = 67043328


def mm(left, right, dims=NN):
    return lax.dot_general(left, right, dims, preferred_element_type=F32)


def forward_kernel(
    members, x_ref, w_ref, bias_ref, docs_ref,
    o_ref, low_ref, lse_ref, q_ref, k_ref, kt_ref, vt_ref,
    top_ref, sum_ref,
):
    blocks = docs_ref.shape[0]
    m = lax.rem(lax.axis_index("rep"), members)

    def project(b, carry):
        rows = pl.ds(pl.multiple_of(b * BLOCK, BLOCK), BLOCK)
        both = mm(w_ref[SLAB:, :], x_ref[rows, :], NT)
        kt = both[:SLAB].astype(BF16)
        kt_ref[b] = kt
        vt_ref[b] = (both[SLAB:] + bias_ref[SLAB:, :]).astype(BF16)
        docs = docs_ref[b]
        extra = jnp.concatenate(
            [docs * FAR - FAR, docs * (-FAR), jnp.zeros((HEAD_DIM - 2, BLOCK), F32)], axis=0
        )
        for h in range(PER):
            part = kt[h * HEAD_DIM : (h + 1) * HEAD_DIM].astype(F32)
            k_ref[h, rows, :] = jnp.concatenate([part, extra], axis=0).T.astype(BF16)
        return carry

    lax.fori_loop(0, blocks, project, 0)
    for i in range(GROUPS):
        b = i * members + m
        rows = pl.ds(pl.multiple_of(b * BLOCK, BLOCK), BLOCK)
        qt = (mm(w_ref[:SLAB, :], x_ref[rows, :], NT) + bias_ref[:SLAB, :]).astype(BF16)
        qt = qt.astype(F32) * HEAD_DIM ** (-0.5)
        docs = docs_ref[b]
        extra = jnp.concatenate(
            [docs, 1.0 - docs, jnp.zeros((HEAD_DIM - 2, BLOCK), F32)], axis=0
        )
        for h in range(PER):
            part = qt[h * HEAD_DIM : (h + 1) * HEAD_DIM]
            q_ref[i, h] = jnp.concatenate([part, extra], axis=0).astype(BF16)
        top_ref[...] = jnp.full(top_ref.shape, -jnp.inf, F32)
        sum_ref[...] = jnp.zeros(sum_ref.shape, F32)
        o_ref[i] = jnp.zeros((SLAB, BLOCK), F32)

        def attend(step, carry):
            kb = b - step
            keys = pl.ds(pl.multiple_of(kb * BLOCK, BLOCK), BLOCK)
            for h in range(PER):
                head = pl.ds(h * HEAD_DIM, HEAD_DIM)
                score = mm(k_ref[h, keys, :], q_ref[i, h])
                old = top_ref[h]
                new = jnp.maximum(old, jnp.max(score, axis=0, keepdims=True))
                probs = jnp.exp(score - new)
                shrink = jnp.exp(old - new)
                top_ref[h] = new
                sum_ref[h] = sum_ref[h] * shrink + jnp.sum(probs, axis=0, keepdims=True)
                o_ref[i, head, :] = o_ref[i, head, :] * shrink + mm(
                    vt_ref[kb, head, :], probs.astype(BF16)
                )
            return carry

        lax.fori_loop(0, b + 1, attend, 0)
        for h in range(PER):
            head = pl.ds(h * HEAD_DIM, HEAD_DIM)
            out = o_ref[i, head, :] / sum_ref[h]
            o_ref[i, head, :] = out
            low_ref[i, head, :] = out.astype(BF16)
            lse_ref[i, h] = top_ref[h] + jnp.log(sum_ref[h])


def attention_forward(x_all, w_group, bias, docs, members):
    blocks = docs.shape[0]
    shape = jax.ShapeDtypeStruct
    return pl.pallas_call(
        lambda *refs: forward_kernel(members, *refs),
        out_shape=(
            shape((GROUPS, SLAB, BLOCK), F32),
            shape((GROUPS, SLAB, BLOCK), BF16),
            shape((GROUPS, PER, 1, BLOCK), F32),
            shape((GROUPS, PER, 2 * HEAD_DIM, BLOCK), BF16),
            shape((PER, blocks * BLOCK, 2 * HEAD_DIM), BF16),
            shape((blocks, SLAB, BLOCK), BF16),
            shape((blocks, SLAB, BLOCK), BF16),
        ),
        in_specs=[VMEM_SPEC] * 4,
        out_specs=(VMEM_SPEC,) * 7,
        scratch_shapes=[pltpu.VMEM((PER, 1, BLOCK), F32), pltpu.VMEM((PER, 1, BLOCK), F32)],
        compiler_params=pltpu.CompilerParams(vmem_limit_bytes=VMEM_LIMIT),
    )(x_all, w_group, bias, docs)


def remote(src, dst, send, recv, rep, shard):
    return pltpu.make_async_remote_copy(
        src_ref=src, dst_ref=dst, send_sem=send, recv_sem=recv,
        device_id=(rep, shard), device_id_type=pl.DeviceIdType.MESH,
    )


def hello(partners):
    barrier = pltpu.get_barrier_semaphore()
    total = 0
    for rep, shard, there in partners:
        if there is True:
            pl.semaphore_signal(
                barrier, inc=1, device_id=(rep, shard), device_id_type=pl.DeviceIdType.MESH
            )
            total = total + 1
        else:

            @pl.when(there)
            def _():
                pl.semaphore_signal(
                    barrier, inc=1, device_id=(rep, shard), device_id_type=pl.DeviceIdType.MESH
                )

            total = total + there.astype(jnp.int32)
    pl.semaphore_wait(barrier, total)


def gather_kernel(
    ring, shards, parts, x_ref, *refs,
):
    n = len(parts)
    own, (xa_ref, *full) = refs[:n], refs[n : 2 * n + 1]
    send, recv, wsend, wrecv, fsend, frecv, lsem = refs[2 * n + 1 :]
    r, s = lax.axis_index("rep"), lax.axis_index("shard")
    levels = ring // 4
    z, c = r // 4, lax.rem(r, 2)
    sib = r + 1 - 2 * c
    yn = r + 2 - 4 * lax.rem(r // 2, 2)
    above, below = z < levels - 1, z > 0
    others = [lax.rem(s + d, shards) for d in range(1, shards)]
    hello(
        [(sib, s, True), (yn, s, True), (r + 4, s, above), (r - 4, s, below)]
        + [(r, t, True) for t in others]
    )

    def move(b, kind):
        src = xa_ref.at[b]
        target = (r + 4, r - 4, yn, sib)[kind]
        return remote(src, xa_ref.at[b], send.at[kind, b], recv.at[b], target, s)

    def first(kind):
        target = (r + 4, r - 4, yn, sib)[kind]
        return remote(x_ref, xa_ref.at[r], send.at[kind, r], recv.at[r], target, s)

    keep = pltpu.make_async_copy(x_ref, xa_ref.at[r], lsem)
    keep.start()
    pl.when(above)(lambda: first(0).start())
    pl.when(below)(lambda: first(1).start())
    first(2).start()
    first(3).start()

    pieces = []
    for w, count in enumerate(parts):
        size = own[w].shape[0] // 2 // count
        for j in range(count):
            pieces.append((w, j, count, size, len(pieces)))

    def across(piece, d):
        w, j, count, size, at = piece
        rows = pl.ds(pl.multiple_of((c * count + j) * size, size), size)
        return remote(
            own[w].at[rows], full[w].at[s, rows], wsend.at[at, d - 1], wrecv.at[at, d - 1],
            r, others[d - 1],
        )

    def along(piece, d, core):
        w, j, count, size, at = piece
        rows = pl.ds(pl.multiple_of((core * count + j) * size, size), size)
        place = full[w].at[lax.rem(s + shards - d, shards), rows]
        return remote(place, place, fsend.at[at, d - 1], frecv.at[at, d - 1], sib, s)

    for piece in pieces:
        for d in range(1, shards):
            across(piece, d).start()

    def pass_on(b, there, kinds):
        def go():
            move(b, 3).wait_recv()
            for kind, also in kinds:
                if also is True:
                    move(b, kind).start()
                else:
                    pl.when(also)(lambda kind=kind: move(b, kind).start())

        if there is True:
            go()
        else:
            pl.when(there)(go)

    for k in range(levels):
        low, high = z >= k, z + k < levels
        if k:
            pass_on(r - 4 * k, low, [(0, above), (2, True), (3, True)])
            pass_on(r + 4 * k, high, [(1, below), (2, True), (3, True)])
            pass_on(yn - 4 * k, low, [(3, True)])
            pass_on(yn + 4 * k, high, [(3, True)])
        else:
            pass_on(yn, True, [(3, True)])
    for piece in pieces:
        for d in range(1, shards):
            across(piece, d).wait_recv()
            along(piece, d, c).start()
    keep.wait()
    for b in range(0, ring, 2):
        move(b + 1 - c, 3).wait_recv()
    for piece in pieces:
        for d in range(1, shards):
            along(piece, d, 1 - c).wait_recv()
    pl.when(above)(lambda: first(0).wait_send())
    pl.when(below)(lambda: first(1).wait_send())
    first(2).wait_send()
    first(3).wait_send()
    for k in range(levels):
        low, high = z >= k, z + k < levels
        if k:
            for b, there, kind, also in (
                (r - 4 * k, low, 0, above), (r + 4 * k, high, 1, below),
            ):

                @pl.when(there)
                def _():
                    pl.when(also)(lambda: move(b, kind).wait_send())
                    move(b, 2).wait_send()
                    move(b, 3).wait_send()

            pl.when(low)(lambda: move(yn - 4 * k, 3).wait_send())
            pl.when(high)(lambda: move(yn + 4 * k, 3).wait_send())
        else:
            move(yn, 3).wait_send()
    for piece in pieces:
        for d in range(1, shards):
            across(piece, d).wait_send()
            along(piece, d, c).wait_send()


ANY_SPEC = pl.BlockSpec(memory_space=pl.ANY)


def gather_all(x, weights, parts, ring, shards):
    shape = jax.ShapeDtypeStruct
    dma = pltpu.SemaphoreType.DMA
    n = sum(parts)
    return pl.pallas_call(
        lambda *refs: gather_kernel(ring, shards, parts, *refs),
        out_shape=(shape((ring,) + x.shape, x.dtype),)
        + tuple(shape((shards,) + w.shape, w.dtype) for w in weights),
        in_specs=[ANY_SPEC] * (1 + len(weights)),
        out_specs=(ANY_SPEC,) * (1 + len(weights)),
        scratch_shapes=[
            dma((4, ring)), dma((ring,)), dma((n, shards - 1)), dma((n, shards - 1)),
            dma((n, shards - 1)), dma((n, shards - 1)), dma(()),
        ],
        compiler_params=pltpu.CompilerParams(collective_id=0, has_side_effects=True),
    )(x, *weights)


def exchange_kernel(ring, in_ref, out_ref, send, recv, lsem):
    r, s = lax.axis_index("rep"), lax.axis_index("shard")
    members = ring // GROUPS
    g, m = r // members, lax.rem(r, members)
    peers = [lax.rem(g + d, GROUPS) for d in range(1, GROUPS)]
    hello([(p * members + m, s, True) for p in peers])
    copies = [
        remote(
            in_ref.at[p], out_ref.at[g], send.at[d], recv.at[d], p * members + m, s
        )
        for d, p in enumerate(peers)
    ]
    for copy in copies:
        copy.start()
    keep = pltpu.make_async_copy(in_ref.at[g], out_ref.at[g], lsem)
    keep.start()
    keep.wait()
    for copy in copies:
        copy.wait()


def exchange_slabs(slabs, ring, ident):
    dma = pltpu.SemaphoreType.DMA
    return pl.pallas_call(
        lambda *refs: exchange_kernel(ring, *refs),
        out_shape=jax.ShapeDtypeStruct(slabs.shape, slabs.dtype),
        in_specs=[VMEM_SPEC],
        out_specs=VMEM_SPEC,
        scratch_shapes=[dma((GROUPS - 1,)), dma((GROUPS - 1,)), dma(())],
        compiler_params=pltpu.CompilerParams(collective_id=ident, has_side_effects=True),
    )(slabs)


def backward_kernel(
    ring, go_ref, q_ref, k_ref, kt_ref, vt_ref, o_ref, lse_ref, xa_ref, w_ref, mid_ref,
    out_ref, dw_ref, db_ref,
    g_ref, x_ref, v_ref, delta_ref, acc_ref, dk_ref, dv_ref, pq_ref, stage_ref, got_ref,
    total_ref, dx_ref, near_ref, far_ref, gsend, grecv, ksend, krecv, xsend, xrecv, lsem,
):
    r, s = lax.axis_index("rep"), lax.axis_index("shard")
    members = ring // GROUPS
    g, m = r // members, lax.rem(r, members)
    peers = [lax.rem(g + d, GROUPS) for d in range(1, GROUPS)]
    mates = [lax.rem(m + d, members) for d in range(1, members)]
    hello(
        [(p * members + m, s, True) for p in peers] + [(g * members + t, s, True) for t in mates]
    )
    loads = [
        pltpu.make_async_copy(xa_ref.at[j * members + m], x_ref.at[j], lsem.at[j])
        for j in range(GROUPS)
    ]
    for load in loads:
        load.start()

    def give(p):
        return remote(go_ref.at[p], g_ref.at[g], gsend.at[p], grecv.at[g], p * members + m, s)

    def take(p):
        return remote(go_ref.at[p], g_ref.at[p], gsend.at[p], grecv.at[p], p * members + m, s)

    for p in peers:
        give(p).start()
    g_ref[g] = go_ref[g]

    def turn(b, carry):
        rows = pl.ds(pl.multiple_of(b * BLOCK, BLOCK), BLOCK)
        for h in range(PER):
            v_ref[h, rows, :] = (
                vt_ref[b, h * HEAD_DIM : (h + 1) * HEAD_DIM, :].astype(F32).T.astype(BF16)
            )
        dk_ref[b] = jnp.zeros((SLAB, BLOCK), F32)
        dv_ref[b] = jnp.zeros((SLAB, BLOCK), F32)
        return carry

    lax.fori_loop(0, ring, turn, 0)
    total_ref[...] = jnp.zeros(total_ref.shape, F32)
    db_ref[...] = jnp.zeros(db_ref.shape, F32)

    def share(j, d):
        return remote(
            stage_ref.at[j, mates[d - 1]], got_ref.at[j, d - 1],
            ksend.at[j, d - 1], krecv.at[j, d - 1], g * members + mates[d - 1], s,
        )

    def attend_block(i):
        b = i * members + m
        pl.when(g != i)(lambda: take(i).wait_recv())
        for h in range(PER):
            head = pl.ds(h * HEAD_DIM, HEAD_DIM)
            delta_ref[h] = jnp.sum(
                g_ref[i, head, :].astype(F32) * o_ref[i, head, :], axis=0, keepdims=True
            )
        acc_ref[...] = jnp.zeros(acc_ref.shape, F32)

        def attend(kb, carry):
            keys = pl.ds(pl.multiple_of(kb * BLOCK, BLOCK), BLOCK)
            for h in range(PER):
                head = pl.ds(h * HEAD_DIM, HEAD_DIM)
                score = mm(k_ref[h, keys, :], q_ref[i, h])
                probs = jnp.exp(score - lse_ref[i, h])
                grad = g_ref[i, head, :]
                moved = (probs * (mm(v_ref[h, keys, :], grad) - delta_ref[h])).astype(BF16)
                acc_ref[h] += mm(kt_ref[kb, head, :], moved)
                dk_ref[kb, head, :] += mm(q_ref[i, h, :HEAD_DIM, :], moved, NT)
                dv_ref[kb, head, :] += mm(grad, probs.astype(BF16), NT)
            return carry

        lax.fori_loop(0, b + 1, attend, 0)
        for h in range(PER):
            pq_ref[i, pl.ds(h * HEAD_DIM, HEAD_DIM), :] = (
                acc_ref[h] * HEAD_DIM ** (-0.5)
            ).astype(BF16)
        for t in range(members):
            stage_ref[i, t, :SLAB, :] = dk_ref[i * members + t].astype(BF16)
            stage_ref[i, t, SLAB:, :] = dv_ref[i * members + t].astype(BF16)
        for d in range(1, members):
            share(i, d).start()

    def send_dx(j):
        return remote(
            dx_ref.at[j], far_ref.at[g], xsend.at[j], xrecv.at[g], j * members + m, s
        )

    def finish_block(j):
        b = j * members + m
        for d in range(1, members):
            share(j, d).wait_recv()
        dk, dv = dk_ref[b], dv_ref[b]
        for d in range(1, members):
            dk = dk + got_ref[j, d - 1, :SLAB, :].astype(F32)
            dv = dv + got_ref[j, d - 1, SLAB:, :].astype(F32)
        proj = jnp.concatenate([pq_ref[j], dk.astype(BF16), dv.astype(BF16)], axis=0)
        db_ref[...] += jnp.sum(proj.astype(F32), axis=1, keepdims=True)
        loads[j].wait()
        total_ref[...] += mm(x_ref[j], proj.T, (((0,), (0,)), ((), ())))
        dx = mm(proj, w_ref[...], (((0,), (0,)), ((), ())))

        @pl.when(g == j)
        def _():
            near_ref[...] = dx

        @pl.when(g != j)
        def _():
            dx_ref[j] = dx.astype(BF16)
            send_dx(j).start()

    order = list(range(GROUPS))[::-1]
    for at, i in enumerate(order):
        attend_block(i)
        if at:
            finish_block(order[at - 1])
    finish_block(order[-1])
    dw_ref[...] = total_ref[...].astype(BF16)
    result = near_ref[...] + mid_ref[...]
    for p in peers:
        remote(dx_ref.at[0], far_ref.at[p], xsend.at[0], xrecv.at[p], r, s).wait_recv()
        result = result + far_ref[p].astype(F32)
    out_ref[...] = result.astype(BF16)
    for p in peers:
        give(p).wait_send()
    for j in range(GROUPS):
        for d in range(1, members):
            share(j, d).wait_send()
        pl.when(g != j)(lambda: send_dx(j).wait_send())


def attention_backward(ring, grads, q, k, kt, vt, o, lse, x_all, w_group, mid, ident):
    members = ring // GROUPS
    width = x_all.shape[-1]
    shape = jax.ShapeDtypeStruct
    dma = pltpu.SemaphoreType.DMA
    vmem = pltpu.VMEM
    return pl.pallas_call(
        lambda *refs: backward_kernel(ring, *refs),
        out_shape=(
            shape((BLOCK, width), BF16), shape((width, 3 * SLAB), BF16), shape((3 * SLAB, 1), F32),
        ),
        in_specs=[VMEM_SPEC] * 7 + [ANY_SPEC] + [VMEM_SPEC] * 2,
        out_specs=(VMEM_SPEC,) * 3,
        scratch_shapes=[
            vmem((GROUPS, SLAB, BLOCK), BF16),
            vmem((GROUPS, BLOCK, width), BF16),
            vmem((PER, ring * BLOCK, HEAD_DIM), BF16),
            vmem((PER, 1, BLOCK), F32),
            vmem((PER, HEAD_DIM, BLOCK), F32),
            vmem((ring, SLAB, BLOCK), F32),
            vmem((ring, SLAB, BLOCK), F32),
            vmem((GROUPS, SLAB, BLOCK), BF16),
            vmem((GROUPS, members, 2 * SLAB, BLOCK), BF16),
            vmem((GROUPS, members - 1, 2 * SLAB, BLOCK), BF16),
            vmem((width, 3 * SLAB), F32),
            vmem((GROUPS, BLOCK, width), BF16),
            vmem((BLOCK, width), F32),
            vmem((GROUPS, BLOCK, width), BF16),
            dma((GROUPS,)), dma((GROUPS,)),
            dma((GROUPS, members - 1)), dma((GROUPS, members - 1)),
            dma((GROUPS,)), dma((GROUPS,)), dma((GROUPS,)),
        ],
        compiler_params=pltpu.CompilerParams(
            collective_id=ident, has_side_effects=True, vmem_limit_bytes=VMEM_LIMIT
        ),
    )(grads, q, k, kt, vt, o, lse, x_all, w_group, mid)


class Links:
    def __init__(self, ring, shards):
        self.ring, self.shards = ring, shards
        self.r, self.s = lax.axis_index("rep"), lax.axis_index("shard")
        self.levels = ring // 4
        self.z, self.c = self.r // 4, lax.rem(self.r, 2)
        self.y = lax.rem(self.r // 2, 2)
        self.sib = self.r + 1 - 2 * self.c
        self.yn = self.r + 2 - 4 * self.y
        self.others = [lax.rem(self.s + d, shards) for d in range(1, shards)]
        self.heights = [lax.rem(self.z + d, self.levels) for d in range(1, self.levels)]
        self.line = lax.rem(self.r, 4)

    def partners(self):
        return (
            [(self.sib, self.s, True), (self.yn, self.s, True)]
            + [(self.r, t, True) for t in self.others]
            + [(h * 4 + self.line, self.s, True) for h in self.heights]
        )


def add_rows(out, terms):
    total = terms[0][...].astype(F32)
    for term in terms[1:]:
        total = total + term[...].astype(F32)
    out[...] = total.astype(out.dtype)


def reduce_steps(net, slab, out, own, near, side, mate, tall, sems, group):
    asend, arecv, bsend, brecv, csend, crecv, dsend, drecv, esend, erecv, fsend, frecv, gsend, grecv, lsem = sems
    r, s, z, y, c = net.r, net.s, net.z, net.y, net.c
    base = z // group * group
    zz = lax.rem(z, group)
    inner = [lax.rem(zz + d, group) for d in range(1, group)]
    near_copy = lambda: remote(slab(1 - c), near, asend, arecv, net.sib, s)
    own_copy = lambda: pltpu.make_async_copy(slab(c), own, lsem)
    across = lambda d: remote(
        near.at[net.others[d]], side.at[d], bsend.at[d], brecv.at[d], r, net.others[d]
    )
    over = lambda: remote(near.at[s, 1 - y], mate, csend, crecv, net.yn, s)
    along = lambda d: remote(
        near.at[s, y, inner[d]], tall.at[d], dsend.at[d], drecv.at[d],
        (base + inner[d]) * 4 + net.line, s,
    )
    mine = out.at[c, y, z]
    spread = lambda d: remote(
        mine, mine, esend.at[d], erecv.at[d], net.heights[d] * 4 + net.line, s
    )
    pair = lambda: remote(out.at[c, y], out.at[c, y], fsend, frecv, net.yn, s)
    last = lambda: remote(out.at[c], out.at[c], gsend, grecv, net.sib, s)
    n_side, n_inner, n_tall = len(net.others), len(inner), len(net.heights)

    def step0():
        near_copy().start()
        own_copy().start()

    def step1():
        near_copy().wait_recv()
        own_copy().wait()
        for t in range(net.shards):
            for half in range(2):
                add_rows(near.at[t, half], [own.at[t, half], near.at[t, half]])
        for d in range(n_side):
            across(d).start()

    def step2():
        for d in range(n_side):
            across(d).wait_recv()
        for half in range(2):
            add_rows(
                near.at[s, half], [near.at[s, half]] + [side.at[d, half] for d in range(n_side)]
            )
        over().start()

    def step3():
        over().wait_recv()
        add_rows(near.at[s, y], [near.at[s, y], mate])
        for d in range(n_inner):
            along(d).start()

    def step4():
        for d in range(n_inner):
            along(d).wait_recv()
        add_rows(mine, [near.at[s, y, zz]] + [tall.at[d] for d in range(n_inner)])
        for d in range(n_tall):
            spread(d).start()

    def step5():
        for d in range(n_tall):
            spread(d).wait_recv()
        pair().start()

    def step6():
        pair().wait_recv()
        last().start()

    def step7():
        last().wait_recv()

    def drain():
        near_copy().wait_send()
        for d in range(n_side):
            across(d).wait_send()
        over().wait_send()
        for d in range(n_inner):
            along(d).wait_send()
        for d in range(n_tall):
            spread(d).wait_send()
        pair().wait_send()
        last().wait_send()

    return [step0, step1, step2, step3, step4, step5, step6, step7], drain


def reduce_scratch(shards, levels, group, rows, cols):
    dma = pltpu.SemaphoreType.DMA
    vmem = pltpu.VMEM
    many = lambda n: dma((max(n, 1),))
    buffers = [
        vmem((shards, 2, group, rows, cols), BF16),
        vmem((shards, 2, group, rows, cols), BF16),
        vmem((max(shards - 1, 1), 2, group, rows, cols), BF16),
        vmem((group, rows, cols), BF16),
        vmem((max(group - 1, 1), rows, cols), BF16),
    ]
    sems = [
        dma(()), dma(()), many(shards - 1), many(shards - 1), dma(()), dma(()),
        many(group - 1), many(group - 1), many(levels - 1), many(levels - 1),
        dma(()), dma(()), dma(()), dma(()), dma(()),
    ]
    return buffers + sems


SCRATCH = 20


def small_steps(net, src, out, near, side, mate, tall, sems):
    asend, arecv, bsend, brecv, csend, crecv, dsend, drecv = sems
    r, s, z, y, c = net.r, net.s, net.z, net.y, net.c
    near_copy = lambda: remote(src, near.at[1], asend, arecv, net.sib, s)
    across = lambda d: remote(
        near.at[0, net.others[d]], side.at[s], bsend.at[d], brecv.at[d], r, net.others[d]
    )
    over = lambda: remote(mate.at[0], mate.at[1], csend, crecv, net.yn, s)
    along = lambda d: remote(
        tall.at[z], tall.at[z], dsend.at[d], drecv.at[d], net.heights[d] * 4 + net.line, s
    )

    def step0():
        near_copy().start()

    def step1():
        near_copy().wait_recv()
        near[0] = src[...] + near[1]
        side[s] = near[0, s]
        for d in range(len(net.others)):
            across(d).start()

    def step2():
        for d in range(len(net.others)):
            across(d).wait_recv()
        total = side[0]
        for t in range(1, net.shards):
            total = total + side[t]
        mate[0] = total
        over().start()

    def step3():
        over().wait_recv()
        tall[z] = mate[0] + mate[1]
        for d in range(len(net.heights)):
            along(d).start()

    def step4():
        for d in range(len(net.heights)):
            along(d).wait_recv()
        total = tall[0]
        for t in range(1, net.levels):
            total = total + tall[t]
        out[...] = total

    def drain():
        near_copy().wait_send()
        for d in range(len(net.others)):
            across(d).wait_send()
        over().wait_send()
        for d in range(len(net.heights)):
            along(d).wait_send()

    return [step0, step1, step2, step3, step4], drain


def small_scratch(shards, levels, rows):
    dma = pltpu.SemaphoreType.DMA
    vmem = pltpu.VMEM
    return [
        vmem((2, shards, rows, LANES), F32), vmem((shards, rows, LANES), F32),
        vmem((2, rows, LANES), F32), vmem((levels, rows, LANES), F32),
        dma(()), dma(()), dma((max(shards - 1, 1),)), dma((max(shards - 1, 1),)),
        dma(()), dma(()), dma((levels - 1,)), dma((levels - 1,)),
    ]


def run_steps(jobs):
    deepest = max(at + len(steps) for at, (steps, _) in enumerate(jobs))
    for tick in range(deepest):
        for at in range(len(jobs)):
            steps = jobs[at][0]
            if 0 <= tick - at < len(steps):
                steps[tick - at]()
    for _, drain in jobs:
        drain()


def total_kernel(ring, shards, specs, *refs):
    n_in = 1 + max(spec[0] for spec in specs)
    terms, small, outs, small_out = refs[:n_in], refs[n_in], refs[n_in + 1 : 2 * n_in + 1], refs[2 * n_in + 1]
    rest = refs[2 * n_in + 2 :]
    net = Links(ring, shards)
    hello(net.partners())
    jobs = []
    for number, (which, k, core_first, group) in enumerate(specs):
        scratch = rest[number * SCRATCH : (number + 1) * SCRATCH]
        ref = terms[which]
        if core_first:
            slab = lambda core, ref=ref, k=k: ref.at[k, core]
        else:
            slab = lambda core, ref=ref, k=k: ref.at[:, k, core]
        jobs.append(reduce_steps(net, slab, outs[which].at[k], *scratch[:5], scratch[5:], group))
    scratch = rest[len(specs) * SCRATCH :]
    jobs.insert(1, small_steps(net, small, small_out, *scratch[:4], scratch[4:]))
    run_steps(jobs)


def total_all(terms, orders, groups, small, ring, shards, ident):
    shape = jax.ShapeDtypeStruct
    levels = ring // 4
    specs, scratch, out_shape = [], [], []
    for i, (term, core_first, group) in enumerate(zip(terms, orders, groups)):
        chunks = term.shape[0] if core_first else term.shape[1]
        rows, cols = term.shape[-2:]
        out_shape.append(shape((chunks, 2, 2, levels, rows, cols), BF16))
        for k in range(chunks):
            specs.append((i, k, core_first, group))
            scratch += reduce_scratch(shards, levels, group, rows, cols)
    scratch += small_scratch(shards, levels, small.shape[1])
    out_shape.append(shape(small.shape[1:], F32))
    return pl.pallas_call(
        lambda *refs: total_kernel(ring, shards, specs, *refs),
        out_shape=tuple(out_shape),
        in_specs=[ANY_SPEC] * len(terms) + [VMEM_SPEC],
        out_specs=(VMEM_SPEC,) * (len(terms) + 1),
        scratch_shapes=scratch,
        compiler_params=pltpu.CompilerParams(
            collective_id=ident, has_side_effects=True, vmem_limit_bytes=VMEM_LIMIT
        ),
    )(*terms, small)


def layer_norm(hidden, gain, shift):
    centre = hidden - jnp.mean(hidden, axis=-1, keepdims=True)
    inverse = lax.rsqrt(jnp.mean(centre * centre, axis=-1, keepdims=True) + EPSILON)
    normed = centre * inverse
    return (normed * gain + shift, normed, inverse)


def norm_back(grad_output, normed, inverse, gain):
    grad_normed = grad_output * gain
    centred = grad_normed - jnp.mean(grad_normed, axis=-1, keepdims=True)
    return inverse * (centred - normed * jnp.mean(grad_normed * normed, axis=-1, keepdims=True))


def gelu_slope(value):
    return (
        0.5 * (1.0 + lax.erf(value * 0.7071067811865476))
        + value * jnp.exp(-0.5 * value * value) * 0.3989422804014327
    )


def on_device(
    tokens, doc_ids, qkv_weight, qv_bias, out_weight, out_bias, mid_gain, mid_shift,
    up_weight, up_bias, down_weight, down_bias, end_gain, end_shift, out_grad,
):
    width = tokens.shape[2]
    ring = lax.axis_size("rep")
    members = ring // GROUPS
    r = lax.axis_index("rep")
    g = r // members
    m = lax.rem(r, members)

    shards = lax.axis_size("shard")
    x = tokens[0]
    local = jnp.concatenate(
        [lax.dynamic_slice_in_dim(qkv_weight, t * width + g * SLAB, SLAB, 1) for t in range(3)], 1
    )
    small = (qv_bias, out_bias, mid_gain, mid_shift, up_bias, down_bias, end_gain, end_shift)
    sizes = [v.shape[0] for v in small]
    flat = jnp.concatenate(small)
    lanes = 128
    flat = jnp.pad(flat, (0, -flat.shape[0] % (32 * lanes))).reshape(-1, lanes)
    x_all, w_group, flat, full_out, full_up, full_down = gather_all(
        x, (local, flat, out_weight, up_weight, down_weight), (1, 1, 1, 2, 2), ring, shards
    )

    def whole(gathered, mine):
        put = lax.dynamic_update_index_in_dim(gathered, mine, lax.axis_index("shard"), 0)
        return put.reshape(shards * mine.shape[0], *mine.shape[1:])

    x_all = x_all.reshape(ring * BLOCK, width)
    w_group = whole(w_group, local).T
    flat_own = jnp.pad(jnp.concatenate(small), (0, -sum(sizes) % (32 * lanes)))
    flat = whole(flat.reshape(shards, -1), flat_own).reshape(shards, -1).astype(F32)
    vectors = []
    at = 0
    for size in sizes:
        vectors.append(flat[:, at : at + size].reshape(-1))
        at += size
    vec_qv, vec_out, gain_mid, shift_mid, vec_up, vec_down, gain_end, shift_end = vectors
    full_out, full_up, full_down = (
        whole(full_out, out_weight), whole(full_up, up_weight), whole(full_down, down_weight)
    )
    bias = jnp.concatenate(
        [
            lax.dynamic_slice_in_dim(vec_qv, g * SLAB, SLAB, 0),
            jnp.zeros((SLAB,), F32),
            lax.dynamic_slice_in_dim(vec_qv, width + g * SLAB, SLAB, 0),
        ]
    )
    bias = jnp.concatenate([bias[:SLAB], bias[2 * SLAB :]]).reshape(2 * SLAB, 1)
    docs = doc_ids.reshape(ring, 1, BLOCK).astype(F32)
    o, o_low, lse, q, k, kt, vt = attention_forward(x_all, w_group, bias, docs, members)
    attended_t = exchange_slabs(o_low, ring, 1).reshape(width, BLOCK)

    attended_low = attended_t.T
    branch = mm(attended_low, full_out) + vec_out
    mid_out, mid_norm, mid_inv = layer_norm(x.astype(F32) + branch, gain_mid, shift_mid)
    mid_low = mid_out.astype(BF16)
    pre_act = mm(mid_low, full_up) + vec_up
    activated = jax.nn.gelu(pre_act, approximate=False).astype(BF16)
    ffn_out = mm(activated, full_down) + vec_down
    end_out, end_norm, end_inv = layer_norm(mid_out + ffn_out, gain_end, shift_end)
    layer_out = end_out.astype(BF16)
    grad_top = out_grad[0].astype(F32)
    grad_end_gain = jnp.sum(grad_top * end_norm, axis=0)
    grad_end_shift = jnp.sum(grad_top, axis=0)
    grad_end_in = norm_back(grad_top, end_norm, end_inv, gain_end)
    grad_ffn = grad_end_in.astype(BF16)
    grad_down_bias = jnp.sum(grad_ffn.astype(F32), axis=0)
    grad_down_weight = mm(activated.T, grad_ffn)
    grad_act = mm(grad_ffn, full_down, NT)
    grad_pre = (grad_act * gelu_slope(pre_act)).astype(BF16)
    grad_up_bias = jnp.sum(grad_pre.astype(F32), axis=0)
    grad_up_weight = mm(mid_low.T, grad_pre)
    grad_mid_out = mm(grad_pre, full_up, NT) + grad_end_in
    grad_mid_gain = jnp.sum(grad_mid_out * mid_norm, axis=0)
    grad_mid_shift = jnp.sum(grad_mid_out, axis=0)
    grad_mid_in = norm_back(grad_mid_out, mid_norm, mid_inv, gain_mid)
    grad_branch = grad_mid_in.astype(BF16)
    grad_out_bias = jnp.sum(grad_branch.astype(F32), axis=0)
    grad_out_weight = mm(attended_t, grad_branch)
    grad_attended_t = mm(full_out, grad_branch, NT).astype(BF16)
    input_grad, dw_group, dbias = attention_backward(
        ring, grad_attended_t.reshape(GROUPS, SLAB, BLOCK), q, k, kt, vt, o, lse,
        x_all.reshape(ring, BLOCK, width), w_group, grad_mid_in, 2,
    )

    levels = ring // 4
    sub = levels // GROUPS
    hidden = up_weight.shape[1]
    down_chunks = 6 if down_weight.shape[0] % (6 * ring * 16) == 0 else 1
    down_terms = grad_down_weight.astype(BF16).reshape(
        shards, down_chunks, 2, 2, levels, -1, width
    )
    up_chunks = 6
    up_terms = grad_up_weight.astype(BF16).reshape(width, up_chunks, 2, -1).transpose(1, 2, 0, 3)
    up_terms = up_terms.reshape(up_chunks, 2, shards, 2, levels, -1, hidden // up_chunks // 2)
    out_terms = grad_out_weight.astype(BF16).reshape(width, 1, 2, -1).transpose(1, 2, 0, 3)
    out_terms = out_terms.reshape(1, 2, shards, 2, levels, -1, width // 2)
    qkv_terms = dw_group.reshape(shards, 1, 2, 2, sub, -1, 3 * SLAB)
    qv = dbias.reshape(3, SLAB)[jnp.array([0, 2])]
    grad_qv_bias = lax.dynamic_update_slice_in_dim(
        jnp.zeros((2, GROUPS, SLAB), F32), qv.reshape(2, 1, SLAB), g, 1
    ).reshape(2 * width)
    vectors = (
        grad_qv_bias, grad_out_bias, grad_mid_gain, grad_mid_shift, grad_up_bias, grad_down_bias,
        grad_end_gain, grad_end_shift,
    )
    flat = jnp.concatenate([v.reshape(shards, -1) for v in vectors], axis=1)
    flat = jnp.pad(flat, ((0, 0), (0, -flat.shape[1] % (8 * LANES)))).reshape(shards, -1, LANES)
    down, up, out, qkv, flat = total_all(
        (down_terms, up_terms, out_terms, qkv_terms), (False, True, True, False),
        (levels, levels, levels, sub), flat, ring, shards, 3,
    )
    total_down = down.reshape(-1, width).astype(F32)
    total_up = up.reshape(up_chunks * 2, width // shards, -1).transpose(1, 0, 2)
    total_up = total_up.reshape(-1, hidden).astype(F32)
    total_out = out.reshape(2, width // shards, -1).transpose(1, 0, 2)
    total_out = total_out.reshape(-1, width).astype(F32)
    total_qkv = qkv.reshape(2, 2, GROUPS, sub, -1, 3, SLAB).transpose(0, 1, 3, 4, 5, 2, 6)
    total_qkv = total_qkv.reshape(-1, 3 * width).astype(F32)
    flat = flat.reshape(-1)
    totals, at = [], 0
    for size in sizes:
        totals.append(flat[at : at + size])
        at += size
    return (
        layer_out[None], input_grad[None], total_qkv, totals[0], total_out, totals[1], totals[2],
        totals[3], total_up, totals[4], total_down, totals[5], totals[6], totals[7],
    )


def solution(mesh):
    rows = P("shard", None)
    flat = P("shard")
    acts = P("shard", "rep", None)
    in_specs = (
        acts, rows, rows, flat, rows, flat, flat, flat, rows, flat, rows, flat, flat, flat, acts
    )
    out_specs = (acts, acts, rows, flat, rows, flat, flat, flat, rows, flat, rows, flat, flat, flat)
    return jax.shard_map(
        on_device, mesh=mesh, in_specs=in_specs, out_specs=out_specs, check_vma=False
    )
```

```python
import jax
import jax.numpy as jnp
from jax import lax
from jax.experimental import pallas as pl
from jax.experimental.pallas import tpu as pltpu
from jax.sharding import PartitionSpec as P

HEADS = 12
HEAD_DIM = 64
BLOCK = 256
GROUPS = 4
PER = HEADS // GROUPS
SLAB = PER * HEAD_DIM
EPSILON = 1e-05
FAR = 2.0**100
F32 = jnp.float32
BF16 = jnp.bfloat16
LANES = 128
NN = (((1,), (0,)), ((), ()))
NT = (((1,), (1,)), ((), ()))
TN = (((0,), (0,)), ((), ()))
VMEM_SPEC = pl.BlockSpec(memory_space=pltpu.VMEM)
VMEM_LIMIT = 67043328


def mm(left, right, dims=NN):
    return lax.dot_general(left, right, dims, preferred_element_type=F32)


ANY_SPEC = pl.BlockSpec(memory_space=pl.ANY)


def remote(src, dst, send, recv, rep, shard):
    return pltpu.make_async_remote_copy(
        src_ref=src, dst_ref=dst, send_sem=send, recv_sem=recv,
        device_id=(rep, shard), device_id_type=pl.DeviceIdType.MESH,
    )


def hello(partners):
    barrier = pltpu.get_barrier_semaphore()
    total = 0
    for rep, shard, there in partners:
        if there is True:
            pl.semaphore_signal(
                barrier, inc=1, device_id=(rep, shard), device_id_type=pl.DeviceIdType.MESH
            )
            total = total + 1
        else:

            @pl.when(there)
            def _():
                pl.semaphore_signal(
                    barrier, inc=1, device_id=(rep, shard), device_id_type=pl.DeviceIdType.MESH
                )

            total = total + there.astype(jnp.int32)
    pl.semaphore_wait(barrier, total)


class Links:
    def __init__(self, ring, shards):
        self.ring, self.shards = ring, shards
        self.r, self.s = lax.axis_index("rep"), lax.axis_index("shard")
        self.levels = ring // 4
        self.z, self.c = self.r // 4, lax.rem(self.r, 2)
        self.y = lax.rem(self.r // 2, 2)
        self.sib = self.r + 1 - 2 * self.c
        self.yn = self.r + 2 - 4 * self.y
        self.others = [lax.rem(self.s + d, shards) for d in range(1, shards)]
        self.heights = [lax.rem(self.z + d, self.levels) for d in range(1, self.levels)]
        self.line = lax.rem(self.r, 4)

    def partners(self):
        return (
            [(self.sib, self.s, True), (self.yn, self.s, True)]
            + [(self.r, t, True) for t in self.others]
            + [(h * 4 + self.line, self.s, True) for h in self.heights]
        )


def forward_kernel(ring, shards, parts, sizes, *refs):
    n_vec = len(sizes)
    x_ref, w_ref, docs_ref = refs[:3]
    vec_refs, own = refs[3 : 3 + n_vec], refs[3 + n_vec : 6 + n_vec]
    outs, rest = refs[6 + n_vec : 19 + n_vec], refs[19 + n_vec :]
    att_ref, flat_ref, wg_ref, lse_ref, o_out, q_out, k_out, kt_out, vt_out, xr_out = outs[:10]
    full = outs[10:]
    (
        xa_ref, wl_ref, low_ref, bias_ref, o_ref, q_ref, k_ref, kt_ref, vt_ref, top_ref, sum_ref,
        send, recv, wsend, wrecv, fsend, frecv, vsend, vrecv, asend, arecv, osem,
    ) = rest
    net = Links(ring, shards)
    r, s, z, y, c = net.r, net.s, net.z, net.y, net.c
    levels, members = net.levels, ring // GROUPS
    g, m = r // members, lax.rem(r, members)
    sib, yn, line, others = net.sib, net.yn, net.line, net.others
    above, below = z < levels - 1, z > 0
    hello(net.partners())

    def move(b, kind, src=None):
        target = (r + 4, r - 4, yn, sib)[kind]
        src = xa_ref.at[b] if src is None else src
        return remote(src, xa_ref.at[b], send.at[kind, b], recv.at[b], target, s)

    pl.when(above)(lambda: move(r, 0, x_ref).start())
    pl.when(below)(lambda: move(r, 1, x_ref).start())
    move(r, 2, x_ref).start()
    move(r, 3, x_ref).start()
    xa_ref[r] = x_ref[...]

    width = x_ref.shape[1]
    for k in range(GROUPS):

        @pl.when(g == k)
        def _():
            wl_ref[s] = jnp.concatenate(
                [w_ref[:, t * width + k * SLAB : t * width + (k + 1) * SLAB] for t in range(3)], 1
            )

    flat_ref[s] = jnp.concatenate([v[...].astype(F32) for v in vec_refs], axis=1)
    lists = [
        remote(flat_ref.at[s], flat_ref.at[s], vsend.at[d], vrecv.at[d], r, t)
        for d, t in enumerate(others)
    ]
    pieces = [(lambda rows: wl_ref.at[s, rows], wl_ref, w_ref.shape[0] // 2, 0, False)]
    for w, first, count, quad in parts:
        size = own[w].shape[0] // (4 if quad else 2) // count
        for j in range(count):
            pieces.append((lambda rows, w=w: own[w].at[rows], full[w], size, (count, j), quad))

    def span(piece, yy, cc):
        size, where, quad = piece[2:]
        count, j = where or (1, 0)
        part = (yy * 2 + cc) if quad else cc
        return pl.ds(pl.multiple_of((part * count + j) * size, size), size)

    def across(at, d):
        rows = span(pieces[at], y, c)
        return remote(
            pieces[at][0](rows), pieces[at][1].at[s, rows], wsend.at[at, d], wrecv.at[at, d],
            r, others[d],
        )

    def shifted(at, d, kind, yy, cc, target):
        rows = span(pieces[at], yy, cc)
        spot = pieces[at][1].at[others[d], rows]
        return remote(spot, spot, fsend.at[at, d, kind], frecv.at[at, d, kind], target, s)

    def relay(at):
        for d in range(shards - 1):
            across(at, d).wait_recv()
            shifted(at, d, 0, y, c, sib).start()
            if pieces[at][4]:
                shifted(at, d, 1, y, c, yn).start()

    def relay_far(at):
        for d in range(shards - 1):
            shifted(at, d, 1, 1 - y, c, yn).wait_recv()
            shifted(at, d, 2, 1 - y, c, sib).start()

    def relayed(at):
        for d in range(shards - 1):
            shifted(at, d, 0, y, 1 - c, sib).wait_recv()
            if pieces[at][4]:
                shifted(at, d, 2, 1 - y, 1 - c, sib).wait_recv()

    for copy in lists:
        copy.start()
    for at in range(len(pieces)):
        for d in range(shards - 1):
            across(at, d).start()
    relay(0)
    for copy in lists:
        copy.wait_recv()
    n0 = sizes[0]
    qv = jnp.concatenate([flat_ref[t, :, :n0] for t in range(shards)], axis=1)
    for k in range(GROUPS):

        @pl.when(g == k)
        def _():
            row = jnp.concatenate(
                [qv[:, k * SLAB : (k + 1) * SLAB], qv[:, width + k * SLAB : width + (k + 1) * SLAB]],
                axis=1,
            )
            bias_ref[...] = jnp.broadcast_to(row, (8, 2 * SLAB)).T[:, :1]

    relayed(0)
    part = width // shards
    for t in range(shards):
        wg_ref[:, t * part : (t + 1) * part] = wl_ref[t].astype(F32).T.astype(BF16)

    def level(q):
        lo, hi = z, levels - 1 - z
        turn = jnp.minimum(lo, hi)
        swing = jnp.where(lax.rem(q, 2) == 1, z - (q + 1) // 2, z + q // 2)
        rest = jnp.where(lo > hi, z - (q - turn), z + (q - turn))
        return jnp.where(q <= 2 * turn, swing, rest)

    def event(n):
        k, t = (n - 2) // 4, lax.rem(n + 2, 4)
        q = jnp.where(n < 2, 0, jnp.where(lax.rem(t, 2) == 0, k + 1, k))
        j = jnp.where(n < 2, 2 * n, t)
        q = jnp.where(n >= ring - 2, levels - 1, q)
        j = jnp.where(n >= ring - 2, 2 * (n - ring + 2) + 1, j)
        lv = level(q)
        return lv * 4 + lax.rem(y + lax.rem(j, 2), 2) * 2 + lax.rem(c + j // 2, 2), lv, j

    sub = levels // GROUPS

    def arrive(n):
        b, lv, j = event(n)

        @pl.when(n > 0)
        def _():
            move(b, 3).wait_recv()

            @pl.when(j == 0)
            def _():
                pl.when(jnp.logical_and(lv < z, above))(lambda: move(b, 0).start())
                pl.when(jnp.logical_and(lv > z, below))(lambda: move(b, 1).start())
                move(b, 2).start()

            pl.when(j < 2)(lambda: move(b, 3).start())

        both = mm(wg_ref[SLAB:, :], xa_ref[b], NT)
        kt = both[:SLAB].astype(BF16)
        kt_ref[b] = kt
        vt_ref[b] = (both[SLAB:] + bias_ref[SLAB:, :]).astype(BF16)
        at = pl.multiple_of(b * BLOCK, BLOCK)
        docs = docs_ref[:, pl.ds(at, BLOCK)].astype(F32)
        blank = jnp.zeros((HEAD_DIM - 2, BLOCK), F32)
        extra = jnp.concatenate([docs * FAR - FAR, docs * (-FAR), blank], axis=0)
        for h in range(PER):
            part = kt[h * HEAD_DIM : (h + 1) * HEAD_DIM].astype(F32)
            k_ref[h, pl.ds(at, BLOCK), :] = jnp.concatenate([part, extra], axis=0).T.astype(BF16)

        @pl.when(jnp.logical_and(j == 0, lax.rem(lv, sub) == lax.rem(z, sub)))
        def _():
            i = lv // sub
            qt = (mm(wg_ref[:SLAB, :], xa_ref[b], NT) + bias_ref[:SLAB, :]).astype(BF16)
            qt = qt.astype(F32) * HEAD_DIM ** (-0.5)
            extra = jnp.concatenate([docs, 1.0 - docs, blank], axis=0)
            for h in range(PER):
                part = qt[h * HEAD_DIM : (h + 1) * HEAD_DIM]
                q_ref[i, h] = jnp.concatenate([part, extra], axis=0).astype(BF16)

    def unit(i, kb):
        keys = pl.ds(pl.multiple_of(kb * BLOCK, BLOCK), BLOCK)
        for h in range(PER):
            head = pl.ds(h * HEAD_DIM, HEAD_DIM)
            score = mm(k_ref[h, keys, :], q_ref[i, h])
            old = top_ref[i, h]
            new = jnp.maximum(old, jnp.max(score, axis=0, keepdims=True))
            probs = jnp.exp(score - new)
            shrink = jnp.exp(old - new)
            top_ref[i, h] = new
            sum_ref[i, h] = sum_ref[i, h] * shrink + jnp.sum(probs, axis=0, keepdims=True)
            o_ref[i, head, :] = o_ref[i, head, :] * shrink + mm(
                vt_ref[kb, head, :], probs.astype(BF16)
            )

    def attend(n):
        b, lv, j = event(n)
        first = jnp.logical_and(j == 0, lax.rem(lv, sub) == lax.rem(z, sub))
        known = jnp.where(n < 2, 1, jnp.minimum((n - 2) // 4 + 2, levels))

        def pair(u, carry):
            near = u < known
            seen = level(jnp.minimum(u, known - 1))
            old = event(jnp.maximum(u - known, 0))[0]
            i = jnp.where(near, seen, lv) // sub
            kb = jnp.where(near, b, old)
            query = i * members + m
            mine = jnp.where(near, lax.rem(seen, sub) == lax.rem(z, sub), old < b)
            pl.when(jnp.logical_and(mine, kb <= query))(lambda: unit(i, kb))
            return carry

        lax.fori_loop(0, known + jnp.where(first, n, 0), pair, 0)

    top_ref[...] = jnp.full(top_ref.shape, -jnp.inf, F32)
    sum_ref[...] = jnp.zeros(sum_ref.shape, F32)
    o_ref[...] = jnp.zeros(o_ref.shape, F32)
    lag = 5
    turn_on = ring - 5

    def advance(n, carry):
        pl.when(n < ring)(lambda: arrive(n))

        @pl.when(n == turn_on)
        def _():
            for at in range(len(pieces)):
                if pieces[at][4]:
                    relay(at)

        pl.when(n >= lag)(lambda: attend(n - lag))
        return carry

    lax.fori_loop(0, ring + lag, advance, 0)
    saves = [
        pltpu.make_async_copy(src, dst, osem.at[n])
        for n, (src, dst) in enumerate(
            ((k_ref, k_out), (kt_ref, kt_out), (vt_ref, vt_out), (q_ref, q_out), (o_ref, o_out))
        )
    ]
    saves += [
        pltpu.make_async_copy(xa_ref.at[i * members + m], xr_out.at[i], osem.at[5 + i])
        for i in range(GROUPS)
    ]
    for save in saves[:3] + saves[5:]:
        save.start()

    def give(i):
        return remote(low_ref.at[i], att_ref.at[g], asend.at[i], arecv.at[g], i * members + m, s)

    for i in range(GROUPS):
        for h in range(PER):
            head = pl.ds(h * HEAD_DIM, HEAD_DIM)
            out = o_ref[i, head, :] / sum_ref[i, h]
            o_ref[i, head, :] = out
            low_ref[i, head, :] = out.astype(BF16)
            lse_ref[i, h] = top_ref[i, h] + jnp.log(sum_ref[i, h])

        @pl.when(g == i)
        def _():
            att_ref[g] = low_ref[i]

        pl.when(g != i)(lambda: give(i).start())
    for save in saves[3:5]:
        save.start()
    for at in range(1, len(pieces)):
        if pieces[at][4]:
            relay_far(at)
        else:
            relay(at)
    for d in range(1, GROUPS):
        p = lax.rem(g + d, GROUPS)
        remote(low_ref.at[0], att_ref.at[p], asend.at[0], arecv.at[p], r, s).wait_recv()
    for at in range(1, len(pieces)):
        relayed(at)
    for i in range(GROUPS):
        pl.when(g != i)(lambda: give(i).wait_send())

    def sent(e, carry):
        b, lv, j = event(e)

        @pl.when(j == 0)
        def _():
            pl.when(jnp.logical_and(lv <= z, above))(lambda: move(b, 0).wait_send())
            pl.when(jnp.logical_and(lv >= z, below))(lambda: move(b, 1).wait_send())
            move(b, 2).wait_send()

        pl.when(j < 2)(lambda: move(b, 3).wait_send())
        return carry

    lax.fori_loop(0, ring, sent, 0)
    for copy in lists:
        copy.wait_send()
    for at in range(len(pieces)):
        for d in range(shards - 1):
            across(at, d).wait_send()
            shifted(at, d, 0, y, c, sib).wait_send()
            if pieces[at][4]:
                shifted(at, d, 1, y, c, yn).wait_send()
                shifted(at, d, 2, 1 - y, c, sib).wait_send()
    for save in saves:
        save.wait()


def forward_all(x, qkv_weight, docs, vectors, weights, parts, ring, shards, ident):
    shape = jax.ShapeDtypeStruct
    dma = pltpu.SemaphoreType.DMA
    vmem = pltpu.VMEM
    n = 1 + sum(part[2] for part in parts)
    width = x.shape[1]
    sizes = [v.shape[1] for v in vectors]
    per = max(shards - 1, 1)
    o = (GROUPS, SLAB, BLOCK)
    q = (GROUPS, PER, 2 * HEAD_DIM, BLOCK)
    k = (PER, ring * BLOCK, 2 * HEAD_DIM)
    t = (ring, SLAB, BLOCK)
    return pl.pallas_call(
        lambda *refs: forward_kernel(ring, shards, parts, sizes, *refs),
        out_shape=(
            shape(o, BF16), shape((shards, 1, sum(sizes)), F32), shape((3 * SLAB, width), BF16),
            shape((GROUPS, PER, 1, BLOCK), F32), shape(o, F32), shape(q, BF16), shape(k, BF16),
            shape(t, BF16), shape(t, BF16), shape((GROUPS,) + x.shape, BF16),
        )
        + tuple(shape((shards,) + w.shape, w.dtype) for w in weights),
        in_specs=[VMEM_SPEC] * (3 + len(vectors)) + [ANY_SPEC] * 3,
        out_specs=(VMEM_SPEC,) * 4 + (ANY_SPEC,) * 9,
        scratch_shapes=[
            vmem((ring,) + x.shape, BF16), vmem((shards, width // shards, 3 * SLAB), BF16),
            vmem(o, BF16), vmem((2 * SLAB, 1), F32), vmem(o, F32), vmem(q, BF16), vmem(k, BF16),
            vmem(t, BF16), vmem(t, BF16),
            vmem((GROUPS, PER, 1, BLOCK), F32), vmem((GROUPS, PER, 1, BLOCK), F32),
            dma((4, ring)), dma((ring,)), dma((n, per)), dma((n, per)), dma((n, per, 3)),
            dma((n, per, 3)), dma((per,)), dma((per,)),
            dma((GROUPS,)), dma((GROUPS,)), dma((5 + GROUPS,)),
        ],
        compiler_params=pltpu.CompilerParams(
            collective_id=ident, has_side_effects=True, vmem_limit_bytes=VMEM_LIMIT
        ),
    )(x, qkv_weight, docs, *vectors, *weights)


def layer_norm(hidden, gain, shift):
    centre = hidden - jnp.mean(hidden, axis=-1, keepdims=True)
    inverse = lax.rsqrt(jnp.mean(centre * centre, axis=-1, keepdims=True) + EPSILON)
    normed = centre * inverse
    return (normed * gain + shift, normed, inverse)


def norm_back(grad_output, normed, inverse, gain):
    grad_normed = grad_output * gain
    centred = grad_normed - jnp.mean(grad_normed, axis=-1, keepdims=True)
    return inverse * (centred - normed * jnp.mean(grad_normed * normed, axis=-1, keepdims=True))


def mlp_kernel(
    shards, sizes, att_ref, x_ref, og_ref, flat_ref, *refs,
):
    own, full = refs[:3], refs[3:6]
    out_ref, gat_ref, mid_ref, small_ref, down_out, up_out, outw_out = refs[6:13]
    wo_ref, wu_ref, wd_ref, act_ref, slope_ref, gd_ref, gu_ref, go_ref, lsem, ssem = refs[13:]
    s = lax.axis_index("shard")
    width = x_ref.shape[1]
    hidden = wu_ref.shape[1]
    loads = []
    for w, ref in enumerate((wo_ref, wu_ref, wd_ref)):
        size = own[w].shape[0]
        group = []
        for d in range(shards):
            t = lax.rem(s + d, shards)
            rows = pl.ds(pl.multiple_of(t * size, size), size)
            src = own[w] if d == 0 else full[w].at[t]
            group.append(pltpu.make_async_copy(src, ref.at[rows], lsem.at[w * shards + d]))
        loads.append(group)
        for load in group:
            load.start()

    def ready(w):
        for load in loads[w]:
            load.wait()

    starts = [sum(sizes[:n]) for n in range(len(sizes))]

    def vector(n):
        return jnp.concatenate(
            [flat_ref[t, :, starts[n] : starts[n] + sizes[n]] for t in range(shards)], axis=1
        )

    def put(n, row):
        for t in range(shards):
            small_ref[t, :, starts[n] : starts[n] + sizes[n]] = row[
                :, t * sizes[n] : (t + 1) * sizes[n]
            ]

    small_ref[...] = jnp.zeros(small_ref.shape, F32)
    att = att_ref[...].reshape(width, BLOCK)
    ready(0)
    branch = mm(att, wo_ref[...], TN) + vector(1)
    gain_mid = vector(2)
    mid_out, mid_norm, mid_inv = layer_norm(x_ref[...].astype(F32) + branch, gain_mid, vector(3))
    mid_low = mid_out.astype(BF16)
    up_bias = vector(4)
    cols = 512
    ready(1)
    for at in range(0, hidden, cols):
        block = slice(at, at + cols)
        pre = mm(mid_low, wu_ref[:, block]) + up_bias[:, block]
        phi = 0.5 * (1.0 + lax.erf(pre * 0.7071067811865476))
        act_ref[:, block] = (pre * phi).astype(BF16)
        slope_ref[:, block] = phi + pre * jnp.exp(-0.5 * pre * pre) * 0.3989422804014327
    ready(2)
    ffn = mm(act_ref[...], wd_ref[...]) + vector(5)
    gain_end = vector(6)
    end_out, end_norm, end_inv = layer_norm(mid_out + ffn, gain_end, vector(7))
    out_ref[...] = end_out.astype(BF16)
    top = og_ref[...].astype(F32)

    def column(value):
        return jnp.sum(value, axis=0, keepdims=True)

    put(6, column(top * end_norm))
    put(7, column(top))
    grad_end_in = norm_back(top, end_norm, end_inv, gain_end)
    grad_ffn = grad_end_in.astype(BF16)
    put(5, column(grad_ffn.astype(F32)))
    saves = []

    def save(src, dst):
        copy = pltpu.make_async_copy(src, dst, ssem.at[len(saves)])
        copy.start()
        saves.append(copy)

    chunks = gd_ref.shape[1]
    rows = hidden // shards // chunks
    for t in range(shards):
        for k in range(chunks):
            at = t * (hidden // shards) + k * rows
            value = mm(act_ref[:, at : at + rows], grad_ffn, TN)
            gd_ref[t, k] = value.astype(BF16).reshape(gd_ref.shape[2:])
        save(gd_ref.at[t], down_out.at[t])
    grad_mid_out = grad_end_in
    ups = []
    wide = hidden // gu_ref.shape[0]
    for k in range(gu_ref.shape[0]):
        block = slice(k * wide, (k + 1) * wide)
        grad_act = mm(grad_ffn, wd_ref[block, :], NT)
        grad_pre = (grad_act * slope_ref[:, block]).astype(BF16)
        ups.append(column(grad_pre.astype(F32)))
        value = mm(mid_low, grad_pre, TN).astype(BF16)
        for half in range(2):
            gu_ref[k, half] = value[:, half * (wide // 2) : (half + 1) * (wide // 2)].reshape(
                gu_ref.shape[2:]
            )
        save(gu_ref.at[k], up_out.at[k])
        grad_mid_out = grad_mid_out + mm(grad_pre, wu_ref[:, block], NT)
    put(4, jnp.concatenate(ups, axis=1))
    put(2, column(grad_mid_out * mid_norm))
    put(3, column(grad_mid_out))
    grad_mid_in = norm_back(grad_mid_out, mid_norm, mid_inv, gain_mid)
    mid_ref[...] = grad_mid_in
    grad_branch = grad_mid_in.astype(BF16)
    put(1, column(grad_branch.astype(F32)))
    gat_ref[...] = mm(wo_ref[...], grad_branch, NT).astype(BF16).reshape(gat_ref.shape)
    value = mm(att, grad_branch).astype(BF16)
    for half in range(2):
        go_ref[0, half] = value[:, half * (width // 2) : (half + 1) * (width // 2)].reshape(
            go_ref.shape[2:]
        )
    save(go_ref, outw_out)
    for copy in saves:
        copy.wait()


def mlp_all(att, x, out_grad, flat, own, full, sizes, shards, levels, down_chunks, up_chunks):
    shape = jax.ShapeDtypeStruct
    dma = pltpu.SemaphoreType.DMA
    vmem = pltpu.VMEM
    width, hidden = own[0].shape[1], own[1].shape[1]
    gd = (shards, down_chunks, 2, 2, levels, hidden // shards // down_chunks // 4 // levels, width)
    gu = (up_chunks, 2, shards, 2, levels, width // shards // 2 // levels, hidden // up_chunks // 2)
    go = (1, 2, shards, 2, levels, width // shards // 2 // levels, width // 2)
    return pl.pallas_call(
        lambda *refs: mlp_kernel(shards, sizes, *refs),
        out_shape=(
            shape((BLOCK, width), BF16), shape((GROUPS, SLAB, BLOCK), BF16),
            shape((BLOCK, width), F32), shape(flat.shape, F32),
            shape(gd, BF16), shape(gu, BF16), shape(go, BF16),
        ),
        in_specs=[VMEM_SPEC] * 4 + [ANY_SPEC] * 6,
        out_specs=(VMEM_SPEC,) * 4 + (ANY_SPEC,) * 3,
        scratch_shapes=[
            vmem((width, width), BF16), vmem((width, hidden), BF16), vmem((hidden, width), BF16),
            vmem((BLOCK, hidden), BF16), vmem((BLOCK, hidden), F32),
            vmem(gd, BF16), vmem(gu, BF16), vmem(go, BF16),
            dma((3 * shards,)), dma((shards + up_chunks + 1,)),
        ],
        compiler_params=pltpu.CompilerParams(vmem_limit_bytes=VMEM_LIMIT),
    )(att, x, out_grad, flat, *own, *full)


def add_rows(out, terms):
    total = terms[0][...].astype(F32)
    for term in terms[1:]:
        total = total + term[...].astype(F32)
    out[...] = total.astype(out.dtype)


def reduce_steps(net, slab, out, own, near, side, mate, tall, sems, group):
    asend, arecv, bsend, brecv, csend, crecv, dsend, drecv, esend, erecv, fsend, frecv, gsend, grecv, lsem = sems
    r, s, z, y, c = net.r, net.s, net.z, net.y, net.c
    base = z // group * group
    zz = lax.rem(z, group)
    inner = [lax.rem(zz + d, group) for d in range(1, group)]
    near_copy = lambda: remote(slab(1 - c), near, asend, arecv, net.sib, s)
    own_copy = lambda: pltpu.make_async_copy(slab(c), own, lsem)
    across = lambda d: remote(
        near.at[net.others[d]], side.at[d], bsend.at[d], brecv.at[d], r, net.others[d]
    )
    over = lambda: remote(near.at[s, 1 - y], mate, csend, crecv, net.yn, s)
    along = lambda d: remote(
        near.at[s, y, inner[d]], tall.at[d], dsend.at[d], drecv.at[d],
        (base + inner[d]) * 4 + net.line, s,
    )
    one, two, four = out
    mine = one(c, y, z)
    spread = lambda d: remote(
        mine, mine, esend.at[d], erecv.at[d], net.heights[d] * 4 + net.line, s
    )
    pair = lambda: remote(two(c, y), two(c, y), fsend, frecv, net.yn, s)
    last = lambda: remote(four(c), four(c), gsend, grecv, net.sib, s)
    n_side, n_inner, n_tall = len(net.others), len(inner), len(net.heights)

    def step0():
        near_copy().start()
        own_copy().start()

    def step1():
        near_copy().wait_recv()
        own_copy().wait()
        for t in range(net.shards):
            for half in range(2):
                add_rows(near.at[t, half], [own.at[t, half], near.at[t, half]])
        for d in range(n_side):
            across(d).start()

    def step2():
        for d in range(n_side):
            across(d).wait_recv()
        for half in range(2):
            add_rows(
                near.at[s, half], [near.at[s, half]] + [side.at[d, half] for d in range(n_side)]
            )
        over().start()

    def step3():
        over().wait_recv()
        add_rows(near.at[s, y], [near.at[s, y], mate])
        for d in range(n_inner):
            along(d).start()

    def step4():
        for d in range(n_inner):
            along(d).wait_recv()
        add_rows(mine, [near.at[s, y, zz]] + [tall.at[d] for d in range(n_inner)])
        for d in range(n_tall):
            spread(d).start()

    def step5():
        for d in range(n_tall):
            spread(d).wait_recv()
        pair().start()

    def step6():
        pair().wait_recv()
        last().start()

    def step7():
        last().wait_recv()

    def drain():
        near_copy().wait_send()
        for d in range(n_side):
            across(d).wait_send()
        over().wait_send()
        for d in range(n_inner):
            along(d).wait_send()
        for d in range(n_tall):
            spread(d).wait_send()
        pair().wait_send()
        last().wait_send()

    return [step0, step1, step2, step3, step4, step5, step6, step7], drain


def reduce_scratch(shards, levels, group, rows, cols):
    dma = pltpu.SemaphoreType.DMA
    vmem = pltpu.VMEM
    many = lambda n: dma((max(n, 1),))
    buffers = [
        vmem((shards, 2, group, rows, cols), BF16),
        vmem((shards, 2, group, rows, cols), BF16),
        vmem((max(shards - 1, 1), 2, group, rows, cols), BF16),
        vmem((group, rows, cols), BF16),
        vmem((max(group - 1, 1), rows, cols), BF16),
    ]
    sems = [
        dma(()), dma(()), many(shards - 1), many(shards - 1), dma(()), dma(()),
        many(group - 1), many(group - 1), many(levels - 1), many(levels - 1),
        dma(()), dma(()), dma(()), dma(()), dma(()),
    ]
    return buffers + sems


SCRATCH = 20


def small_steps(net, src, out, near, side, mate, tall, sems):
    asend, arecv, bsend, brecv, csend, crecv, dsend, drecv = sems
    r, s, z, y, c = net.r, net.s, net.z, net.y, net.c
    near_copy = lambda: remote(src, near.at[1], asend, arecv, net.sib, s)
    across = lambda d: remote(
        near.at[0, net.others[d]], side.at[s], bsend.at[d], brecv.at[d], r, net.others[d]
    )
    over = lambda: remote(mate.at[0], mate.at[1], csend, crecv, net.yn, s)
    along = lambda d: remote(
        tall.at[z], tall.at[z], dsend.at[d], drecv.at[d], net.heights[d] * 4 + net.line, s
    )

    def step0():
        near_copy().start()

    def step1():
        near_copy().wait_recv()
        near[0] = src[...] + near[1]
        side[s] = near[0, s]
        for d in range(len(net.others)):
            across(d).start()

    def step2():
        for d in range(len(net.others)):
            across(d).wait_recv()
        total = side[0]
        for t in range(1, net.shards):
            total = total + side[t]
        mate[0] = total
        over().start()

    def step3():
        over().wait_recv()
        tall[z] = mate[0] + mate[1]
        for d in range(len(net.heights)):
            along(d).start()

    def step4():
        for d in range(len(net.heights)):
            along(d).wait_recv()
        total = tall[0]
        for t in range(1, net.levels):
            total = total + tall[t]
        out[...] = total

    def drain():
        near_copy().wait_send()
        for d in range(len(net.others)):
            across(d).wait_send()
        over().wait_send()
        for d in range(len(net.heights)):
            along(d).wait_send()

    return [step0, step1, step2, step3, step4], drain


def small_scratch(shards, levels, rows):
    dma = pltpu.SemaphoreType.DMA
    vmem = pltpu.VMEM
    return [
        vmem((2, shards, 1, rows), F32), vmem((shards, 1, rows), F32),
        vmem((2, 1, rows), F32), vmem((levels, 1, rows), F32),
        dma(()), dma(()), dma((max(shards - 1, 1),)), dma((max(shards - 1, 1),)),
        dma(()), dma(()), dma((levels - 1,)), dma((levels - 1,)),
    ]


def places(ref, chunk, core_first, levels, rows, cols):
    if len(ref.shape) != 2:
        return (
            lambda c, y, z: ref.at[chunk, c, y, z], lambda c, y: ref.at[chunk, c, y],
            lambda c: ref.at[chunk, c],
        )
    if core_first:

        def view(c, at, size):
            lanes = pl.ds(pl.multiple_of((chunk * 2 + c) * cols, cols), cols)
            return ref.at[pl.ds(pl.multiple_of(at, rows), size), lanes]

        return (
            lambda c, y, z: view(c, (y * levels + z) * rows, rows),
            lambda c, y: view(c, y * levels * rows, levels * rows),
            lambda c: view(c, 0, 2 * levels * rows),
        )

    def span(at, count):
        first = (chunk * 4 * levels + at) * rows
        return ref.at[pl.ds(pl.multiple_of(first, rows), count * rows)]

    return (
        lambda c, y, z: span((c * 2 + y) * levels + z, 1),
        lambda c, y: span((c * 2 + y) * levels, levels),
        lambda c: span(c * 2 * levels, 2 * levels),
    )


def spread_out(jobs, offsets):
    ticks = {}
    for n, steps in enumerate(jobs):
        for t, step in enumerate(steps):
            ticks.setdefault(n + offsets[t], []).append(step)
    return [ticks.get(t, []) for t in range(max(ticks, default=-1) + 1)]


def term_jobs(net, specs, chunk_shapes, terms, outs, rest):
    jobs, drains = [], []
    for number, (which, k, core_first) in enumerate(specs):
        scratch = rest[number * SCRATCH : (number + 1) * SCRATCH]
        ref = terms[which]
        if core_first:
            slab = lambda core, ref=ref, k=k: ref.at[k, core]
        else:
            slab = lambda core, ref=ref, k=k: ref.at[:, k, core]
        spot = places(outs[which], k, core_first, net.levels, *chunk_shapes[which])
        steps, drain = reduce_steps(net, slab, spot, *scratch[:5], scratch[5:], net.levels)
        jobs.append(steps)
        drains.append(drain)
    return jobs, drains, rest[len(specs) * SCRATCH :]


def sums_kernel(ring, shards, specs, chunk_shapes, *refs):
    n = len(chunk_shapes)
    net = Links(ring, shards)
    hello(net.partners())
    jobs, drains, _ = term_jobs(net, specs, chunk_shapes, refs[:n], refs[n : 2 * n], refs[2 * n :])
    for steps in spread_out(jobs, OFFSETS):
        for step in steps:
            step()
    for drain in drains:
        drain()


def tail_kernel(ring, shards, specs, chunk_shapes, n0, *refs):
    (
        go_ref, lse_ref, w_ref, mid_ref, small_ref, q_in, k_in, kt_in, vt_in, o_in, xr_in,
    ) = refs[:11]
    n_terms = len(chunk_shapes)
    terms, refs = refs[11 : 11 + n_terms], refs[11 + n_terms :]
    out_ref, outs, (qkv_ref, total_small) = refs[0], refs[1 : 1 + n_terms], refs[1 + n_terms : 3 + n_terms]
    (
        q_ref, k_ref, kt_ref, vt_ref, o_ref,
        g_ref, x_ref, v_ref, delta_ref, acc_ref, dk_ref, dv_ref, pq_ref, stage_ref, got_ref, got2_ref,
        dw_ref, dx_ref, near_ref, far_ref, db_ref, dwl_ref, row_ref, all_ref,
        gsend, grecv, ksend, krecv, xsend, xrecv, lsem,
    ) = refs[3 + n_terms : 34 + n_terms]
    rest = refs[34 + n_terms :]
    net = Links(ring, shards)
    r, s = net.r, net.s
    levels, members = net.levels, ring // GROUPS
    sub = levels // GROUPS
    g, m = r // members, lax.rem(r, members)
    peers = [lax.rem(g + d, GROUPS) for d in range(1, GROUPS)]
    mates = [lax.rem(m + d, members) for d in range(1, members)]
    partners = net.partners()
    if levels != GROUPS:
        partners = partners + [(p * members + m, s, True) for p in peers]
        partners = partners + [(g * members + t, s, True) for t in mates]
    else:
        partners = partners + [(g * members + 3 - m, s, True)]
    hello(partners)

    def give(p):
        return remote(go_ref.at[p], g_ref.at[g], gsend.at[p], grecv.at[g], p * members + m, s)

    def take(p):
        return remote(go_ref.at[p], g_ref.at[p], gsend.at[p], grecv.at[p], p * members + m, s)

    for p in peers:
        give(p).start()
    loads = [
        pltpu.make_async_copy(src, dst, lsem.at[n])
        for n, (src, dst) in enumerate(
            ((vt_in, vt_ref), (k_in, k_ref), (q_in, q_ref), (kt_in, kt_ref), (o_in, o_ref),
             (xr_in, x_ref))
        )
    ]
    for load in loads:
        load.start()
    g_ref[g] = go_ref[g]

    jobs, drains, rest = term_jobs(net, specs, chunk_shapes, terms, outs, rest)
    qkv_jobs = []
    for k in range(2):
        steps, drain = reduce_steps(
            net, lambda core, k=k: dwl_ref.at[:, k, core], places(all_ref, k, False, levels, 0, 0),
            *rest[:5], rest[5:SCRATCH], sub
        )
        qkv_jobs.append(steps)
        drains.append(drain)
        rest = rest[SCRATCH:]
    vec_steps, drain = small_steps(net, small_ref, total_small, *rest[:4], rest[4:])
    drains.append(drain)
    ticks = spread_out(jobs, OFFSETS)

    def tick(t, lo, hi):
        if hi - lo == 1:
            for step in ticks[lo]:
                step()
        else:
            mid = (lo + hi) // 2
            pl.when(t < mid)(lambda: tick(t, lo, mid))
            pl.when(t >= mid)(lambda: tick(t, mid, hi))

    for load in loads[:1]:
        load.wait()

    def turn(b, carry):
        rows = pl.ds(pl.multiple_of(b * BLOCK, BLOCK), BLOCK)
        for h in range(PER):
            v_ref[h, rows, :] = (
                vt_ref[b, h * HEAD_DIM : (h + 1) * HEAD_DIM, :].astype(F32).T.astype(BF16)
            )
        dk_ref[b] = jnp.zeros((SLAB, BLOCK), F32)
        dv_ref[b] = jnp.zeros((SLAB, BLOCK), F32)
        return carry

    lax.fori_loop(0, ring, turn, 0)
    dw_ref[...] = jnp.zeros(dw_ref.shape, F32)
    db_ref[...] = jnp.zeros(db_ref.shape, F32)
    for load in loads[1:]:
        load.wait()

    pairs = members // 2
    c, mt = net.c, m // 2
    fellows = [lax.rem(mt + d, pairs) for d in range(1, pairs)]
    pieces = 4
    size = BLOCK // pieces

    def cross():
        return lambda j: remote(
            stage_ref.at[j], got_ref.at[j], ksend.at[j, 0], krecv.at[j, 0], net.sib, s
        )

    to_core = cross()

    def share(j, d):
        t = fellows[d]
        return remote(
            got_ref.at[j, t], got2_ref.at[j, d], ksend.at[j, d + 1], krecv.at[j, d + 1],
            g * members + t * 2 + c, s,
        )

    def hop(j, u, side, target):
        rows = pl.ds(u * size, size)
        return remote(
            dx_ref.at[j, rows], far_ref.at[j, side, rows], xsend.at[j, u], xrecv.at[j, side, u],
            target, s,
        )

    def pass_dx(j, u):
        down = lambda: hop(j, u, 0, r - members)
        up = lambda: hop(j, u, 1, r + members)
        return down, up

    def begin(i):
        pl.when(g != i)(lambda: take(i).wait_recv())
        for h in range(PER):
            head = pl.ds(h * HEAD_DIM, HEAD_DIM)
            delta_ref[h] = jnp.sum(
                g_ref[i, head, :].astype(F32) * o_ref[i, head, :], axis=0, keepdims=True
            )
        acc_ref[...] = jnp.zeros(acc_ref.shape, F32)

    def unit(i, kb):
        keys = pl.ds(pl.multiple_of(kb * BLOCK, BLOCK), BLOCK)
        for h in range(PER):
            head = pl.ds(h * HEAD_DIM, HEAD_DIM)
            score = mm(k_ref[h, keys, :], q_ref[i, h])
            probs = jnp.exp(score - lse_ref[i, h])
            grad = g_ref[i, head, :]
            moved = (probs * (mm(v_ref[h, keys, :], grad) - delta_ref[h])).astype(BF16)
            acc_ref[h] += mm(kt_ref[kb, head, :], moved)
            dk_ref[kb, head, :] += mm(q_ref[i, h, :HEAD_DIM, :], moved, NT)
            dv_ref[kb, head, :] += mm(grad, probs.astype(BF16), NT)

    def end(i):
        for h in range(PER):
            pq_ref[i, pl.ds(h * HEAD_DIM, HEAD_DIM), :] = (
                acc_ref[h] * HEAD_DIM ** (-0.5)
            ).astype(BF16)
        for t in range(pairs):
            b = i * members + t * 2 + 1 - c
            stage_ref[i, t, :SLAB, :] = dk_ref[b].astype(BF16)
            stage_ref[i, t, SLAB:, :] = dv_ref[b].astype(BF16)
        to_core(i).start()

    def merge(j):
        to_core(j).wait_recv()
        for d, t in enumerate(fellows):
            b = j * members + t * 2 + c
            for half, ref in enumerate((dk_ref, dv_ref)):
                rows = pl.ds(half * SLAB, SLAB)
                got_ref[j, t, rows, :] = (ref[b] + got_ref[j, t, rows, :].astype(F32)).astype(BF16)
            share(j, d).start()

    def finish(j):
        b = j * members + m
        dk = dk_ref[b] + got_ref[j, mt, :SLAB, :].astype(F32)
        dv = dv_ref[b] + got_ref[j, mt, SLAB:, :].astype(F32)
        for d in range(pairs - 1):
            share(j, d).wait_recv()
            dk = dk + got2_ref[j, d, :SLAB, :].astype(F32)
            dv = dv + got2_ref[j, d, SLAB:, :].astype(F32)
        proj = jnp.concatenate([pq_ref[j], dk.astype(BF16), dv.astype(BF16)], axis=0)
        db_ref[...] += jnp.sum(proj.astype(F32), axis=1, keepdims=True)
        dx = mm(proj, w_ref[...], TN)
        near_ref[j] = dx
        dx_ref[j] = dx.astype(BF16)
        start_dx(j, 0)
        dw_ref[...] += mm(x_ref[j], proj.T, TN)

    def start_dx(j, depth):
        from_below = jnp.logical_and(g < j, g == depth)
        from_above = jnp.logical_and(g > j, GROUPS - 1 - g == depth)
        for u in range(pieces):
            rows = pl.ds(u * size, size)
            down, up = pass_dx(j, u)

            @pl.when(from_below)
            def _():
                if depth:
                    hop(j, u, 1, r).wait_recv()
                    dx_ref[j, rows] = (near_ref[j, rows] + far_ref[j, 1, rows].astype(F32)).astype(BF16)
                up().start()

            @pl.when(from_above)
            def _():
                if depth:
                    hop(j, u, 0, r).wait_recv()
                    dx_ref[j, rows] = (near_ref[j, rows] + far_ref[j, 0, rows].astype(F32)).astype(BF16)
                down().start()

    def own_dx():
        for side, there in ((0, g < GROUPS - 1), (1, g > 0)):

            @pl.when(there)
            def _():
                for u in range(pieces):
                    hop(g, u, side, r).wait_recv()
                near_ref[g] += far_ref[g, side].astype(F32)

    sizes = [i * members + m + 1 for i in range(GROUPS)][::-1]
    ends = [sum(sizes[: n + 1]) for n in range(GROUPS)]
    units = ends[-1]
    finishes = [members * n + 2 for n in (4, 7, 9, 10)]

    def advance(it, carry):
        past = [(it >= e).astype(jnp.int32) for e in ends]
        i = GROUPS - 1 - past[0] - past[1] - past[2]
        first = jnp.where(i == 3, 0, jnp.where(i == 2, ends[0], jnp.where(i == 1, ends[1], ends[2])))
        kb = it - first

        t = it // PACE
        if ticks:
            pl.when(jnp.logical_and(lax.rem(it, PACE) == 0, t < len(ticks)))(
                lambda: tick(t, 0, len(ticks))
            )

        @pl.when(it < units)
        def _():
            pl.when(kb == 0)(lambda: begin(i))
            unit(i, kb)

            @pl.when(kb == i * members + m)
            def _():
                end(i)

        def at_times(shift, act):
            n_due = sum((it - shift >= at).astype(jnp.int32) for at in finishes)
            n_done = sum((it - shift > at).astype(jnp.int32) for at in finishes)
            pl.when(n_due > n_done)(lambda: act(GROUPS - n_due))

        at_times(0, merge)
        at_times(1, finish)
        for depth in range(1, GROUPS - 1):
            at_times(1 + depth, lambda j, depth=depth: start_dx(j, depth))
        return carry

    count = max(finishes[-1] + 2, PACE * len(ticks))
    lax.fori_loop(0, count, advance, 0)

    width = w_ref.shape[1]
    dwl_ref[...] = dw_ref[...].astype(BF16).reshape(dwl_ref.shape)
    row = jnp.broadcast_to(db_ref[...], (3 * SLAB, 8)).T[:1]
    row_ref[...] = jnp.zeros(row_ref.shape, F32)
    for k in range(GROUPS):

        @pl.when(g == k)
        def _():
            row_ref[:, k * SLAB : (k + 1) * SLAB] = row[:, :SLAB]
            row_ref[:, width + k * SLAB : width + (k + 1) * SLAB] = row[:, 2 * SLAB :]

    for t in range(shards):
        small_ref[t, :, :n0] = row_ref[:, t * n0 : (t + 1) * n0]
    for job in qkv_jobs:
        job[0]()
    vec_steps[0]()
    for depth in range(1, GROUPS - 1):
        if count <= finishes[-1] + 1 + depth:
            start_dx(0, depth)
    for job in qkv_jobs:
        job[1]()
    vec_steps[1]()
    own_dx()
    out_ref[...] = (near_ref[g] + mid_ref[...]).astype(BF16)
    for t in range(2, 8):
        for job in qkv_jobs:
            job[t]()
        if t < len(vec_steps):
            vec_steps[t]()
    if len(qkv_ref.shape) == 2:
        rows = all_ref.shape[-2]
        for part in range(8):
            for z in range(levels):
                at = (part * sub + z % sub) * rows
                piece = all_ref[part // 4, part // 2 % 2, part % 2, z]
                for t in range(3):
                    lane = t * width + z // sub * SLAB
                    qkv_ref[at : at + rows, lane : lane + SLAB] = piece[
                        :, t * SLAB : (t + 1) * SLAB
                    ]
    else:
        qkv_ref[...] = all_ref[...]
    for p in peers:
        give(p).wait_send()
    for j in range(GROUPS):
        to_core(j).wait_send()
        for d in range(pairs - 1):
            share(j, d).wait_send()
        for u in range(pieces):
            pl.when(g != j)(lambda: hop(j, u, 0, r).wait_send())
    for drain in drains:
        drain()


PACE = 2
OFFSETS = (0, 1, 3, 4, 5, 6, 7, 8)


def tail_all(gat, lse, w_group, mid, small, saved, terms, n0, ring, shards, ident):
    members, levels = ring // GROUPS, ring // 4
    sub = levels // GROUPS
    width = mid.shape[1]
    part = width // shards
    shape = jax.ShapeDtypeStruct
    dma = pltpu.SemaphoreType.DMA
    vmem = pltpu.VMEM
    specs, scratch, out_shape, chunk_shapes = [], [], [], []
    for i, term in enumerate(terms):
        core_first = i > 0
        chunks = term.shape[0] if core_first else term.shape[1]
        rows, cols = term.shape[-2:]
        chunk_shapes.append((rows, cols))
        if rows % 16:
            out_shape.append(shape((chunks, 2, 2, levels, rows, cols), BF16))
        elif core_first:
            out_shape.append(shape((2 * levels * rows, chunks * 2 * cols), BF16))
        else:
            out_shape.append(shape((chunks * 4 * levels * rows, cols), BF16))
        for k in range(chunks):
            specs.append((i, k, core_first))
            scratch += reduce_scratch(shards, levels, levels, rows, cols)
    term_scratch, term_shapes = scratch, out_shape
    apart = ring * BLOCK > 4096
    if apart:
        sums = pl.pallas_call(
            lambda *refs: sums_kernel(ring, shards, specs, chunk_shapes, *refs),
            out_shape=tuple(term_shapes),
            in_specs=[ANY_SPEC] * 3,
            out_specs=(VMEM_SPEC,) * 3,
            scratch_shapes=term_scratch,
            compiler_params=pltpu.CompilerParams(
                collective_id=ident + 1, has_side_effects=True, vmem_limit_bytes=VMEM_LIMIT
            ),
        )(*terms)
    specs, chunk_shapes = ([], []) if apart else (specs, chunk_shapes)
    scratch = [] if apart else list(term_scratch)
    out_shape = [] if apart else list(term_shapes)
    terms = () if apart else terms
    rows = part // 8 // sub
    buffer = (2, 2, 2, levels, rows, 3 * SLAB)
    scratch += reduce_scratch(shards, levels, sub, rows, 3 * SLAB)
    scratch += reduce_scratch(shards, levels, sub, rows, 3 * SLAB)
    scratch += small_scratch(shards, levels, small.shape[2])
    out_shape.append(shape(buffer if rows % 16 else (part, 3 * width), BF16))
    slab = (GROUPS, SLAB, BLOCK)
    tall = (ring, SLAB, BLOCK)
    result = pl.pallas_call(
        lambda *refs: tail_kernel(ring, shards, specs, chunk_shapes, n0, *refs),
        out_shape=(shape((BLOCK, width), BF16), *out_shape, shape((1, small.shape[2]), F32)),
        in_specs=[VMEM_SPEC] * 5 + [ANY_SPEC] * (6 + len(terms)),
        out_specs=(VMEM_SPEC,) * (3 + len(terms)),
        scratch_shapes=[
            vmem((GROUPS, PER, 2 * HEAD_DIM, BLOCK), BF16),
            vmem((PER, ring * BLOCK, 2 * HEAD_DIM), BF16),
            vmem(tall, BF16), vmem(tall, BF16), vmem(slab, F32),
            vmem(slab, BF16),
            vmem((GROUPS, BLOCK, width), BF16),
            vmem((PER, ring * BLOCK, HEAD_DIM), BF16),
            vmem((PER, 1, BLOCK), F32),
            vmem((PER, HEAD_DIM, BLOCK), F32),
            vmem(tall, F32), vmem(tall, F32), vmem(slab, BF16),
            vmem((GROUPS, members // 2, 2 * SLAB, BLOCK), BF16),
            vmem((GROUPS, members // 2, 2 * SLAB, BLOCK), BF16),
            vmem((GROUPS, members // 2 - 1, 2 * SLAB, BLOCK), BF16),
            vmem((width, 3 * SLAB), F32),
            vmem((GROUPS, BLOCK, width), BF16),
            vmem((GROUPS, BLOCK, width), F32),
            vmem((GROUPS, 2, BLOCK, width), BF16),
            vmem((3 * SLAB, 1), F32),
            vmem((shards, 2, 2, 2, sub, rows, 3 * SLAB), BF16),
            vmem((1, 2 * width), F32),
            vmem(buffer, BF16),
            dma((GROUPS,)), dma((GROUPS,)),
            dma((GROUPS, members // 2)), dma((GROUPS, members // 2)),
            dma((GROUPS, 4)), dma((GROUPS, 2, 4)), dma((6,)),
            *scratch,
        ],
        compiler_params=pltpu.CompilerParams(
            collective_id=ident, has_side_effects=True, vmem_limit_bytes=VMEM_LIMIT
        ),
    )(gat, lse, w_group, mid, small, *saved, *terms)
    return (result[0], *sums, *result[1:]) if apart else result


def on_device(
    tokens, doc_ids, qkv_weight, qv_bias, out_weight, out_bias, mid_gain, mid_shift,
    up_weight, up_bias, down_weight, down_bias, end_gain, end_shift, out_grad,
):
    width, hidden = tokens.shape[2], up_weight.shape[1]
    ring, shards = lax.axis_size("rep"), lax.axis_size("shard")
    levels = ring // 4
    sub = levels // GROUPS
    x = tokens[0]
    small = (qv_bias, out_bias, mid_gain, mid_shift, up_bias, down_bias, end_gain, end_shift)
    sizes = [v.shape[0] for v in small]
    own = (out_weight, up_weight, down_weight)
    att, flat, w_group, lse, o, q, k, kt, vt, x_rows, *full = forward_all(
        x, qkv_weight, doc_ids, [v.reshape(1, -1) for v in small], own, ((2, 0, 1, True), (0, 0, 1, False), (1, 0, 2, False)), ring, shards, 0
    )
    down_chunks = 6 if hidden % (6 * shards * ring * 16) == 0 else 1
    layer_out, gat, mid, flat, down, up, out = mlp_all(
        att, x, out_grad[0], flat, own, full, sizes, shards, levels, down_chunks, 6
    )
    input_grad, down, up, out, qkv, flat = tail_all(
        gat, lse, w_group, mid, flat, (q, k, kt, vt, o, x_rows), (down, up, out), sizes[0],
        ring, shards, 1,
    )
    total_down = down.reshape(-1, width).astype(F32)
    if up.ndim > 2:
        up = up.reshape(12, width // shards, -1).transpose(1, 0, 2).reshape(-1, hidden)
        out = out.reshape(2, width // shards, -1).transpose(1, 0, 2).reshape(-1, width)
    if qkv.ndim > 2:
        qkv = qkv.reshape(8, GROUPS, sub, -1, 3, SLAB).transpose(0, 2, 3, 4, 1, 5)
        qkv = qkv.reshape(-1, 3 * width)
    total_up, total_out, total_qkv = up.astype(F32), out.astype(F32), qkv.astype(F32)
    flat = flat.reshape(-1)
    totals, at = [], 0
    for size in sizes:
        totals.append(flat[at : at + size])
        at += size
    return (
        layer_out[None], input_grad[None], total_qkv, totals[0], total_out, totals[1], totals[2],
        totals[3], total_up, totals[4], total_down, totals[5], totals[6], totals[7],
    )


def solution(mesh):
    rows = P("shard", None)
    flat = P("shard")
    acts = P("shard", "rep", None)
    in_specs = (
        acts, rows, rows, flat, rows, flat, flat, flat, rows, flat, rows, flat, flat, flat, acts
    )
    out_specs = (acts, acts, rows, flat, rows, flat, flat, flat, rows, flat, rows, flat, flat, flat)
    return jax.shard_map(
        on_device, mesh=mesh, in_specs=in_specs, out_specs=out_specs, check_vma=False
    )
```

```python
import jax
import jax.numpy as jnp
from jax import lax
from jax.experimental import pallas as pl
from jax.experimental.pallas import tpu as pltpu
from jax.sharding import PartitionSpec as P

HEADS = 12
HEAD_DIM = 64
BLOCK = 256
GROUPS = 4
PER = HEADS // GROUPS
SLAB = PER * HEAD_DIM
EPSILON = 1e-05
FAR = 2.0**100
F32 = jnp.float32
BF16 = jnp.bfloat16
LANES = 128
NN = (((1,), (0,)), ((), ()))
NT = (((1,), (1,)), ((), ()))
TN = (((0,), (0,)), ((), ()))
VMEM_SPEC = pl.BlockSpec(memory_space=pltpu.VMEM)
VMEM_LIMIT = 67043328


def mm(left, right, dims=NN):
    return lax.dot_general(left, right, dims, preferred_element_type=F32)


ANY_SPEC = pl.BlockSpec(memory_space=pl.ANY)


def remote(src, dst, send, recv, rep, shard):
    return pltpu.make_async_remote_copy(
        src_ref=src, dst_ref=dst, send_sem=send, recv_sem=recv,
        device_id=(rep, shard), device_id_type=pl.DeviceIdType.MESH,
    )


def hello(partners):
    barrier = pltpu.get_barrier_semaphore()
    total = 0
    for rep, shard, there in partners:
        if there is True:
            pl.semaphore_signal(
                barrier, inc=1, device_id=(rep, shard), device_id_type=pl.DeviceIdType.MESH
            )
            total = total + 1
        else:

            @pl.when(there)
            def _():
                pl.semaphore_signal(
                    barrier, inc=1, device_id=(rep, shard), device_id_type=pl.DeviceIdType.MESH
                )

            total = total + there.astype(jnp.int32)
    pl.semaphore_wait(barrier, total)


class Links:
    def __init__(self, ring, shards):
        self.ring, self.shards = ring, shards
        self.r, self.s = lax.axis_index("rep"), lax.axis_index("shard")
        self.levels = ring // 4
        self.z, self.c = self.r // 4, lax.rem(self.r, 2)
        self.y = lax.rem(self.r // 2, 2)
        self.sib = self.r + 1 - 2 * self.c
        self.yn = self.r + 2 - 4 * self.y
        self.others = [lax.rem(self.s + d, shards) for d in range(1, shards)]
        self.heights = [lax.rem(self.z + d, self.levels) for d in range(1, self.levels)]
        self.line = lax.rem(self.r, 4)

    def partners(self):
        return (
            [(self.sib, self.s, True), (self.yn, self.s, True)]
            + [(self.r, t, True) for t in self.others]
            + [(h * 4 + self.line, self.s, True) for h in self.heights]
        )


def forward_kernel(ring, shards, parts, sizes, *refs):
    n_vec = len(sizes)
    x_ref, w_ref, docs_ref = refs[:3]
    vec_refs, own = refs[3 : 3 + n_vec], refs[3 + n_vec : 6 + n_vec]
    outs, rest = refs[6 + n_vec : 19 + n_vec], refs[19 + n_vec :]
    att_ref, flat_ref, wg_ref, lse_ref, o_out, q_out, k_out, kt_out, vt_out, xr_out = outs[:10]
    full = outs[10:]
    (
        xa_ref, wl_ref, low_ref, bias_ref, o_ref, q_ref, k_ref, kt_ref, vt_ref, top_ref, sum_ref,
        send, recv, wsend, wrecv, fsend, frecv, vsend, vrecv, asend, arecv, osem,
    ) = rest
    net = Links(ring, shards)
    r, s, z, y, c = net.r, net.s, net.z, net.y, net.c
    levels, members = net.levels, ring // GROUPS
    g, m = r // members, lax.rem(r, members)
    sib, yn, line, others = net.sib, net.yn, net.line, net.others
    above, below = z < levels - 1, z > 0
    hello(net.partners())

    halves = 2

    def move(b, kind, u, src=None):
        target = (r + 4, r - 4, yn, sib)[kind]
        rows = pl.ds(u * (BLOCK // halves), BLOCK // halves)
        src = xa_ref.at[b, rows] if src is None else src.at[rows]
        return remote(src, xa_ref.at[b, rows], send.at[kind, b, u], recv.at[b, u], target, s)

    for u in range(halves):
        pl.when(above)(lambda: move(r, 0, u, x_ref).start())
        pl.when(below)(lambda: move(r, 1, u, x_ref).start())
        move(r, 2, u, x_ref).start()
        move(r, 3, u, x_ref).start()
    xa_ref[r] = x_ref[...]

    width = x_ref.shape[1]
    for k in range(GROUPS):

        @pl.when(g == k)
        def _():
            wl_ref[s] = jnp.concatenate(
                [w_ref[:, t * width + k * SLAB : t * width + (k + 1) * SLAB] for t in range(3)], 1
            )

    flat_ref[s] = jnp.concatenate([v[...].astype(F32).reshape(1, -1) for v in vec_refs], axis=1)
    lists = [
        remote(flat_ref.at[s], flat_ref.at[s], vsend.at[d], vrecv.at[d], r, t)
        for d, t in enumerate(others)
    ]
    pieces = [(lambda rows: wl_ref.at[s, rows], wl_ref, w_ref.shape[0] // 2, 0, False)]
    for w, count, quad in parts:
        size = own[w].shape[0] // (4 if quad else 2) // count
        for j in range(count):
            pieces.append((lambda rows, w=w: own[w].at[rows], full[w], size, (count, j), quad))

    def span(piece, yy, cc):
        size, where, quad = piece[2:]
        count, j = where or (1, 0)
        part = (yy * 2 + cc) if quad else cc
        return pl.ds(pl.multiple_of((part * count + j) * size, size), size)

    def across(at, d):
        rows = span(pieces[at], y, c)
        return remote(
            pieces[at][0](rows), pieces[at][1].at[s, rows], wsend.at[at, d], wrecv.at[at, d],
            r, others[d],
        )

    def shifted(at, d, kind, yy, cc, target):
        rows = span(pieces[at], yy, cc)
        spot = pieces[at][1].at[others[d], rows]
        return remote(spot, spot, fsend.at[at, d, kind], frecv.at[at, d, kind], target, s)

    def relay(at):
        for d in range(shards - 1):
            across(at, d).wait_recv()
            shifted(at, d, 0, y, c, sib).start()
            if pieces[at][4]:
                shifted(at, d, 1, y, c, yn).start()

    def relay_far(at):
        for d in range(shards - 1):
            shifted(at, d, 1, 1 - y, c, yn).wait_recv()
            shifted(at, d, 2, 1 - y, c, sib).start()

    def relayed(at):
        for d in range(shards - 1):
            shifted(at, d, 0, y, 1 - c, sib).wait_recv()
            if pieces[at][4]:
                shifted(at, d, 2, 1 - y, 1 - c, sib).wait_recv()

    for copy in lists:
        copy.start()
    for at in range(len(pieces)):
        for d in range(shards - 1):
            across(at, d).start()
    relay(0)
    for copy in lists:
        copy.wait_recv()
    n0 = sizes[0]
    qv = jnp.concatenate([flat_ref[t, :, :n0] for t in range(shards)], axis=1)
    for k in range(GROUPS):

        @pl.when(g == k)
        def _():
            row = jnp.concatenate(
                [qv[:, k * SLAB : (k + 1) * SLAB], qv[:, width + k * SLAB : width + (k + 1) * SLAB]],
                axis=1,
            )
            bias_ref[...] = jnp.broadcast_to(row, (8, 2 * SLAB)).T[:, :1]

    relayed(0)
    part = width // shards
    for t in range(shards):
        wg_ref[:, t * part : (t + 1) * part] = wl_ref[t].astype(F32).T.astype(BF16)

    def level(q):
        lo, hi = z, levels - 1 - z
        turn = jnp.minimum(lo, hi)
        swing = jnp.where(lax.rem(q, 2) == 1, z - (q + 1) // 2, z + q // 2)
        rest = jnp.where(lo > hi, z - (q - turn), z + (q - turn))
        return jnp.where(q <= 2 * turn, swing, rest)

    def event(n):
        k, t = (n - 2) // 4, lax.rem(n + 2, 4)
        q = jnp.where(n < 2, 0, jnp.where(lax.rem(t, 2) == 0, k + 1, k))
        j = jnp.where(n < 2, 2 * n, t)
        q = jnp.where(n >= ring - 2, levels - 1, q)
        j = jnp.where(n >= ring - 2, 2 * (n - ring + 2) + 1, j)
        lv = level(q)
        return lv * 4 + lax.rem(y + lax.rem(j, 2), 2) * 2 + lax.rem(c + j // 2, 2), lv, j

    sub = levels // GROUPS

    def arrive(n):
        b, lv, j = event(n)

        @pl.when(n > 0)
        def _():
            for u in range(halves):
                move(b, 3, u).wait_recv()

                @pl.when(j == 0)
                def _():
                    pl.when(jnp.logical_and(lv < z, above))(lambda: move(b, 0, u).start())
                    pl.when(jnp.logical_and(lv > z, below))(lambda: move(b, 1, u).start())
                    move(b, 2, u).start()

                pl.when(j < 2)(lambda: move(b, 3, u).start())

        both = mm(wg_ref[SLAB:, :], xa_ref[b], NT)
        kt = both[:SLAB].astype(BF16)
        kt_ref[b] = kt
        vt_ref[b] = (both[SLAB:] + bias_ref[SLAB:, :]).astype(BF16)
        at = pl.multiple_of(b * BLOCK, BLOCK)
        docs = docs_ref[:, pl.ds(at, BLOCK)].astype(F32)
        blank = jnp.zeros((HEAD_DIM - 2, BLOCK), F32)
        extra = jnp.concatenate([docs * FAR - FAR, docs * (-FAR), blank], axis=0)
        for h in range(PER):
            part = kt[h * HEAD_DIM : (h + 1) * HEAD_DIM].astype(F32)
            k_ref[h, pl.ds(at, BLOCK), :] = jnp.concatenate([part, extra], axis=0).T.astype(BF16)

        @pl.when(jnp.logical_and(j == 0, lax.rem(lv, sub) == lax.rem(z, sub)))
        def _():
            i = lv // sub
            qt = (mm(wg_ref[:SLAB, :], xa_ref[b], NT) + bias_ref[:SLAB, :]).astype(BF16)
            qt = qt.astype(F32) * HEAD_DIM ** (-0.5)
            extra = jnp.concatenate([docs, 1.0 - docs, blank], axis=0)
            for h in range(PER):
                part = qt[h * HEAD_DIM : (h + 1) * HEAD_DIM]
                q_ref[i, h] = jnp.concatenate([part, extra], axis=0).astype(BF16)

    def unit(i, kb):
        keys = pl.ds(pl.multiple_of(kb * BLOCK, BLOCK), BLOCK)
        for h in range(PER):
            head = pl.ds(h * HEAD_DIM, HEAD_DIM)
            score = mm(k_ref[h, keys, :], q_ref[i, h])
            old = top_ref[i, h]
            new = jnp.maximum(old, jnp.max(score, axis=0, keepdims=True))
            probs = jnp.exp(score - new)
            shrink = jnp.exp(old - new)
            top_ref[i, h] = new
            sum_ref[i, h] = sum_ref[i, h] * shrink + jnp.sum(probs, axis=0, keepdims=True)
            o_ref[i, head, :] = o_ref[i, head, :] * shrink + mm(
                vt_ref[kb, head, :], probs.astype(BF16)
            )

    def attend(n):
        b, lv, j = event(n)
        first = jnp.logical_and(j == 0, lax.rem(lv, sub) == lax.rem(z, sub))
        known = jnp.where(n < 2, 1, jnp.minimum((n - 2) // 4 + 2, levels))

        def pair(u, carry):
            near = u < known
            seen = level(jnp.minimum(u, known - 1))
            old = event(jnp.maximum(u - known, 0))[0]
            i = jnp.where(near, seen, lv) // sub
            kb = jnp.where(near, b, old)
            query = i * members + m
            mine = jnp.where(near, lax.rem(seen, sub) == lax.rem(z, sub), old < b)
            pl.when(jnp.logical_and(mine, kb <= query))(lambda: unit(i, kb))
            return carry

        lax.fori_loop(0, known + jnp.where(first, n, 0), pair, 0)

    top_ref[...] = jnp.full(top_ref.shape, -jnp.inf, F32)
    sum_ref[...] = jnp.zeros(sum_ref.shape, F32)
    o_ref[...] = jnp.zeros(o_ref.shape, F32)
    lag = 4
    turn_on = ring - 5

    def advance(n, carry):
        pl.when(n < ring)(lambda: arrive(n))

        @pl.when(n == turn_on)
        def _():
            for at in range(len(pieces)):
                if pieces[at][4]:
                    relay(at)

        pl.when(n >= lag)(lambda: attend(n - lag))
        return carry

    lax.fori_loop(0, ring + lag, advance, 0)
    saves = [
        pltpu.make_async_copy(src, dst, osem.at[n])
        for n, (src, dst) in enumerate(
            ((k_ref, k_out), (kt_ref, kt_out), (vt_ref, vt_out), (q_ref, q_out), (o_ref, o_out))
        )
    ]
    saves += [
        pltpu.make_async_copy(xa_ref.at[i * members + m], xr_out.at[i], osem.at[5 + i])
        for i in range(GROUPS)
    ]
    for save in saves[:3] + saves[5:]:
        save.start()

    def give(i):
        return remote(low_ref.at[i], att_ref.at[g], asend.at[i], arecv.at[g], i * members + m, s)

    for i in range(GROUPS):
        for h in range(PER):
            head = pl.ds(h * HEAD_DIM, HEAD_DIM)
            out = o_ref[i, head, :] / sum_ref[i, h]
            o_ref[i, head, :] = out
            low_ref[i, head, :] = out.astype(BF16)
            lse_ref[i, h] = top_ref[i, h] + jnp.log(sum_ref[i, h])

        @pl.when(g == i)
        def _():
            att_ref[g] = low_ref[i]

        pl.when(g != i)(lambda: give(i).start())
    for save in saves[3:5]:
        save.start()
    for at in range(1, len(pieces)):
        if pieces[at][4]:
            relay_far(at)
        else:
            relay(at)
    for d in range(1, GROUPS):
        p = lax.rem(g + d, GROUPS)
        remote(low_ref.at[0], att_ref.at[p], asend.at[0], arecv.at[p], r, s).wait_recv()
    for at in range(1, len(pieces)):
        relayed(at)
    for i in range(GROUPS):
        pl.when(g != i)(lambda: give(i).wait_send())

    def sent(e, carry):
        b, lv, j = event(e)

        for u in range(halves):

            @pl.when(j == 0)
            def _():
                pl.when(jnp.logical_and(lv <= z, above))(lambda: move(b, 0, u).wait_send())
                pl.when(jnp.logical_and(lv >= z, below))(lambda: move(b, 1, u).wait_send())
                move(b, 2, u).wait_send()

            pl.when(j < 2)(lambda: move(b, 3, u).wait_send())
        return carry

    lax.fori_loop(0, ring, sent, 0)
    for copy in lists:
        copy.wait_send()
    for at in range(len(pieces)):
        for d in range(shards - 1):
            across(at, d).wait_send()
            shifted(at, d, 0, y, c, sib).wait_send()
            if pieces[at][4]:
                shifted(at, d, 1, y, c, yn).wait_send()
                shifted(at, d, 2, 1 - y, c, sib).wait_send()
    for save in saves:
        save.wait()


def forward_all(x, qkv_weight, docs, vectors, weights, parts, ring, shards, ident):
    shape = jax.ShapeDtypeStruct
    dma = pltpu.SemaphoreType.DMA
    vmem = pltpu.VMEM
    n = 1 + sum(part[1] for part in parts)
    width = x.shape[1]
    sizes = [v.shape[0] for v in vectors]
    per = max(shards - 1, 1)
    o = (GROUPS, SLAB, BLOCK)
    q = (GROUPS, PER, 2 * HEAD_DIM, BLOCK)
    k = (PER, ring * BLOCK, 2 * HEAD_DIM)
    t = (ring, SLAB, BLOCK)
    return pl.pallas_call(
        lambda *refs: forward_kernel(ring, shards, parts, sizes, *refs),
        out_shape=(
            shape(o, BF16), shape((shards, 1, sum(sizes)), F32), shape((3 * SLAB, width), BF16),
            shape((GROUPS, PER, 1, BLOCK), F32), shape(o, F32), shape(q, BF16), shape(k, BF16),
            shape(t, BF16), shape(t, BF16), shape((GROUPS,) + x.shape, BF16),
        )
        + tuple(shape((shards,) + w.shape, w.dtype) for w in weights),
        in_specs=[VMEM_SPEC] * (3 + len(vectors)) + [ANY_SPEC] * 3,
        out_specs=(VMEM_SPEC,) * 4 + (ANY_SPEC,) * 9,
        scratch_shapes=[
            vmem((ring,) + x.shape, BF16), vmem((shards, width // shards, 3 * SLAB), BF16),
            vmem(o, BF16), vmem((2 * SLAB, 1), F32), vmem(o, F32), vmem(q, BF16), vmem(k, BF16),
            vmem(t, BF16), vmem(t, BF16),
            vmem((GROUPS, PER, 1, BLOCK), F32), vmem((GROUPS, PER, 1, BLOCK), F32),
            dma((4, ring, 2)), dma((ring, 2)), dma((n, per)), dma((n, per)), dma((n, per, 3)),
            dma((n, per, 3)), dma((per,)), dma((per,)),
            dma((GROUPS,)), dma((GROUPS,)), dma((5 + GROUPS,)),
        ],
        compiler_params=pltpu.CompilerParams(
            collective_id=ident, has_side_effects=True, vmem_limit_bytes=VMEM_LIMIT
        ),
    )(x, qkv_weight, docs, *vectors, *weights)


def layer_norm(hidden, gain, shift):
    centre = hidden - jnp.mean(hidden, axis=-1, keepdims=True)
    inverse = lax.rsqrt(jnp.mean(centre * centre, axis=-1, keepdims=True) + EPSILON)
    normed = centre * inverse
    return (normed * gain + shift, normed, inverse)


def norm_back(grad_output, normed, inverse, gain):
    grad_normed = grad_output * gain
    centred = grad_normed - jnp.mean(grad_normed, axis=-1, keepdims=True)
    return inverse * (centred - normed * jnp.mean(grad_normed * normed, axis=-1, keepdims=True))


def mlp_kernel(
    shards, sizes, att_ref, x_ref, og_ref, flat_ref, *refs,
):
    own, full = refs[:3], refs[3:6]
    out_ref, gat_ref, mid_ref, small_ref, down_out, up_out, outw_out = refs[6:13]
    wo_ref, wu_ref, wd_ref, act_ref, slope_ref, gd_ref, gu_ref, go_ref, lsem, ssem = refs[13:]
    s = lax.axis_index("shard")
    width = x_ref.shape[1]
    hidden = wu_ref.shape[1]
    loads = []
    for w, ref in enumerate((wo_ref, wu_ref, wd_ref)):
        size = own[w].shape[0]
        group = []
        for d in range(shards):
            t = lax.rem(s + d, shards)
            rows = pl.ds(pl.multiple_of(t * size, size), size)
            src = own[w] if d == 0 else full[w].at[t]
            group.append(pltpu.make_async_copy(src, ref.at[rows], lsem.at[w * shards + d]))
        loads.append(group)
        for load in group:
            load.start()

    def ready(w):
        for load in loads[w]:
            load.wait()

    starts = [sum(sizes[:n]) for n in range(len(sizes))]

    def vector(n):
        return jnp.concatenate(
            [flat_ref[t, :, starts[n] : starts[n] + sizes[n]] for t in range(shards)], axis=1
        )

    def put(n, row):
        for t in range(shards):
            small_ref[t, :, starts[n] : starts[n] + sizes[n]] = row[
                :, t * sizes[n] : (t + 1) * sizes[n]
            ]

    small_ref[...] = jnp.zeros(small_ref.shape, F32)
    att = att_ref[...].reshape(width, BLOCK)
    ready(0)
    branch = mm(att, wo_ref[...], TN) + vector(1)
    gain_mid = vector(2)
    mid_out, mid_norm, mid_inv = layer_norm(x_ref[...].astype(F32) + branch, gain_mid, vector(3))
    mid_low = mid_out.astype(BF16)
    up_bias = vector(4)
    cols = 512
    ready(1)
    for at in range(0, hidden, cols):
        block = slice(at, at + cols)
        pre = mm(mid_low, wu_ref[:, block]) + up_bias[:, block]
        phi = 0.5 * (1.0 + lax.erf(pre * 0.7071067811865476))
        act_ref[:, block] = (pre * phi).astype(BF16)
        slope_ref[:, block] = phi + pre * jnp.exp(-0.5 * pre * pre) * 0.3989422804014327
    ready(2)
    ffn = mm(act_ref[...], wd_ref[...]) + vector(5)
    gain_end = vector(6)
    end_out, end_norm, end_inv = layer_norm(mid_out + ffn, gain_end, vector(7))
    out_ref[...] = end_out.astype(BF16)
    top = og_ref[...].astype(F32)

    def column(value):
        return jnp.sum(value, axis=0, keepdims=True)

    put(6, column(top * end_norm))
    put(7, column(top))
    grad_end_in = norm_back(top, end_norm, end_inv, gain_end)
    grad_ffn = grad_end_in.astype(BF16)
    put(5, column(grad_ffn.astype(F32)))
    saves = []

    def save(src, dst):
        copy = pltpu.make_async_copy(src, dst, ssem.at[len(saves)])
        copy.start()
        saves.append(copy)

    chunks = gd_ref.shape[1]
    rows = hidden // shards // chunks
    for t in range(shards):
        for k in range(chunks):
            at = t * (hidden // shards) + k * rows
            value = mm(act_ref[:, at : at + rows], grad_ffn, TN)
            gd_ref[t, k] = value.astype(BF16).reshape(gd_ref.shape[2:])
        save(gd_ref.at[t], down_out.at[t])
    grad_mid_out = grad_end_in
    ups = []
    wide = hidden // gu_ref.shape[0]
    for k in range(gu_ref.shape[0]):
        block = slice(k * wide, (k + 1) * wide)
        grad_act = mm(grad_ffn, wd_ref[block, :], NT)
        grad_pre = (grad_act * slope_ref[:, block]).astype(BF16)
        ups.append(column(grad_pre.astype(F32)))
        value = mm(mid_low, grad_pre, TN).astype(BF16)
        for half in range(2):
            gu_ref[k, half] = value[:, half * (wide // 2) : (half + 1) * (wide // 2)].reshape(
                gu_ref.shape[2:]
            )
        save(gu_ref.at[k], up_out.at[k])
        grad_mid_out = grad_mid_out + mm(grad_pre, wu_ref[:, block], NT)
    put(4, jnp.concatenate(ups, axis=1))
    put(2, column(grad_mid_out * mid_norm))
    put(3, column(grad_mid_out))
    grad_mid_in = norm_back(grad_mid_out, mid_norm, mid_inv, gain_mid)
    mid_ref[...] = grad_mid_in
    grad_branch = grad_mid_in.astype(BF16)
    put(1, column(grad_branch.astype(F32)))
    gat_ref[...] = mm(wo_ref[...], grad_branch, NT).astype(BF16).reshape(gat_ref.shape)
    value = mm(att, grad_branch).astype(BF16)
    for half in range(2):
        go_ref[0, half] = value[:, half * (width // 2) : (half + 1) * (width // 2)].reshape(
            go_ref.shape[2:]
        )
    save(go_ref, outw_out)
    for copy in saves:
        copy.wait()


def mlp_all(att, x, out_grad, flat, own, full, sizes, shards, levels, down_chunks, up_chunks):
    shape = jax.ShapeDtypeStruct
    dma = pltpu.SemaphoreType.DMA
    vmem = pltpu.VMEM
    width, hidden = own[0].shape[1], own[1].shape[1]
    gd = (shards, down_chunks, 2, 2, levels, hidden // shards // down_chunks // 4 // levels, width)
    gu = (up_chunks, 2, shards, 2, levels, width // shards // 2 // levels, hidden // up_chunks // 2)
    go = (1, 2, shards, 2, levels, width // shards // 2 // levels, width // 2)
    return pl.pallas_call(
        lambda *refs: mlp_kernel(shards, sizes, *refs),
        out_shape=(
            shape((BLOCK, width), BF16), shape((GROUPS, SLAB, BLOCK), BF16),
            shape((BLOCK, width), F32), shape(flat.shape, F32),
            shape(gd, BF16), shape(gu, BF16), shape(go, BF16),
        ),
        in_specs=[VMEM_SPEC] * 4 + [ANY_SPEC] * 6,
        out_specs=(VMEM_SPEC,) * 4 + (ANY_SPEC,) * 3,
        scratch_shapes=[
            vmem((width, width), BF16), vmem((width, hidden), BF16), vmem((hidden, width), BF16),
            vmem((BLOCK, hidden), BF16), vmem((BLOCK, hidden), F32),
            vmem(gd, BF16), vmem(gu, BF16), vmem(go, BF16),
            dma((3 * shards,)), dma((shards + up_chunks + 1,)),
        ],
        compiler_params=pltpu.CompilerParams(vmem_limit_bytes=VMEM_LIMIT),
    )(att, x, out_grad, flat, *own, *full)


def add_rows(out, terms):
    total = terms[0][...].astype(F32)
    for term in terms[1:]:
        total = total + term[...].astype(F32)
    out[...] = total.astype(out.dtype)


def reduce_steps(net, slab, out, own, near, side, mate, tall, sems, group):
    asend, arecv, bsend, brecv, csend, crecv, dsend, drecv, esend, erecv, fsend, frecv, gsend, grecv, lsem = sems
    r, s, z, y, c = net.r, net.s, net.z, net.y, net.c
    base = z // group * group
    zz = lax.rem(z, group)
    inner = [lax.rem(zz + d, group) for d in range(1, group)]
    near_copy = lambda: remote(slab(1 - c), near, asend, arecv, net.sib, s)
    own_copy = lambda: pltpu.make_async_copy(slab(c), own, lsem)
    across = lambda d: remote(
        near.at[net.others[d]], side.at[d], bsend.at[d], brecv.at[d], r, net.others[d]
    )
    over = lambda: remote(near.at[s, 1 - y], mate, csend, crecv, net.yn, s)
    along = lambda d: remote(
        near.at[s, y, inner[d]], tall.at[d], dsend.at[d], drecv.at[d],
        (base + inner[d]) * 4 + net.line, s,
    )
    one, two, four = out
    mine = one(c, y, z)
    levels = net.levels

    def climb(k, up):
        at = z - k if up else z + k
        piece = one(c, y, at)
        target = (z + 1 if up else z - 1) * 4 + net.line
        return remote(piece, piece, esend.at[int(up), k], erecv.at[int(up), k], target, s)

    def landed(k, up):
        at = z - k if up else z + k
        piece = one(c, y, at)
        return remote(piece, piece, esend.at[int(up), k], erecv.at[int(up), k - 1], net.r, s)

    def both_ways(k, act):
        here = (z - k >= 0, z + k < levels)
        more = (z + 1 < levels, z > 0)
        pl.when(jnp.logical_and(here[0], more[0]))(lambda: act(True))
        pl.when(jnp.logical_and(here[1], more[1]))(lambda: act(False))

    def wait_from(k):
        pl.when(z - k >= 0)(lambda: landed(k, True).wait_recv())
        pl.when(z + k < levels)(lambda: landed(k, False).wait_recv())

    pair = lambda: remote(two(c, y), two(c, y), fsend, frecv, net.yn, s)
    last = lambda: remote(four(c), four(c), gsend, grecv, net.sib, s)
    n_side, n_inner = len(net.others), len(inner)

    def step0():
        near_copy().start()
        own_copy().start()

    def step1():
        near_copy().wait_recv()
        own_copy().wait()
        for t in range(net.shards):
            for half in range(2):
                add_rows(near.at[t, half], [own.at[t, half], near.at[t, half]])
        for d in range(n_side):
            across(d).start()

    def step2():
        for d in range(n_side):
            across(d).wait_recv()
        for half in range(2):
            add_rows(
                near.at[s, half], [near.at[s, half]] + [side.at[d, half] for d in range(n_side)]
            )
        over().start()

    def step3():
        over().wait_recv()
        add_rows(near.at[s, y], [near.at[s, y], mate])
        for d in range(n_inner):
            along(d).start()

    def step4():
        for d in range(n_inner):
            along(d).wait_recv()
        add_rows(mine, [near.at[s, y, zz]] + [tall.at[d] for d in range(n_inner)])
        both_ways(0, lambda up: climb(0, up).start())

    def onward(k):
        def step():
            wait_from(k)
            both_ways(k, lambda up: climb(k, up).start())

        return step

    def step5():
        wait_from(levels - 1)
        pair().start()

    def step6():
        pair().wait_recv()
        last().start()

    def step7():
        last().wait_recv()

    def drain():
        near_copy().wait_send()
        for d in range(n_side):
            across(d).wait_send()
        over().wait_send()
        for d in range(n_inner):
            along(d).wait_send()
        for k in range(levels - 1):
            both_ways(k, lambda up: climb(k, up).wait_send())
        pair().wait_send()
        last().wait_send()

    middle = [onward(k) for k in range(1, levels - 1)]
    return [step0, step1, step2, step3, step4, *middle, step5, step6, step7], drain


def reduce_scratch(shards, levels, group, rows, cols):
    dma = pltpu.SemaphoreType.DMA
    vmem = pltpu.VMEM
    many = lambda n: dma((max(n, 1),))
    buffers = [
        vmem((shards, 2, group, rows, cols), BF16),
        vmem((shards, 2, group, rows, cols), BF16),
        vmem((max(shards - 1, 1), 2, group, rows, cols), BF16),
        vmem((group, rows, cols), BF16),
        vmem((max(group - 1, 1), rows, cols), BF16),
    ]
    sems = [
        dma(()), dma(()), many(shards - 1), many(shards - 1), dma(()), dma(()),
        many(group - 1), many(group - 1), dma((2, levels)), dma((2, levels)),
        dma(()), dma(()), dma(()), dma(()), dma(()),
    ]
    return buffers + sems


SCRATCH = 20


def small_steps(net, src, out, near, side, mate, tall, sems):
    asend, arecv, bsend, brecv, csend, crecv, dsend, drecv = sems
    r, s, z, y, c = net.r, net.s, net.z, net.y, net.c
    near_copy = lambda: remote(src, near.at[1], asend, arecv, net.sib, s)
    across = lambda d: remote(
        near.at[0, net.others[d]], side.at[s], bsend.at[d], brecv.at[d], r, net.others[d]
    )
    over = lambda: remote(mate.at[0], mate.at[1], csend, crecv, net.yn, s)
    along = lambda d: remote(
        tall.at[z], tall.at[z], dsend.at[d], drecv.at[d], net.heights[d] * 4 + net.line, s
    )

    def step0():
        near_copy().start()

    def step1():
        near_copy().wait_recv()
        near[0] = src[...] + near[1]
        side[s] = near[0, s]
        for d in range(len(net.others)):
            across(d).start()

    def step2():
        for d in range(len(net.others)):
            across(d).wait_recv()
        total = side[0]
        for t in range(1, net.shards):
            total = total + side[t]
        mate[0] = total
        over().start()

    def step3():
        over().wait_recv()
        tall[z] = mate[0] + mate[1]
        for d in range(len(net.heights)):
            along(d).start()

    def step4():
        for d in range(len(net.heights)):
            along(d).wait_recv()
        total = tall[0]
        for t in range(1, net.levels):
            total = total + tall[t]
        out[...] = total

    def drain():
        near_copy().wait_send()
        for d in range(len(net.others)):
            across(d).wait_send()
        over().wait_send()
        for d in range(len(net.heights)):
            along(d).wait_send()

    return [step0, step1, step2, step3, step4], drain


def small_scratch(shards, levels, rows):
    dma = pltpu.SemaphoreType.DMA
    vmem = pltpu.VMEM
    return [
        vmem((2, shards, 1, rows), F32), vmem((shards, 1, rows), F32),
        vmem((2, 1, rows), F32), vmem((levels, 1, rows), F32),
        dma(()), dma(()), dma((max(shards - 1, 1),)), dma((max(shards - 1, 1),)),
        dma(()), dma(()), dma((levels - 1,)), dma((levels - 1,)),
    ]


def places(ref, chunk, core_first, levels, rows, cols):
    if len(ref.shape) != 2:
        return (
            lambda c, y, z: ref.at[chunk, c, y, z], lambda c, y: ref.at[chunk, c, y],
            lambda c: ref.at[chunk, c],
        )
    if core_first:

        def view(c, at, size):
            lanes = pl.ds(pl.multiple_of((chunk * 2 + c) * cols, cols), cols)
            return ref.at[pl.ds(pl.multiple_of(at, rows), size), lanes]

        return (
            lambda c, y, z: view(c, (y * levels + z) * rows, rows),
            lambda c, y: view(c, y * levels * rows, levels * rows),
            lambda c: view(c, 0, 2 * levels * rows),
        )

    def span(at, count):
        first = (chunk * 4 * levels + at) * rows
        return ref.at[pl.ds(pl.multiple_of(first, rows), count * rows)]

    return (
        lambda c, y, z: span((c * 2 + y) * levels + z, 1),
        lambda c, y: span((c * 2 + y) * levels, levels),
        lambda c: span(c * 2 * levels, 2 * levels),
    )


def spread_out(jobs, offsets):
    ticks = {}
    for n, steps in enumerate(jobs):
        for t, step in enumerate(steps):
            ticks.setdefault(n + offsets[t], []).append(step)
    return [ticks.get(t, []) for t in range(max(ticks, default=-1) + 1)]


def term_jobs(net, specs, chunk_shapes, terms, outs, rest):
    jobs, drains = [], []
    for number, (which, k, core_first) in enumerate(specs):
        scratch = rest[number * SCRATCH : (number + 1) * SCRATCH]
        ref = terms[which]
        if core_first:
            slab = lambda core, ref=ref, k=k: ref.at[k, core]
        else:
            slab = lambda core, ref=ref, k=k: ref.at[:, k, core]
        spot = places(outs[which], k, core_first, net.levels, *chunk_shapes[which])
        steps, drain = reduce_steps(net, slab, spot, *scratch[:5], scratch[5:], net.levels)
        jobs.append(steps)
        drains.append(drain)
    return jobs, drains, rest[len(specs) * SCRATCH :]


def sums_kernel(ring, shards, specs, chunk_shapes, *refs):
    n = len(chunk_shapes)
    net = Links(ring, shards)
    hello(net.partners())
    jobs, drains, _ = term_jobs(net, specs, chunk_shapes, refs[:n], refs[n : 2 * n], refs[2 * n :])
    for steps in spread_out(jobs, offsets(net.levels)):
        for step in steps:
            step()
    for drain in drains:
        drain()


def tail_kernel(ring, shards, specs, chunk_shapes, n0, *refs):
    (
        go_ref, lse_ref, w_ref, mid_ref, small_ref, q_in, k_in, kt_in, vt_in, o_in, xr_in,
    ) = refs[:11]
    n_terms = len(chunk_shapes)
    terms, refs = refs[11 : 11 + n_terms], refs[11 + n_terms :]
    out_ref, outs, (qkv_ref, total_small) = refs[0], refs[1 : 1 + n_terms], refs[1 + n_terms : 3 + n_terms]
    (
        q_ref, k_ref, kt_ref, vt_ref, o_ref,
        g_ref, x_ref, v_ref, delta_ref, acc_ref, dk_ref, dv_ref, pq_ref, stage_ref, got_ref, got2_ref,
        dw_ref, dx_ref, near_ref, far_ref, db_ref, dwl_ref, row_ref, all_ref,
        gsend, grecv, ksend, krecv, xsend, xrecv, lsem,
    ) = refs[3 + n_terms : 34 + n_terms]
    rest = refs[34 + n_terms :]
    net = Links(ring, shards)
    r, s = net.r, net.s
    levels, members = net.levels, ring // GROUPS
    sub = levels // GROUPS
    g, m = r // members, lax.rem(r, members)
    peers = [lax.rem(g + d, GROUPS) for d in range(1, GROUPS)]
    mates = [lax.rem(m + d, members) for d in range(1, members)]
    partners = net.partners()
    if levels != GROUPS:
        partners = partners + [(p * members + m, s, True) for p in peers]
        partners = partners + [(g * members + t, s, True) for t in mates]
    else:
        partners = partners + [(g * members + 3 - m, s, True)]
    hello(partners)

    def give(p):
        return remote(go_ref.at[p], g_ref.at[g], gsend.at[p], grecv.at[g], p * members + m, s)

    def take(p):
        return remote(go_ref.at[p], g_ref.at[p], gsend.at[p], grecv.at[p], p * members + m, s)

    for p in peers:
        give(p).start()
    loads = [
        pltpu.make_async_copy(src, dst, lsem.at[n])
        for n, (src, dst) in enumerate(
            ((vt_in, vt_ref), (k_in, k_ref), (q_in, q_ref), (kt_in, kt_ref), (o_in, o_ref),
             (xr_in, x_ref))
        )
    ]
    for load in loads:
        load.start()
    g_ref[g] = go_ref[g]

    jobs, drains, rest = term_jobs(net, specs, chunk_shapes, terms, outs, rest)
    qkv_jobs = []
    for k in range(QKV_CHUNKS):
        steps, drain = reduce_steps(
            net, lambda core, k=k: dwl_ref.at[:, k, core], places(all_ref, k, False, levels, 0, 0),
            *rest[:5], rest[5:SCRATCH], sub
        )
        qkv_jobs.append(steps)
        drains.append(drain)
        rest = rest[SCRATCH:]
    vec_steps, drain = small_steps(net, small_ref, total_small, *rest[:4], rest[4:])
    drains.append(drain)
    ticks = spread_out(jobs, offsets(levels))

    width = w_ref.shape[1]

    def prepare():
        dwl_ref[...] = dw_ref[...].astype(BF16).reshape(dwl_ref.shape)
        row = jnp.broadcast_to(db_ref[...], (3 * SLAB, 8)).T[:1]
        row_ref[...] = jnp.zeros(row_ref.shape, F32)
        for k in range(GROUPS):

            @pl.when(g == k)
            def _():
                row_ref[:, k * SLAB : (k + 1) * SLAB] = row[:, :SLAB]
                row_ref[:, width + k * SLAB : width + (k + 1) * SLAB] = row[:, 2 * SLAB :]

        for t in range(shards):
            small_ref[t, :, :n0] = row_ref[:, t * n0 : (t + 1) * n0]

    ready = -(-(10 * members + 2 + SHIFTS[0] + 1) // PACE)
    late = [[list(steps) for steps in zip(*qkv_jobs)], [[step] for step in vec_steps]]
    ticks += [[] for _ in range(ready + max(map(len, late)) - len(ticks))]
    ticks[ready].append(prepare)
    for series in late:
        for t, steps in enumerate(series):
            ticks[ready + t] += steps

    def tick(t, lo, hi):
        if hi - lo == 1:
            for step in ticks[lo]:
                step()
        else:
            mid = (lo + hi) // 2
            pl.when(t < mid)(lambda: tick(t, lo, mid))
            pl.when(t >= mid)(lambda: tick(t, mid, hi))

    for load in loads[:1]:
        load.wait()

    def turn(b, carry):
        rows = pl.ds(pl.multiple_of(b * BLOCK, BLOCK), BLOCK)
        for h in range(PER):
            v_ref[h, rows, :] = (
                vt_ref[b, h * HEAD_DIM : (h + 1) * HEAD_DIM, :].astype(F32).T.astype(BF16)
            )
        dk_ref[b] = jnp.zeros((SLAB, BLOCK), F32)
        dv_ref[b] = jnp.zeros((SLAB, BLOCK), F32)
        return carry

    lax.fori_loop(0, ring, turn, 0)
    dw_ref[...] = jnp.zeros(dw_ref.shape, F32)
    db_ref[...] = jnp.zeros(db_ref.shape, F32)
    for load in loads[1:]:
        load.wait()

    pairs = members // 2
    c, mt = net.c, m // 2
    fellows = [lax.rem(mt + d, pairs) for d in range(1, pairs)]
    pieces = 4
    size = BLOCK // pieces

    def cross():
        return lambda j: remote(
            stage_ref.at[j], got_ref.at[j], ksend.at[j, 0], krecv.at[j, 0], net.sib, s
        )

    to_core = cross()

    def share(j, d):
        t = fellows[d]
        return remote(
            got_ref.at[j, t], got2_ref.at[j, d], ksend.at[j, d + 1], krecv.at[j, d + 1],
            g * members + t * 2 + c, s,
        )

    def hop(j, u, side, target):
        rows = pl.ds(u * size, size)
        return remote(
            dx_ref.at[j, rows], far_ref.at[j, side, rows], xsend.at[j, u], xrecv.at[j, side, u],
            target, s,
        )

    def pass_dx(j, u):
        down = lambda: hop(j, u, 0, r - members)
        up = lambda: hop(j, u, 1, r + members)
        return down, up

    def begin(i):
        pl.when(g != i)(lambda: take(i).wait_recv())
        for h in range(PER):
            head = pl.ds(h * HEAD_DIM, HEAD_DIM)
            delta_ref[h] = jnp.sum(
                g_ref[i, head, :].astype(F32) * o_ref[i, head, :], axis=0, keepdims=True
            )
        acc_ref[...] = jnp.zeros(acc_ref.shape, F32)

    def unit(i, kb):
        keys = pl.ds(pl.multiple_of(kb * BLOCK, BLOCK), BLOCK)
        for h in range(PER):
            head = pl.ds(h * HEAD_DIM, HEAD_DIM)
            score = mm(k_ref[h, keys, :], q_ref[i, h])
            probs = jnp.exp(score - lse_ref[i, h])
            grad = g_ref[i, head, :]
            moved = (probs * (mm(v_ref[h, keys, :], grad) - delta_ref[h])).astype(BF16)
            acc_ref[h] += mm(kt_ref[kb, head, :], moved)
            dk_ref[kb, head, :] += mm(q_ref[i, h, :HEAD_DIM, :], moved, NT)
            dv_ref[kb, head, :] += mm(grad, probs.astype(BF16), NT)

    def end(i):
        for h in range(PER):
            pq_ref[i, pl.ds(h * HEAD_DIM, HEAD_DIM), :] = (
                acc_ref[h] * HEAD_DIM ** (-0.5)
            ).astype(BF16)
        for t in range(pairs):
            b = i * members + t * 2 + 1 - c
            stage_ref[i, t, :SLAB, :] = dk_ref[b].astype(BF16)
            stage_ref[i, t, SLAB:, :] = dv_ref[b].astype(BF16)
        to_core(i).start()

    def merge(j):
        to_core(j).wait_recv()
        for d, t in enumerate(fellows):
            b = j * members + t * 2 + c
            for half, ref in enumerate((dk_ref, dv_ref)):
                rows = pl.ds(half * SLAB, SLAB)
                got_ref[j, t, rows, :] = (ref[b] + got_ref[j, t, rows, :].astype(F32)).astype(BF16)
            share(j, d).start()

    def finish(j):
        b = j * members + m
        dk = dk_ref[b] + got_ref[j, mt, :SLAB, :].astype(F32)
        dv = dv_ref[b] + got_ref[j, mt, SLAB:, :].astype(F32)
        for d in range(pairs - 1):
            share(j, d).wait_recv()
            dk = dk + got2_ref[j, d, :SLAB, :].astype(F32)
            dv = dv + got2_ref[j, d, SLAB:, :].astype(F32)
        proj = jnp.concatenate([pq_ref[j], dk.astype(BF16), dv.astype(BF16)], axis=0)
        db_ref[...] += jnp.sum(proj.astype(F32), axis=1, keepdims=True)
        dx = mm(proj, w_ref[...], TN)
        near_ref[j] = dx
        dx_ref[j] = dx.astype(BF16)
        start_dx(j, 0)
        dw_ref[...] += mm(x_ref[j], proj.T, TN)

    def start_dx(j, depth):
        from_below = jnp.logical_and(g < j, g == depth)
        from_above = jnp.logical_and(g > j, GROUPS - 1 - g == depth)
        for u in range(pieces):
            rows = pl.ds(u * size, size)
            down, up = pass_dx(j, u)

            @pl.when(from_below)
            def _():
                if depth:
                    hop(j, u, 1, r).wait_recv()
                    dx_ref[j, rows] = (near_ref[j, rows] + far_ref[j, 1, rows].astype(F32)).astype(BF16)
                up().start()

            @pl.when(from_above)
            def _():
                if depth:
                    hop(j, u, 0, r).wait_recv()
                    dx_ref[j, rows] = (near_ref[j, rows] + far_ref[j, 0, rows].astype(F32)).astype(BF16)
                down().start()

    def own_dx():
        for side, there in ((0, g < GROUPS - 1), (1, g > 0)):

            @pl.when(there)
            def _():
                for u in range(pieces):
                    hop(g, u, side, r).wait_recv()
                near_ref[g] += far_ref[g, side].astype(F32)

    sizes = [i * members + m + 1 for i in range(GROUPS)][::-1]
    ends = [sum(sizes[: n + 1]) for n in range(GROUPS)]
    units = ends[-1]
    finishes = [members * n + 2 for n in (4, 7, 9, 10)]

    def advance(it, carry):
        past = [(it >= e).astype(jnp.int32) for e in ends]
        i = GROUPS - 1 - past[0] - past[1] - past[2]
        first = jnp.where(i == 3, 0, jnp.where(i == 2, ends[0], jnp.where(i == 1, ends[1], ends[2])))
        kb = it - first

        t = it // PACE
        if ticks:
            pl.when(jnp.logical_and(lax.rem(it, PACE) == 0, t < len(ticks)))(
                lambda: tick(t, 0, len(ticks))
            )

        @pl.when(it < units)
        def _():
            pl.when(kb == 0)(lambda: begin(i))
            unit(i, kb)

            @pl.when(kb == i * members + m)
            def _():
                end(i)

        def at_times(shift, act):
            n_due = sum((it - shift >= at).astype(jnp.int32) for at in finishes)
            n_done = sum((it - shift > at).astype(jnp.int32) for at in finishes)
            pl.when(n_due > n_done)(lambda: act(GROUPS - n_due))

        at_times(0, merge)
        at_times(SHIFTS[0], finish)
        for depth in range(1, GROUPS - 1):
            at_times(SHIFTS[depth], lambda j, depth=depth: start_dx(j, depth))
        return carry

    lax.fori_loop(0, PACE * len(ticks), advance, 0)

    own_dx()
    out_ref[...] = (near_ref[g] + mid_ref[...]).astype(BF16)
    if len(qkv_ref.shape) == 2:
        rows = all_ref.shape[-2]
        for part in range(4 * QKV_CHUNKS):
            for z in range(levels):
                at = (part * sub + z % sub) * rows
                piece = all_ref[part // 4, part // 2 % 2, part % 2, z]
                for t in range(3):
                    lane = t * width + z // sub * SLAB
                    qkv_ref[at : at + rows, lane : lane + SLAB] = piece[
                        :, t * SLAB : (t + 1) * SLAB
                    ]
    else:
        qkv_ref[...] = all_ref[...]
    for p in peers:
        give(p).wait_send()
    for j in range(GROUPS):
        to_core(j).wait_send()
        for d in range(pairs - 1):
            share(j, d).wait_send()
        for u in range(pieces):
            pl.when(g != j)(lambda: hop(j, u, 0, r).wait_send())
    for drain in drains:
        drain()


PACE = 2
QKV_CHUNKS = 3


def offsets(levels, gaps=(2, 2, 2, 2, 2, 2, 2, 2)):
    steps = gaps[:4] + gaps[4:5] * (levels - 2) + gaps[5:]
    return [sum(steps[:t]) for t in range(len(steps) + 1)]


SHIFTS = (2, 5, 7)


def tail_all(gat, lse, w_group, mid, small, saved, terms, n0, ring, shards, ident):
    members, levels = ring // GROUPS, ring // 4
    sub = levels // GROUPS
    width = mid.shape[1]
    part = width // shards
    shape = jax.ShapeDtypeStruct
    dma = pltpu.SemaphoreType.DMA
    vmem = pltpu.VMEM
    specs, scratch, out_shape, chunk_shapes = [], [], [], []
    for i, term in enumerate(terms):
        core_first = i > 0
        chunks = term.shape[0] if core_first else term.shape[1]
        rows, cols = term.shape[-2:]
        chunk_shapes.append((rows, cols))
        if rows % 16:
            out_shape.append(shape((chunks, 2, 2, levels, rows, cols), BF16))
        elif core_first:
            out_shape.append(shape((2 * levels * rows, chunks * 2 * cols), BF16))
        else:
            out_shape.append(shape((chunks * 4 * levels * rows, cols), BF16))
        for k in range(chunks):
            specs.append((i, k, core_first))
            scratch += reduce_scratch(shards, levels, levels, rows, cols)
    term_scratch, term_shapes = scratch, out_shape
    apart = ring * BLOCK > 4096
    if apart:
        sums = pl.pallas_call(
            lambda *refs: sums_kernel(ring, shards, specs, chunk_shapes, *refs),
            out_shape=tuple(term_shapes),
            in_specs=[ANY_SPEC] * 3,
            out_specs=(VMEM_SPEC,) * 3,
            scratch_shapes=term_scratch,
            compiler_params=pltpu.CompilerParams(
                collective_id=ident + 1, has_side_effects=True, vmem_limit_bytes=VMEM_LIMIT
            ),
        )(*terms)
    specs, chunk_shapes = ([], []) if apart else (specs, chunk_shapes)
    scratch = [] if apart else list(term_scratch)
    out_shape = [] if apart else list(term_shapes)
    terms = () if apart else terms
    rows = part // (4 * QKV_CHUNKS) // sub
    buffer = (QKV_CHUNKS, 2, 2, levels, rows, 3 * SLAB)
    for _ in range(QKV_CHUNKS):
        scratch += reduce_scratch(shards, levels, sub, rows, 3 * SLAB)
    scratch += small_scratch(shards, levels, small.shape[2])
    out_shape.append(shape(buffer if rows % 16 else (part, 3 * width), BF16))
    slab = (GROUPS, SLAB, BLOCK)
    tall = (ring, SLAB, BLOCK)
    result = pl.pallas_call(
        lambda *refs: tail_kernel(ring, shards, specs, chunk_shapes, n0, *refs),
        out_shape=(shape((BLOCK, width), BF16), *out_shape, shape((1, small.shape[2]), F32)),
        in_specs=[VMEM_SPEC] * 5 + [ANY_SPEC] * (6 + len(terms)),
        out_specs=(VMEM_SPEC,) * (3 + len(terms)),
        scratch_shapes=[
            vmem((GROUPS, PER, 2 * HEAD_DIM, BLOCK), BF16),
            vmem((PER, ring * BLOCK, 2 * HEAD_DIM), BF16),
            vmem(tall, BF16), vmem(tall, BF16), vmem(slab, F32),
            vmem(slab, BF16),
            vmem((GROUPS, BLOCK, width), BF16),
            vmem((PER, ring * BLOCK, HEAD_DIM), BF16),
            vmem((PER, 1, BLOCK), F32),
            vmem((PER, HEAD_DIM, BLOCK), F32),
            vmem(tall, F32), vmem(tall, F32), vmem(slab, BF16),
            vmem((GROUPS, members // 2, 2 * SLAB, BLOCK), BF16),
            vmem((GROUPS, members // 2, 2 * SLAB, BLOCK), BF16),
            vmem((GROUPS, members // 2 - 1, 2 * SLAB, BLOCK), BF16),
            vmem((width, 3 * SLAB), F32),
            vmem((GROUPS, BLOCK, width), BF16),
            vmem((GROUPS, BLOCK, width), F32),
            vmem((GROUPS, 2, BLOCK, width), BF16),
            vmem((3 * SLAB, 1), F32),
            vmem((shards, QKV_CHUNKS, 2, 2, sub, rows, 3 * SLAB), BF16),
            vmem((1, 2 * width), F32),
            vmem(buffer, BF16),
            dma((GROUPS,)), dma((GROUPS,)),
            dma((GROUPS, members // 2)), dma((GROUPS, members // 2)),
            dma((GROUPS, 4)), dma((GROUPS, 2, 4)), dma((6,)),
            *scratch,
        ],
        compiler_params=pltpu.CompilerParams(
            collective_id=ident, has_side_effects=True, vmem_limit_bytes=VMEM_LIMIT
        ),
    )(gat, lse, w_group, mid, small, *saved, *terms)
    return (result[0], *sums, *result[1:]) if apart else result


def on_device(
    tokens, doc_ids, qkv_weight, qv_bias, out_weight, out_bias, mid_gain, mid_shift,
    up_weight, up_bias, down_weight, down_bias, end_gain, end_shift, out_grad,
):
    width, hidden = tokens.shape[2], up_weight.shape[1]
    ring, shards = lax.axis_size("rep"), lax.axis_size("shard")
    levels = ring // 4
    sub = levels // GROUPS
    x = tokens[0]
    small = (qv_bias, out_bias, mid_gain, mid_shift, up_bias, down_bias, end_gain, end_shift)
    sizes = [v.shape[0] for v in small]
    own = (out_weight, up_weight, down_weight)
    att, flat, w_group, lse, o, q, k, kt, vt, x_rows, *full = forward_all(
        x, qkv_weight, doc_ids, list(small), own, ((2, 1, True), (0, 1, False), (1, 2, False)), ring, shards, 0
    )
    down_chunks = 6 if hidden % (6 * shards * ring * 16) == 0 else 1
    layer_out, gat, mid, flat, down, up, out = mlp_all(
        att, x, out_grad[0], flat, own, full, sizes, shards, levels, down_chunks, 6
    )
    input_grad, down, up, out, qkv, flat = tail_all(
        gat, lse, w_group, mid, flat, (q, k, kt, vt, o, x_rows), (down, up, out), sizes[0],
        ring, shards, 1,
    )
    total_down = down.reshape(-1, width).astype(F32)
    if up.ndim > 2:
        up = up.reshape(12, width // shards, -1).transpose(1, 0, 2).reshape(-1, hidden)
        out = out.reshape(2, width // shards, -1).transpose(1, 0, 2).reshape(-1, width)
    if qkv.ndim > 2:
        qkv = qkv.reshape(4 * QKV_CHUNKS, GROUPS, sub, -1, 3, SLAB).transpose(0, 2, 3, 4, 1, 5)
        qkv = qkv.reshape(-1, 3 * width)
    total_up, total_out, total_qkv = up.astype(F32), out.astype(F32), qkv.astype(F32)
    flat = flat.reshape(-1)
    totals, at = [], 0
    for size in sizes:
        totals.append(flat[at : at + size])
        at += size
    return (
        layer_out[None], input_grad[None], total_qkv, totals[0], total_out, totals[1], totals[2],
        totals[3], total_up, totals[4], total_down, totals[5], totals[6], totals[7],
    )


def solution(mesh):
    rows = P("shard", None)
    flat = P("shard")
    acts = P("shard", "rep", None)
    in_specs = (
        acts, rows, rows, flat, rows, flat, flat, flat, rows, flat, rows, flat, flat, flat, acts
    )
    out_specs = (acts, acts, rows, flat, rows, flat, flat, flat, rows, flat, rows, flat, flat, flat)
    return jax.shard_map(
        on_device, mesh=mesh, in_specs=in_specs, out_specs=out_specs, check_vma=False
    )
```

```python
import jax
import jax.numpy as jnp
from jax import lax
from jax.experimental import pallas as pl
from jax.experimental.pallas import tpu as pltpu
from jax.sharding import PartitionSpec as P

HEADS = 12
HEAD_DIM = 64
BLOCK = 256
GROUPS = 4
PER = HEADS // GROUPS
SLAB = PER * HEAD_DIM
EPSILON = 1e-05
FAR = 2.0**100
F32 = jnp.float32
BF16 = jnp.bfloat16
LANES = 128
NN = (((1,), (0,)), ((), ()))
NT = (((1,), (1,)), ((), ()))
TN = (((0,), (0,)), ((), ()))
VMEM_SPEC = pl.BlockSpec(memory_space=pltpu.VMEM)
VMEM_LIMIT = 67043328


def mm(left, right, dims=NN):
    return lax.dot_general(left, right, dims, preferred_element_type=F32)


ANY_SPEC = pl.BlockSpec(memory_space=pl.ANY)


def remote(src, dst, send, recv, rep, shard):
    return pltpu.make_async_remote_copy(
        src_ref=src, dst_ref=dst, send_sem=send, recv_sem=recv,
        device_id=(rep, shard), device_id_type=pl.DeviceIdType.MESH,
    )


def hello(partners):
    barrier = pltpu.get_barrier_semaphore()
    total = 0
    for rep, shard, there in partners:
        if there is True:
            pl.semaphore_signal(
                barrier, inc=1, device_id=(rep, shard), device_id_type=pl.DeviceIdType.MESH
            )
            total = total + 1
        else:

            @pl.when(there)
            def _():
                pl.semaphore_signal(
                    barrier, inc=1, device_id=(rep, shard), device_id_type=pl.DeviceIdType.MESH
                )

            total = total + there.astype(jnp.int32)
    pl.semaphore_wait(barrier, total)


class Links:
    def __init__(self, ring, shards):
        self.ring, self.shards = ring, shards
        self.r, self.s = lax.axis_index("rep"), lax.axis_index("shard")
        self.levels = ring // 4
        self.z, self.c = self.r // 4, lax.rem(self.r, 2)
        self.y = lax.rem(self.r // 2, 2)
        self.sib = self.r + 1 - 2 * self.c
        self.yn = self.r + 2 - 4 * self.y
        self.others = [lax.rem(self.s + d, shards) for d in range(1, shards)]
        self.heights = [lax.rem(self.z + d, self.levels) for d in range(1, self.levels)]
        self.line = lax.rem(self.r, 4)

    def partners(self):
        return (
            [(self.sib, self.s, True), (self.yn, self.s, True)]
            + [(self.r, t, True) for t in self.others]
            + [(h * 4 + self.line, self.s, True) for h in self.heights]
        )


def forward_kernel(ring, shards, parts, sizes, *refs):
    n_vec = len(sizes)
    x_ref, w_ref, docs_ref = refs[:3]
    vec_refs, own = refs[3 : 3 + n_vec], refs[3 + n_vec : 6 + n_vec]
    outs, rest = refs[6 + n_vec : 19 + n_vec], refs[19 + n_vec :]
    att_ref, flat_ref, wg_ref, lse_ref, o_out, q_out, k_out, kt_out, vt_out, xr_out = outs[:10]
    full = outs[10:]
    (
        xa_ref, wl_ref, low_ref, bias_ref, o_ref, q_ref, k_ref, kt_ref, vt_ref, top_ref, sum_ref,
        send, recv, wsend, wrecv, fsend, frecv, vsend, vrecv, asend, arecv, osem,
    ) = rest
    net = Links(ring, shards)
    r, s, z, y, c = net.r, net.s, net.z, net.y, net.c
    levels, members = net.levels, ring // GROUPS
    g, m = r // members, lax.rem(r, members)
    sib, yn, line, others = net.sib, net.yn, net.line, net.others
    above, below = z < levels - 1, z > 0
    hello(net.partners())

    halves = 2

    def move(b, kind, u, src=None):
        target = (r + 4, r - 4, yn, sib)[kind]
        rows = pl.ds(u * (BLOCK // halves), BLOCK // halves)
        src = xa_ref.at[b, rows] if src is None else src.at[rows]
        return remote(src, xa_ref.at[b, rows], send.at[kind, b, u], recv.at[b, u], target, s)

    for u in range(halves):
        pl.when(above)(lambda: move(r, 0, u, x_ref).start())
        pl.when(below)(lambda: move(r, 1, u, x_ref).start())
        move(r, 2, u, x_ref).start()
        move(r, 3, u, x_ref).start()
    xa_ref[r] = x_ref[...]

    width = x_ref.shape[1]
    for k in range(GROUPS):

        @pl.when(g == k)
        def _():
            wl_ref[s] = jnp.concatenate(
                [w_ref[:, t * width + k * SLAB : t * width + (k + 1) * SLAB] for t in range(3)], 1
            )

    flat_ref[s] = jnp.concatenate([v[...].astype(F32).reshape(1, -1) for v in vec_refs], axis=1)
    lists = [
        remote(flat_ref.at[s], flat_ref.at[s], vsend.at[d], vrecv.at[d], r, t)
        for d, t in enumerate(others)
    ]
    pieces = [(lambda rows: wl_ref.at[s, rows], wl_ref, w_ref.shape[0] // 2, 0, False)]
    for w, count, quad in parts:
        size = own[w].shape[0] // (4 if quad else 2) // count
        for j in range(count):
            pieces.append((lambda rows, w=w: own[w].at[rows], full[w], size, (count, j), quad))

    def span(piece, yy, cc):
        size, where, quad = piece[2:]
        count, j = where or (1, 0)
        part = (yy * 2 + cc) if quad else cc
        return pl.ds(pl.multiple_of((part * count + j) * size, size), size)

    def across(at, d):
        rows = span(pieces[at], y, c)
        return remote(
            pieces[at][0](rows), pieces[at][1].at[s, rows], wsend.at[at, d], wrecv.at[at, d],
            r, others[d],
        )

    def shifted(at, d, kind, yy, cc, target):
        rows = span(pieces[at], yy, cc)
        spot = pieces[at][1].at[others[d], rows]
        return remote(spot, spot, fsend.at[at, d, kind], frecv.at[at, d, kind], target, s)

    def relay(at):
        for d in range(shards - 1):
            across(at, d).wait_recv()
            shifted(at, d, 0, y, c, sib).start()
            if pieces[at][4]:
                shifted(at, d, 1, y, c, yn).start()

    def relay_far(at):
        for d in range(shards - 1):
            shifted(at, d, 1, 1 - y, c, yn).wait_recv()
            shifted(at, d, 2, 1 - y, c, sib).start()

    def relayed(at):
        for d in range(shards - 1):
            shifted(at, d, 0, y, 1 - c, sib).wait_recv()
            if pieces[at][4]:
                shifted(at, d, 2, 1 - y, 1 - c, sib).wait_recv()

    for copy in lists:
        copy.start()
    for at in range(len(pieces)):
        for d in range(shards - 1):
            across(at, d).start()
    relay(0)
    for copy in lists:
        copy.wait_recv()
    n0 = sizes[0]
    qv = jnp.concatenate([flat_ref[t, :, :n0] for t in range(shards)], axis=1)
    for k in range(GROUPS):

        @pl.when(g == k)
        def _():
            row = jnp.concatenate(
                [qv[:, k * SLAB : (k + 1) * SLAB], qv[:, width + k * SLAB : width + (k + 1) * SLAB]],
                axis=1,
            )
            bias_ref[...] = jnp.broadcast_to(row, (8, 2 * SLAB)).T[:, :1]

    relayed(0)
    part = width // shards
    for t in range(shards):
        wg_ref[:, t * part : (t + 1) * part] = wl_ref[t].astype(F32).T.astype(BF16)

    def level(q):
        lo, hi = z, levels - 1 - z
        turn = jnp.minimum(lo, hi)
        swing = jnp.where(lax.rem(q, 2) == 1, z - (q + 1) // 2, z + q // 2)
        rest = jnp.where(lo > hi, z - (q - turn), z + (q - turn))
        return jnp.where(q <= 2 * turn, swing, rest)

    def event(n):
        k, t = (n - 2) // 4, lax.rem(n + 2, 4)
        q = jnp.where(n < 2, 0, jnp.where(lax.rem(t, 2) == 0, k + 1, k))
        j = jnp.where(n < 2, 2 * n, t)
        q = jnp.where(n >= ring - 2, levels - 1, q)
        j = jnp.where(n >= ring - 2, 2 * (n - ring + 2) + 1, j)
        lv = level(q)
        return lv * 4 + lax.rem(y + lax.rem(j, 2), 2) * 2 + lax.rem(c + j // 2, 2), lv, j

    sub = levels // GROUPS

    def arrive(n):
        b, lv, j = event(n)

        @pl.when(n > 0)
        def _():
            for u in range(halves):
                move(b, 3, u).wait_recv()

                @pl.when(j == 0)
                def _():
                    pl.when(jnp.logical_and(lv < z, above))(lambda: move(b, 0, u).start())
                    pl.when(jnp.logical_and(lv > z, below))(lambda: move(b, 1, u).start())
                    move(b, 2, u).start()

                pl.when(j < 2)(lambda: move(b, 3, u).start())

        both = mm(wg_ref[SLAB:, :], xa_ref[b], NT)
        kt = both[:SLAB].astype(BF16)
        kt_ref[b] = kt
        vt_ref[b] = (both[SLAB:] + bias_ref[SLAB:, :]).astype(BF16)
        at = pl.multiple_of(b * BLOCK, BLOCK)
        docs = docs_ref[:, pl.ds(at, BLOCK)].astype(F32)
        blank = jnp.zeros((HEAD_DIM - 2, BLOCK), F32)
        extra = jnp.concatenate([docs * FAR - FAR, docs * (-FAR), blank], axis=0)
        for h in range(PER):
            part = kt[h * HEAD_DIM : (h + 1) * HEAD_DIM].astype(F32)
            k_ref[h, pl.ds(at, BLOCK), :] = jnp.concatenate([part, extra], axis=0).T.astype(BF16)

        @pl.when(jnp.logical_and(j == 0, lax.rem(lv, sub) == lax.rem(z, sub)))
        def _():
            i = lv // sub
            qt = (mm(wg_ref[:SLAB, :], xa_ref[b], NT) + bias_ref[:SLAB, :]).astype(BF16)
            qt = qt.astype(F32) * HEAD_DIM ** (-0.5)
            extra = jnp.concatenate([docs, 1.0 - docs, blank], axis=0)
            for h in range(PER):
                part = qt[h * HEAD_DIM : (h + 1) * HEAD_DIM]
                q_ref[i, h] = jnp.concatenate([part, extra], axis=0).astype(BF16)

    def unit(i, kb):
        keys = pl.ds(pl.multiple_of(kb * BLOCK, BLOCK), BLOCK)
        for h in range(PER):
            head = pl.ds(h * HEAD_DIM, HEAD_DIM)
            score = mm(k_ref[h, keys, :], q_ref[i, h])
            old = top_ref[i, h]
            new = jnp.maximum(old, jnp.max(score, axis=0, keepdims=True))
            probs = jnp.exp(score - new)
            shrink = jnp.exp(old - new)
            top_ref[i, h] = new
            sum_ref[i, h] = sum_ref[i, h] * shrink + jnp.sum(probs, axis=0, keepdims=True)
            o_ref[i, head, :] = o_ref[i, head, :] * shrink + mm(
                vt_ref[kb, head, :], probs.astype(BF16)
            )

    def attend(n):
        b, lv, j = event(n)
        first = jnp.logical_and(j == 0, lax.rem(lv, sub) == lax.rem(z, sub))
        known = jnp.where(n < 2, 1, jnp.minimum((n - 2) // 4 + 2, levels))

        def pair(u, carry):
            near = u < known
            seen = level(jnp.minimum(u, known - 1))
            old = event(jnp.maximum(u - known, 0))[0]
            i = jnp.where(near, seen, lv) // sub
            kb = jnp.where(near, b, old)
            query = i * members + m
            mine = jnp.where(near, lax.rem(seen, sub) == lax.rem(z, sub), old < b)
            pl.when(jnp.logical_and(mine, kb <= query))(lambda: unit(i, kb))
            return carry

        lax.fori_loop(0, known + jnp.where(first, n, 0), pair, 0)

    top_ref[...] = jnp.full(top_ref.shape, -jnp.inf, F32)
    sum_ref[...] = jnp.zeros(sum_ref.shape, F32)
    o_ref[...] = jnp.zeros(o_ref.shape, F32)
    lag = 4
    turn_on = ring - 5

    def advance(n, carry):
        pl.when(n < ring)(lambda: arrive(n))

        @pl.when(n == turn_on)
        def _():
            for at in range(len(pieces)):
                if pieces[at][4]:
                    relay(at)

        pl.when(n >= lag)(lambda: attend(n - lag))
        return carry

    lax.fori_loop(0, ring + lag, advance, 0)
    saves = [
        pltpu.make_async_copy(src, dst, osem.at[n])
        for n, (src, dst) in enumerate(
            ((k_ref, k_out), (kt_ref, kt_out), (vt_ref, vt_out), (q_ref, q_out), (o_ref, o_out))
        )
    ]
    saves += [
        pltpu.make_async_copy(xa_ref.at[i * members + m], xr_out.at[i], osem.at[5 + i])
        for i in range(GROUPS)
    ]
    for save in saves[:3] + saves[5:]:
        save.start()

    def give(i):
        return remote(low_ref.at[i], att_ref.at[g], asend.at[i], arecv.at[g], i * members + m, s)

    for i in range(GROUPS):
        for h in range(PER):
            head = pl.ds(h * HEAD_DIM, HEAD_DIM)
            out = o_ref[i, head, :] / sum_ref[i, h]
            o_ref[i, head, :] = out
            low_ref[i, head, :] = out.astype(BF16)
            lse_ref[i, h] = top_ref[i, h] + jnp.log(sum_ref[i, h])

        @pl.when(g == i)
        def _():
            att_ref[g] = low_ref[i]

        pl.when(g != i)(lambda: give(i).start())
    for save in saves[3:5]:
        save.start()
    for at in range(1, len(pieces)):
        if pieces[at][4]:
            relay_far(at)
        else:
            relay(at)
    for d in range(1, GROUPS):
        p = lax.rem(g + d, GROUPS)
        remote(low_ref.at[0], att_ref.at[p], asend.at[0], arecv.at[p], r, s).wait_recv()
    for at in range(1, len(pieces)):
        relayed(at)
    for i in range(GROUPS):
        pl.when(g != i)(lambda: give(i).wait_send())

    def sent(e, carry):
        b, lv, j = event(e)

        for u in range(halves):

            @pl.when(j == 0)
            def _():
                pl.when(jnp.logical_and(lv <= z, above))(lambda: move(b, 0, u).wait_send())
                pl.when(jnp.logical_and(lv >= z, below))(lambda: move(b, 1, u).wait_send())
                move(b, 2, u).wait_send()

            pl.when(j < 2)(lambda: move(b, 3, u).wait_send())
        return carry

    lax.fori_loop(0, ring, sent, 0)
    for copy in lists:
        copy.wait_send()
    for at in range(len(pieces)):
        for d in range(shards - 1):
            across(at, d).wait_send()
            shifted(at, d, 0, y, c, sib).wait_send()
            if pieces[at][4]:
                shifted(at, d, 1, y, c, yn).wait_send()
                shifted(at, d, 2, 1 - y, c, sib).wait_send()
    for save in saves:
        save.wait()


def forward_all(x, qkv_weight, docs, vectors, weights, parts, ring, shards, ident):
    shape = jax.ShapeDtypeStruct
    dma = pltpu.SemaphoreType.DMA
    vmem = pltpu.VMEM
    n = 1 + sum(part[1] for part in parts)
    width = x.shape[1]
    sizes = [v.shape[0] for v in vectors]
    per = max(shards - 1, 1)
    o = (GROUPS, SLAB, BLOCK)
    q = (GROUPS, PER, 2 * HEAD_DIM, BLOCK)
    k = (PER, ring * BLOCK, 2 * HEAD_DIM)
    t = (ring, SLAB, BLOCK)
    return pl.pallas_call(
        lambda *refs: forward_kernel(ring, shards, parts, sizes, *refs),
        out_shape=(
            shape(o, BF16), shape((shards, 1, sum(sizes)), F32), shape((3 * SLAB, width), BF16),
            shape((GROUPS, PER, 1, BLOCK), F32), shape(o, F32), shape(q, BF16), shape(k, BF16),
            shape(t, BF16), shape(t, BF16), shape((GROUPS,) + x.shape, BF16),
        )
        + tuple(shape((shards,) + w.shape, w.dtype) for w in weights),
        in_specs=[VMEM_SPEC] * (3 + len(vectors)) + [ANY_SPEC] * 3,
        out_specs=(VMEM_SPEC,) * 4 + (ANY_SPEC,) * 9,
        scratch_shapes=[
            vmem((ring,) + x.shape, BF16), vmem((shards, width // shards, 3 * SLAB), BF16),
            vmem(o, BF16), vmem((2 * SLAB, 1), F32), vmem(o, F32), vmem(q, BF16), vmem(k, BF16),
            vmem(t, BF16), vmem(t, BF16),
            vmem((GROUPS, PER, 1, BLOCK), F32), vmem((GROUPS, PER, 1, BLOCK), F32),
            dma((4, ring, 2)), dma((ring, 2)), dma((n, per)), dma((n, per)), dma((n, per, 3)),
            dma((n, per, 3)), dma((per,)), dma((per,)),
            dma((GROUPS,)), dma((GROUPS,)), dma((5 + GROUPS,)),
        ],
        compiler_params=pltpu.CompilerParams(
            collective_id=ident, has_side_effects=True, vmem_limit_bytes=VMEM_LIMIT
        ),
    )(x, qkv_weight, docs, *vectors, *weights)


def layer_norm(hidden, gain, shift):
    centre = hidden - jnp.mean(hidden, axis=-1, keepdims=True)
    inverse = lax.rsqrt(jnp.mean(centre * centre, axis=-1, keepdims=True) + EPSILON)
    normed = centre * inverse
    return (normed * gain + shift, normed, inverse)


def norm_back(grad_output, normed, inverse, gain):
    grad_normed = grad_output * gain
    centred = grad_normed - jnp.mean(grad_normed, axis=-1, keepdims=True)
    return inverse * (centred - normed * jnp.mean(grad_normed * normed, axis=-1, keepdims=True))


def mlp_kernel(
    shards, sizes, att_ref, x_ref, og_ref, flat_ref, *refs,
):
    own, full = refs[:3], refs[3:6]
    out_ref, gat_ref, mid_ref, small_ref, down_out, up_out, outw_out = refs[6:13]
    wo_ref, wu_ref, wd_ref, act_ref, slope_ref, gd_ref, gu_ref, go_ref, lsem, ssem = refs[13:]
    s = lax.axis_index("shard")
    width = x_ref.shape[1]
    hidden = wu_ref.shape[1]
    loads = []
    for w, ref in enumerate((wo_ref, wu_ref, wd_ref)):
        size = own[w].shape[0]
        group = []
        for d in range(shards):
            t = lax.rem(s + d, shards)
            rows = pl.ds(pl.multiple_of(t * size, size), size)
            src = own[w] if d == 0 else full[w].at[t]
            group.append(pltpu.make_async_copy(src, ref.at[rows], lsem.at[w * shards + d]))
        loads.append(group)
        for load in group:
            load.start()

    def ready(w):
        for load in loads[w]:
            load.wait()

    starts = [sum(sizes[:n]) for n in range(len(sizes))]

    def vector(n):
        return jnp.concatenate(
            [flat_ref[t, :, starts[n] : starts[n] + sizes[n]] for t in range(shards)], axis=1
        )

    def put(n, row):
        for t in range(shards):
            small_ref[t, :, starts[n] : starts[n] + sizes[n]] = row[
                :, t * sizes[n] : (t + 1) * sizes[n]
            ]

    small_ref[...] = jnp.zeros(small_ref.shape, F32)
    att = att_ref[...].reshape(width, BLOCK)
    ready(0)
    branch = mm(att, wo_ref[...], TN) + vector(1)
    gain_mid = vector(2)
    mid_out, mid_norm, mid_inv = layer_norm(x_ref[...].astype(F32) + branch, gain_mid, vector(3))
    mid_low = mid_out.astype(BF16)
    up_bias = vector(4)
    cols = 512
    ready(1)
    for at in range(0, hidden, cols):
        block = slice(at, at + cols)
        pre = mm(mid_low, wu_ref[:, block]) + up_bias[:, block]
        phi = 0.5 * (1.0 + lax.erf(pre * 0.7071067811865476))
        act_ref[:, block] = (pre * phi).astype(BF16)
        slope_ref[:, block] = phi + pre * jnp.exp(-0.5 * pre * pre) * 0.3989422804014327
    ready(2)
    ffn = mm(act_ref[...], wd_ref[...]) + vector(5)
    gain_end = vector(6)
    end_out, end_norm, end_inv = layer_norm(mid_out + ffn, gain_end, vector(7))
    out_ref[...] = end_out.astype(BF16)
    top = og_ref[...].astype(F32)

    def column(value):
        return jnp.sum(value, axis=0, keepdims=True)

    put(6, column(top * end_norm))
    put(7, column(top))
    grad_end_in = norm_back(top, end_norm, end_inv, gain_end)
    grad_ffn = grad_end_in.astype(BF16)
    put(5, column(grad_ffn.astype(F32)))
    saves = []

    def save(src, dst):
        copy = pltpu.make_async_copy(src, dst, ssem.at[len(saves)])
        copy.start()
        saves.append(copy)

    chunks = gd_ref.shape[1]
    rows = hidden // shards // chunks
    for t in range(shards):
        for k in range(chunks):
            at = t * (hidden // shards) + k * rows
            value = mm(act_ref[:, at : at + rows], grad_ffn, TN)
            gd_ref[t, k] = value.astype(BF16).reshape(gd_ref.shape[2:])
        save(gd_ref.at[t], down_out.at[t])
    grad_mid_out = grad_end_in
    ups = []
    wide = hidden // gu_ref.shape[0]
    for k in range(gu_ref.shape[0]):
        block = slice(k * wide, (k + 1) * wide)
        grad_act = mm(grad_ffn, wd_ref[block, :], NT)
        grad_pre = (grad_act * slope_ref[:, block]).astype(BF16)
        ups.append(column(grad_pre.astype(F32)))
        value = mm(mid_low, grad_pre, TN).astype(BF16)
        for half in range(2):
            gu_ref[k, half] = value[:, half * (wide // 2) : (half + 1) * (wide // 2)].reshape(
                gu_ref.shape[2:]
            )
        save(gu_ref.at[k], up_out.at[k])
        grad_mid_out = grad_mid_out + mm(grad_pre, wu_ref[:, block], NT)
    put(4, jnp.concatenate(ups, axis=1))
    put(2, column(grad_mid_out * mid_norm))
    put(3, column(grad_mid_out))
    grad_mid_in = norm_back(grad_mid_out, mid_norm, mid_inv, gain_mid)
    mid_ref[...] = grad_mid_in
    grad_branch = grad_mid_in.astype(BF16)
    put(1, column(grad_branch.astype(F32)))
    gat_ref[...] = mm(wo_ref[...], grad_branch, NT).astype(BF16).reshape(gat_ref.shape)
    value = mm(att, grad_branch).astype(BF16)
    for half in range(2):
        go_ref[0, half] = value[:, half * (width // 2) : (half + 1) * (width // 2)].reshape(
            go_ref.shape[2:]
        )
    save(go_ref, outw_out)
    for copy in saves:
        copy.wait()


def mlp_all(att, x, out_grad, flat, own, full, sizes, shards, levels, down_chunks, up_chunks):
    shape = jax.ShapeDtypeStruct
    dma = pltpu.SemaphoreType.DMA
    vmem = pltpu.VMEM
    width, hidden = own[0].shape[1], own[1].shape[1]
    gd = (shards, down_chunks, 2, 2, levels, hidden // shards // down_chunks // 4 // levels, width)
    gu = (up_chunks, 2, shards, 2, levels, width // shards // 2 // levels, hidden // up_chunks // 2)
    go = (1, 2, shards, 2, levels, width // shards // 2 // levels, width // 2)
    return pl.pallas_call(
        lambda *refs: mlp_kernel(shards, sizes, *refs),
        out_shape=(
            shape((BLOCK, width), BF16), shape((GROUPS, SLAB, BLOCK), BF16),
            shape((BLOCK, width), F32), shape(flat.shape, F32),
            shape(gd, BF16), shape(gu, BF16), shape(go, BF16),
        ),
        in_specs=[VMEM_SPEC] * 4 + [ANY_SPEC] * 6,
        out_specs=(VMEM_SPEC,) * 4 + (ANY_SPEC,) * 3,
        scratch_shapes=[
            vmem((width, width), BF16), vmem((width, hidden), BF16), vmem((hidden, width), BF16),
            vmem((BLOCK, hidden), BF16), vmem((BLOCK, hidden), F32),
            vmem(gd, BF16), vmem(gu, BF16), vmem(go, BF16),
            dma((3 * shards,)), dma((shards + up_chunks + 1,)),
        ],
        compiler_params=pltpu.CompilerParams(vmem_limit_bytes=VMEM_LIMIT),
    )(att, x, out_grad, flat, *own, *full)


def add_rows(out, terms):
    total = terms[0][...].astype(F32)
    for term in terms[1:]:
        total = total + term[...].astype(F32)
    out[...] = total.astype(out.dtype)


def reduce_steps(net, slab, out, own, near, side, mate, tall, sems, group):
    asend, arecv, bsend, brecv, csend, crecv, dsend, drecv, esend, erecv, fsend, frecv, gsend, grecv, lsem = sems
    r, s, z, y, c = net.r, net.s, net.z, net.y, net.c
    base = z // group * group
    zz = lax.rem(z, group)
    inner = [lax.rem(zz + d, group) for d in range(1, group)]
    near_copy = lambda: remote(slab(1 - c), near, asend, arecv, net.sib, s)
    own_copy = lambda: pltpu.make_async_copy(slab(c), own, lsem)
    across = lambda d: remote(
        near.at[net.others[d]], side.at[d], bsend.at[d], brecv.at[d], r, net.others[d]
    )
    over = lambda: remote(near.at[s, 1 - y], mate, csend, crecv, net.yn, s)
    along = lambda d: remote(
        near.at[s, y, inner[d]], tall.at[d], dsend.at[d], drecv.at[d],
        (base + inner[d]) * 4 + net.line, s,
    )
    one, four = out
    mine = one(c, y, z)
    levels = net.levels

    def climb(k, up):
        at = z - k if up else z + k
        piece = one(c, y, at)
        target = (z + 1 if up else z - 1) * 4 + net.line
        return remote(piece, piece, esend.at[int(up), k], erecv.at[int(up), k], target, s)

    def landed(k, up):
        at = z - k if up else z + k
        piece = one(c, y, at)
        return remote(piece, piece, esend.at[int(up), k], erecv.at[int(up), k - 1], net.r, s)

    def both_ways(k, act):
        here = (z - k >= 0, z + k < levels)
        more = (z + 1 < levels, z > 0)
        pl.when(jnp.logical_and(here[0], more[0]))(lambda: act(True))
        pl.when(jnp.logical_and(here[1], more[1]))(lambda: act(False))

    def wait_from(k):
        pl.when(z - k >= 0)(lambda: landed(k, True).wait_recv())
        pl.when(z + k < levels)(lambda: landed(k, False).wait_recv())


    def pair(at):
        return remote(one(c, y, at), one(c, y, at), fsend.at[at], frecv.at[at], net.yn, s)

    def pair_from(k):
        if k:
            pl.when(z - k >= 0)(lambda: pair(z - k).start())
            pl.when(z + k < levels)(lambda: pair(z + k).start())
        else:
            pair(z).start()

    last = lambda: remote(four(c), four(c), gsend, grecv, net.sib, s)
    n_side, n_inner = len(net.others), len(inner)

    def step0():
        near_copy().start()
        own_copy().start()

    def step1():
        near_copy().wait_recv()
        own_copy().wait()
        for t in range(net.shards):
            for half in range(2):
                add_rows(near.at[t, half], [own.at[t, half], near.at[t, half]])
        for d in range(n_side):
            across(d).start()

    def step2():
        for d in range(n_side):
            across(d).wait_recv()
        for half in range(2):
            add_rows(
                near.at[s, half], [near.at[s, half]] + [side.at[d, half] for d in range(n_side)]
            )
        over().start()

    def step3():
        over().wait_recv()
        add_rows(near.at[s, y], [near.at[s, y], mate])
        for d in range(n_inner):
            along(d).start()

    def step4():
        for d in range(n_inner):
            along(d).wait_recv()
        add_rows(mine, [near.at[s, y, zz]] + [tall.at[d] for d in range(n_inner)])
        both_ways(0, lambda up: climb(0, up).start())
        pair_from(0)

    def onward(k):
        def step():
            wait_from(k)
            both_ways(k, lambda up: climb(k, up).start())
            pair_from(k)

        return step

    def step5():
        wait_from(levels - 1)
        pair_from(levels - 1)

    def step6():
        for at in range(levels):
            piece = one(c, 1 - y, at)
            remote(piece, piece, fsend.at[at], frecv.at[at], net.yn, s).wait_recv()
        last().start()

    def step7():
        last().wait_recv()

    def drain():
        near_copy().wait_send()
        for d in range(n_side):
            across(d).wait_send()
        over().wait_send()
        for d in range(n_inner):
            along(d).wait_send()
        for k in range(levels - 1):
            both_ways(k, lambda up: climb(k, up).wait_send())
        for at in range(levels):
            pair(at).wait_send()
        last().wait_send()

    middle = [onward(k) for k in range(1, levels - 1)]
    return [step0, step1, step2, step3, step4, *middle, step5, step6, step7], drain


def reduce_scratch(shards, levels, group, rows, cols):
    dma = pltpu.SemaphoreType.DMA
    vmem = pltpu.VMEM
    many = lambda n: dma((max(n, 1),))
    buffers = [
        vmem((shards, 2, group, rows, cols), BF16),
        vmem((shards, 2, group, rows, cols), BF16),
        vmem((max(shards - 1, 1), 2, group, rows, cols), BF16),
        vmem((group, rows, cols), BF16),
        vmem((max(group - 1, 1), rows, cols), BF16),
    ]
    sems = [
        dma(()), dma(()), many(shards - 1), many(shards - 1), dma(()), dma(()),
        many(group - 1), many(group - 1), dma((2, levels)), dma((2, levels)),
        dma((levels,)), dma((levels,)), dma(()), dma(()), dma(()),
    ]
    return buffers + sems


SCRATCH = 20


def small_steps(net, src, out, near, side, mate, tall, sems):
    asend, arecv, bsend, brecv, csend, crecv, dsend, drecv = sems
    r, s, z, y, c = net.r, net.s, net.z, net.y, net.c
    near_copy = lambda: remote(src, near.at[1], asend, arecv, net.sib, s)
    across = lambda d: remote(
        near.at[0, net.others[d]], side.at[s], bsend.at[d], brecv.at[d], r, net.others[d]
    )
    over = lambda: remote(mate.at[0], mate.at[1], csend, crecv, net.yn, s)
    along = lambda d: remote(
        tall.at[z], tall.at[z], dsend.at[d], drecv.at[d], net.heights[d] * 4 + net.line, s
    )

    def step0():
        near_copy().start()

    def step1():
        near_copy().wait_recv()
        near[0] = src[...] + near[1]
        side[s] = near[0, s]
        for d in range(len(net.others)):
            across(d).start()

    def step2():
        for d in range(len(net.others)):
            across(d).wait_recv()
        total = side[0]
        for t in range(1, net.shards):
            total = total + side[t]
        mate[0] = total
        over().start()

    def step3():
        over().wait_recv()
        tall[z] = mate[0] + mate[1]
        for d in range(len(net.heights)):
            along(d).start()

    def step4():
        for d in range(len(net.heights)):
            along(d).wait_recv()
        total = tall[0]
        for t in range(1, net.levels):
            total = total + tall[t]
        out[...] = total

    def drain():
        near_copy().wait_send()
        for d in range(len(net.others)):
            across(d).wait_send()
        over().wait_send()
        for d in range(len(net.heights)):
            along(d).wait_send()

    return [step0, step1, step2, step3, step4], drain


def small_scratch(shards, levels, rows):
    dma = pltpu.SemaphoreType.DMA
    vmem = pltpu.VMEM
    return [
        vmem((2, shards, 1, rows), F32), vmem((shards, 1, rows), F32),
        vmem((2, 1, rows), F32), vmem((levels, 1, rows), F32),
        dma(()), dma(()), dma((max(shards - 1, 1),)), dma((max(shards - 1, 1),)),
        dma(()), dma(()), dma((levels - 1,)), dma((levels - 1,)),
    ]


def places(ref, chunk, core_first, levels, rows, cols):
    if len(ref.shape) != 2:
        return (
            lambda c, y, z: ref.at[chunk, c, y, z], lambda c: ref.at[chunk, c],
        )
    if core_first:

        def view(c, at, size):
            lanes = pl.ds(pl.multiple_of((chunk * 2 + c) * cols, cols), cols)
            return ref.at[pl.ds(pl.multiple_of(at, rows), size), lanes]

        return (
            lambda c, y, z: view(c, (y * levels + z) * rows, rows),
            lambda c: view(c, 0, 2 * levels * rows),
        )

    def span(at, count):
        first = (chunk * 4 * levels + at) * rows
        return ref.at[pl.ds(pl.multiple_of(first, rows), count * rows)]

    return (
        lambda c, y, z: span((c * 2 + y) * levels + z, 1),
        lambda c: span(c * 2 * levels, 2 * levels),
    )


def spread_out(jobs, offsets):
    ticks = {}
    for n, steps in enumerate(jobs):
        for t, step in enumerate(steps):
            ticks.setdefault(n + offsets[t], []).append(step)
    return [ticks.get(t, []) for t in range(max(ticks, default=-1) + 1)]


def term_jobs(net, specs, chunk_shapes, terms, outs, rest):
    jobs, drains = [], []
    for number, (which, k, core_first) in enumerate(specs):
        scratch = rest[number * SCRATCH : (number + 1) * SCRATCH]
        ref = terms[which]
        if core_first:
            slab = lambda core, ref=ref, k=k: ref.at[k, core]
        else:
            slab = lambda core, ref=ref, k=k: ref.at[:, k, core]
        spot = places(outs[which], k, core_first, net.levels, *chunk_shapes[which])
        steps, drain = reduce_steps(net, slab, spot, *scratch[:5], scratch[5:], net.levels)
        jobs.append(steps)
        drains.append(drain)
    return jobs, drains, rest[len(specs) * SCRATCH :]


def sums_kernel(ring, shards, specs, chunk_shapes, *refs):
    n = len(chunk_shapes)
    net = Links(ring, shards)
    hello(net.partners())
    jobs, drains, _ = term_jobs(net, specs, chunk_shapes, refs[:n], refs[n : 2 * n], refs[2 * n :])
    for steps in spread_out(jobs, offsets(net.levels)):
        for step in steps:
            step()
    for drain in drains:
        drain()


def tail_kernel(ring, shards, specs, chunk_shapes, n0, *refs):
    (
        go_ref, lse_ref, w_ref, mid_ref, small_ref, q_in, k_in, kt_in, vt_in, o_in, xr_in,
    ) = refs[:11]
    n_terms = len(chunk_shapes)
    terms, refs = refs[11 : 11 + n_terms], refs[11 + n_terms :]
    out_ref, outs, (qkv_ref, total_small) = refs[0], refs[1 : 1 + n_terms], refs[1 + n_terms : 3 + n_terms]
    (
        q_ref, k_ref, kt_ref, vt_ref, o_ref,
        g_ref, x_ref, v_ref, delta_ref, acc_ref, dk_ref, dv_ref, pq_ref, stage_ref, got_ref, got2_ref,
        dw_ref, dx_ref, near_ref, far_ref, db_ref, dwl_ref, row_ref, all_ref,
        gsend, grecv, ksend, krecv, xsend, xrecv, lsem,
    ) = refs[3 + n_terms : 34 + n_terms]
    rest = refs[34 + n_terms :]
    net = Links(ring, shards)
    r, s = net.r, net.s
    levels, members = net.levels, ring // GROUPS
    sub = levels // GROUPS
    g, m = r // members, lax.rem(r, members)
    peers = [lax.rem(g + d, GROUPS) for d in range(1, GROUPS)]
    mates = [lax.rem(m + d, members) for d in range(1, members)]
    partners = net.partners()
    if levels != GROUPS:
        partners = partners + [(p * members + m, s, True) for p in peers]
        partners = partners + [(g * members + t, s, True) for t in mates]
    else:
        partners = partners + [(g * members + 3 - m, s, True)]
    hello(partners)

    def give(p):
        return remote(go_ref.at[p], g_ref.at[g], gsend.at[p], grecv.at[g], p * members + m, s)

    def take(p):
        return remote(go_ref.at[p], g_ref.at[p], gsend.at[p], grecv.at[p], p * members + m, s)

    for p in peers:
        give(p).start()
    loads = [
        pltpu.make_async_copy(src, dst, lsem.at[n])
        for n, (src, dst) in enumerate(
            ((vt_in, vt_ref), (k_in, k_ref), (q_in, q_ref), (kt_in, kt_ref), (o_in, o_ref),
             (xr_in, x_ref))
        )
    ]
    for load in loads:
        load.start()
    g_ref[g] = go_ref[g]

    jobs, drains, rest = term_jobs(net, specs, chunk_shapes, terms, outs, rest)
    qkv_jobs = []
    for k in range(QKV_CHUNKS):
        steps, drain = reduce_steps(
            net, lambda core, k=k: dwl_ref.at[:, k, core], places(all_ref, k, False, levels, 0, 0),
            *rest[:5], rest[5:SCRATCH], sub
        )
        qkv_jobs.append(steps)
        drains.append(drain)
        rest = rest[SCRATCH:]
    vec_steps, drain = small_steps(net, small_ref, total_small, *rest[:4], rest[4:])
    drains.append(drain)
    ticks = spread_out(jobs, offsets(levels))

    width = w_ref.shape[1]

    def prepare():
        dwl_ref[...] = dw_ref[...].astype(BF16).reshape(dwl_ref.shape)
        row = jnp.broadcast_to(db_ref[...], (3 * SLAB, 8)).T[:1]
        row_ref[...] = jnp.zeros(row_ref.shape, F32)
        for k in range(GROUPS):

            @pl.when(g == k)
            def _():
                row_ref[:, k * SLAB : (k + 1) * SLAB] = row[:, :SLAB]
                row_ref[:, width + k * SLAB : width + (k + 1) * SLAB] = row[:, 2 * SLAB :]

        for t in range(shards):
            small_ref[t, :, :n0] = row_ref[:, t * n0 : (t + 1) * n0]

    ready = -(-(10 * members + 2 + SHIFTS[0] + 1) // PACE)
    late = [[list(steps) for steps in zip(*qkv_jobs)], [[step] for step in vec_steps]]
    ticks += [[] for _ in range(ready + max(map(len, late)) - len(ticks))]
    ticks[ready].append(prepare)
    for series in late:
        for t, steps in enumerate(series):
            ticks[ready + t] += steps

    def tick(t, lo, hi):
        if hi - lo == 1:
            for step in ticks[lo]:
                step()
        else:
            mid = (lo + hi) // 2
            pl.when(t < mid)(lambda: tick(t, lo, mid))
            pl.when(t >= mid)(lambda: tick(t, mid, hi))

    for load in loads[:1]:
        load.wait()

    def turn(b, carry):
        rows = pl.ds(pl.multiple_of(b * BLOCK, BLOCK), BLOCK)
        for h in range(PER):
            v_ref[h, rows, :] = (
                vt_ref[b, h * HEAD_DIM : (h + 1) * HEAD_DIM, :].astype(F32).T.astype(BF16)
            )
        dk_ref[b] = jnp.zeros((SLAB, BLOCK), F32)
        dv_ref[b] = jnp.zeros((SLAB, BLOCK), F32)
        return carry

    lax.fori_loop(0, ring, turn, 0)
    dw_ref[...] = jnp.zeros(dw_ref.shape, F32)
    db_ref[...] = jnp.zeros(db_ref.shape, F32)
    for load in loads[1:]:
        load.wait()

    pairs = members // 2
    c, mt = net.c, m // 2
    fellows = [lax.rem(mt + d, pairs) for d in range(1, pairs)]
    pieces = 4
    size = BLOCK // pieces

    def cross():
        return lambda j: remote(
            stage_ref.at[j], got_ref.at[j], ksend.at[j, 0], krecv.at[j, 0], net.sib, s
        )

    to_core = cross()

    def share(j, d):
        t = fellows[d]
        return remote(
            got_ref.at[j, t], got2_ref.at[j, d], ksend.at[j, d + 1], krecv.at[j, d + 1],
            g * members + t * 2 + c, s,
        )

    def hop(j, u, side, target):
        rows = pl.ds(u * size, size)
        return remote(
            dx_ref.at[j, rows], far_ref.at[j, side, rows], xsend.at[j, u], xrecv.at[j, side, u],
            target, s,
        )

    def pass_dx(j, u):
        down = lambda: hop(j, u, 0, r - members)
        up = lambda: hop(j, u, 1, r + members)
        return down, up

    def begin(i):
        pl.when(g != i)(lambda: take(i).wait_recv())
        for h in range(PER):
            head = pl.ds(h * HEAD_DIM, HEAD_DIM)
            delta_ref[h] = jnp.sum(
                g_ref[i, head, :].astype(F32) * o_ref[i, head, :], axis=0, keepdims=True
            )
        acc_ref[...] = jnp.zeros(acc_ref.shape, F32)

    def unit(i, kb):
        keys = pl.ds(pl.multiple_of(kb * BLOCK, BLOCK), BLOCK)
        for h in range(PER):
            head = pl.ds(h * HEAD_DIM, HEAD_DIM)
            score = mm(k_ref[h, keys, :], q_ref[i, h])
            probs = jnp.exp(score - lse_ref[i, h])
            grad = g_ref[i, head, :]
            moved = (probs * (mm(v_ref[h, keys, :], grad) - delta_ref[h])).astype(BF16)
            acc_ref[h] += mm(kt_ref[kb, head, :], moved)
            dk_ref[kb, head, :] += mm(q_ref[i, h, :HEAD_DIM, :], moved, NT)
            dv_ref[kb, head, :] += mm(grad, probs.astype(BF16), NT)

    def end(i):
        for h in range(PER):
            pq_ref[i, pl.ds(h * HEAD_DIM, HEAD_DIM), :] = (
                acc_ref[h] * HEAD_DIM ** (-0.5)
            ).astype(BF16)
        for t in range(pairs):
            b = i * members + t * 2 + 1 - c
            stage_ref[i, t, :SLAB, :] = dk_ref[b].astype(BF16)
            stage_ref[i, t, SLAB:, :] = dv_ref[b].astype(BF16)
        to_core(i).start()

    def merge(j):
        to_core(j).wait_recv()
        for d, t in enumerate(fellows):
            b = j * members + t * 2 + c
            for half, ref in enumerate((dk_ref, dv_ref)):
                rows = pl.ds(half * SLAB, SLAB)
                got_ref[j, t, rows, :] = (ref[b] + got_ref[j, t, rows, :].astype(F32)).astype(BF16)
            share(j, d).start()

    def finish(j):
        b = j * members + m
        dk = dk_ref[b] + got_ref[j, mt, :SLAB, :].astype(F32)
        dv = dv_ref[b] + got_ref[j, mt, SLAB:, :].astype(F32)
        for d in range(pairs - 1):
            share(j, d).wait_recv()
            dk = dk + got2_ref[j, d, :SLAB, :].astype(F32)
            dv = dv + got2_ref[j, d, SLAB:, :].astype(F32)
        proj = jnp.concatenate([pq_ref[j], dk.astype(BF16), dv.astype(BF16)], axis=0)
        db_ref[...] += jnp.sum(proj.astype(F32), axis=1, keepdims=True)
        dx = mm(proj, w_ref[...], TN)
        near_ref[j] = dx
        dx_ref[j] = dx.astype(BF16)
        start_dx(j, 0)
        dw_ref[...] += mm(x_ref[j], proj.T, TN)

    def start_dx(j, depth):
        from_below = jnp.logical_and(g < j, g == depth)
        from_above = jnp.logical_and(g > j, GROUPS - 1 - g == depth)
        for u in range(pieces):
            rows = pl.ds(u * size, size)
            down, up = pass_dx(j, u)

            @pl.when(from_below)
            def _():
                if depth:
                    hop(j, u, 1, r).wait_recv()
                    dx_ref[j, rows] = (near_ref[j, rows] + far_ref[j, 1, rows].astype(F32)).astype(BF16)
                up().start()

            @pl.when(from_above)
            def _():
                if depth:
                    hop(j, u, 0, r).wait_recv()
                    dx_ref[j, rows] = (near_ref[j, rows] + far_ref[j, 0, rows].astype(F32)).astype(BF16)
                down().start()

    def own_dx():
        for side, there in ((0, g < GROUPS - 1), (1, g > 0)):

            @pl.when(there)
            def _():
                for u in range(pieces):
                    hop(g, u, side, r).wait_recv()
                near_ref[g] += far_ref[g, side].astype(F32)

    sizes = [i * members + m + 1 for i in range(GROUPS)][::-1]
    ends = [sum(sizes[: n + 1]) for n in range(GROUPS)]
    units = ends[-1]
    finishes = [members * n + 2 for n in (4, 7, 9, 10)]

    def advance(it, carry):
        past = [(it >= e).astype(jnp.int32) for e in ends]
        i = GROUPS - 1 - past[0] - past[1] - past[2]
        first = jnp.where(i == 3, 0, jnp.where(i == 2, ends[0], jnp.where(i == 1, ends[1], ends[2])))
        kb = it - first

        t = it // PACE
        if ticks:
            pl.when(jnp.logical_and(lax.rem(it, PACE) == 0, t < len(ticks)))(
                lambda: tick(t, 0, len(ticks))
            )

        @pl.when(it < units)
        def _():
            pl.when(kb == 0)(lambda: begin(i))
            unit(i, kb)

            @pl.when(kb == i * members + m)
            def _():
                end(i)

        def at_times(shift, act):
            n_due = sum((it - shift >= at).astype(jnp.int32) for at in finishes)
            n_done = sum((it - shift > at).astype(jnp.int32) for at in finishes)
            pl.when(n_due > n_done)(lambda: act(GROUPS - n_due))

        at_times(0, merge)
        at_times(SHIFTS[0], finish)
        for depth in range(1, GROUPS - 1):
            at_times(SHIFTS[depth], lambda j, depth=depth: start_dx(j, depth))
        return carry

    lax.fori_loop(0, PACE * len(ticks), advance, 0)

    own_dx()
    out_ref[...] = (near_ref[g] + mid_ref[...]).astype(BF16)
    if len(qkv_ref.shape) == 2:
        rows = all_ref.shape[-2]
        for part in range(4 * QKV_CHUNKS):
            for z in range(levels):
                at = (part * sub + z % sub) * rows
                piece = all_ref[part // 4, part // 2 % 2, part % 2, z]
                for t in range(3):
                    lane = t * width + z // sub * SLAB
                    qkv_ref[at : at + rows, lane : lane + SLAB] = piece[
                        :, t * SLAB : (t + 1) * SLAB
                    ]
    else:
        qkv_ref[...] = all_ref[...]
    for p in peers:
        give(p).wait_send()
    for j in range(GROUPS):
        to_core(j).wait_send()
        for d in range(pairs - 1):
            share(j, d).wait_send()
        for u in range(pieces):
            pl.when(g != j)(lambda: hop(j, u, 0, r).wait_send())
    for drain in drains:
        drain()


PACE = 2
QKV_CHUNKS = 3


def offsets(levels, gaps=(2, 2, 2, 2, 2, 2, 2, 2)):
    steps = gaps[:4] + gaps[4:5] * (levels - 2) + gaps[5:]
    return [sum(steps[:t]) for t in range(len(steps) + 1)]


SHIFTS = (2, 5, 7)


def tail_all(gat, lse, w_group, mid, small, saved, terms, n0, ring, shards, ident):
    members, levels = ring // GROUPS, ring // 4
    sub = levels // GROUPS
    width = mid.shape[1]
    part = width // shards
    shape = jax.ShapeDtypeStruct
    dma = pltpu.SemaphoreType.DMA
    vmem = pltpu.VMEM
    specs, scratch, out_shape, chunk_shapes = [], [], [], []
    for i, term in enumerate(terms):
        core_first = i > 0
        chunks = term.shape[0] if core_first else term.shape[1]
        rows, cols = term.shape[-2:]
        chunk_shapes.append((rows, cols))
        if rows % 16:
            out_shape.append(shape((chunks, 2, 2, levels, rows, cols), BF16))
        elif core_first:
            out_shape.append(shape((2 * levels * rows, chunks * 2 * cols), BF16))
        else:
            out_shape.append(shape((chunks * 4 * levels * rows, cols), BF16))
        for k in range(chunks):
            specs.append((i, k, core_first))
            scratch += reduce_scratch(shards, levels, levels, rows, cols)
    term_scratch, term_shapes = scratch, out_shape
    apart = ring * BLOCK > 4096
    if apart:
        sums = pl.pallas_call(
            lambda *refs: sums_kernel(ring, shards, specs, chunk_shapes, *refs),
            out_shape=tuple(term_shapes),
            in_specs=[ANY_SPEC] * 3,
            out_specs=(VMEM_SPEC,) * 3,
            scratch_shapes=term_scratch,
            compiler_params=pltpu.CompilerParams(
                collective_id=ident + 1, has_side_effects=True, vmem_limit_bytes=VMEM_LIMIT
            ),
        )(*terms)
    specs, chunk_shapes = ([], []) if apart else (specs, chunk_shapes)
    scratch = [] if apart else list(term_scratch)
    out_shape = [] if apart else list(term_shapes)
    terms = () if apart else terms
    rows = part // (4 * QKV_CHUNKS) // sub
    buffer = (QKV_CHUNKS, 2, 2, levels, rows, 3 * SLAB)
    for _ in range(QKV_CHUNKS):
        scratch += reduce_scratch(shards, levels, sub, rows, 3 * SLAB)
    scratch += small_scratch(shards, levels, small.shape[2])
    out_shape.append(shape(buffer if rows % 16 else (part, 3 * width), BF16))
    slab = (GROUPS, SLAB, BLOCK)
    tall = (ring, SLAB, BLOCK)
    result = pl.pallas_call(
        lambda *refs: tail_kernel(ring, shards, specs, chunk_shapes, n0, *refs),
        out_shape=(shape((BLOCK, width), BF16), *out_shape, shape((1, small.shape[2]), F32)),
        in_specs=[VMEM_SPEC] * 5 + [ANY_SPEC] * (6 + len(terms)),
        out_specs=(VMEM_SPEC,) * (3 + len(terms)),
        scratch_shapes=[
            vmem((GROUPS, PER, 2 * HEAD_DIM, BLOCK), BF16),
            vmem((PER, ring * BLOCK, 2 * HEAD_DIM), BF16),
            vmem(tall, BF16), vmem(tall, BF16), vmem(slab, F32),
            vmem(slab, BF16),
            vmem((GROUPS, BLOCK, width), BF16),
            vmem((PER, ring * BLOCK, HEAD_DIM), BF16),
            vmem((PER, 1, BLOCK), F32),
            vmem((PER, HEAD_DIM, BLOCK), F32),
            vmem(tall, F32), vmem(tall, F32), vmem(slab, BF16),
            vmem((GROUPS, members // 2, 2 * SLAB, BLOCK), BF16),
            vmem((GROUPS, members // 2, 2 * SLAB, BLOCK), BF16),
            vmem((GROUPS, members // 2 - 1, 2 * SLAB, BLOCK), BF16),
            vmem((width, 3 * SLAB), F32),
            vmem((GROUPS, BLOCK, width), BF16),
            vmem((GROUPS, BLOCK, width), F32),
            vmem((GROUPS, 2, BLOCK, width), BF16),
            vmem((3 * SLAB, 1), F32),
            vmem((shards, QKV_CHUNKS, 2, 2, sub, rows, 3 * SLAB), BF16),
            vmem((1, 2 * width), F32),
            vmem(buffer, BF16),
            dma((GROUPS,)), dma((GROUPS,)),
            dma((GROUPS, members // 2)), dma((GROUPS, members // 2)),
            dma((GROUPS, 4)), dma((GROUPS, 2, 4)), dma((6,)),
            *scratch,
        ],
        compiler_params=pltpu.CompilerParams(
            collective_id=ident, has_side_effects=True, vmem_limit_bytes=VMEM_LIMIT
        ),
    )(gat, lse, w_group, mid, small, *saved, *terms)
    return (result[0], *sums, *result[1:]) if apart else result


def widen_kernel(sizes, cuts, flat_ref, *refs):
    n = len(cuts)
    sources, targets, vectors = refs[:n], refs[n : 2 * n], refs[2 * n : 2 * n + len(sizes)]
    low, wide, isem, osem = refs[-2 * n - 2 : -n - 2], refs[-n - 2 : -2], refs[-2], refs[-1]
    loads, saves = [], []
    for w, parts in enumerate(cuts):
        size = sources[w].shape[0] // parts
        for j in range(parts):
            rows = pl.ds(j * size, size)
            at = len(loads)
            loads.append(pltpu.make_async_copy(sources[w].at[rows], low[w].at[rows], isem.at[at]))
            saves.append(
                (w, rows, pltpu.make_async_copy(wide[w].at[rows], targets[w].at[rows], osem.at[at]))
            )
    for load in loads:
        load.start()
    at = 0
    for ref, size in zip(vectors, sizes):
        ref[...] = flat_ref[:, at : at + size].reshape(size)
        at += size
    for load, (w, rows, save) in zip(loads, saves):
        load.wait()
        wide[w][rows] = low[w][rows].astype(wide[w].dtype)
        save.start()
    for _, _, save in saves:
        save.wait()


def widen_all(flat, arrays, same, sizes):
    shape = jax.ShapeDtypeStruct
    arrays = (*arrays, same)
    types = [F32] * (len(arrays) - 1) + [same.dtype]
    dma = pltpu.SemaphoreType.DMA
    cuts = [next(n for n in (4, 3, 2, 1) if a.shape[0] % (16 * n) == 0 or n == 1) for a in arrays]
    return pl.pallas_call(
        lambda *refs: widen_kernel(sizes, cuts, *refs),
        out_shape=tuple(shape(a.shape, t) for a, t in zip(arrays, types))
        + tuple(shape((size,), F32) for size in sizes),
        in_specs=[VMEM_SPEC] + [ANY_SPEC] * len(arrays),
        out_specs=(ANY_SPEC,) * len(arrays) + (VMEM_SPEC,) * len(sizes),
        scratch_shapes=[pltpu.VMEM(a.shape, BF16) for a in arrays]
        + [pltpu.VMEM(a.shape, t) for a, t in zip(arrays, types)]
        + [dma((sum(cuts),)), dma((sum(cuts),))],
        compiler_params=pltpu.CompilerParams(vmem_limit_bytes=VMEM_LIMIT),
    )(flat, *arrays)


def on_device(
    tokens, doc_ids, qkv_weight, qv_bias, out_weight, out_bias, mid_gain, mid_shift,
    up_weight, up_bias, down_weight, down_bias, end_gain, end_shift, out_grad,
):
    width, hidden = tokens.shape[2], up_weight.shape[1]
    ring, shards = lax.axis_size("rep"), lax.axis_size("shard")
    levels = ring // 4
    sub = levels // GROUPS
    x = tokens[0]
    small = (qv_bias, out_bias, mid_gain, mid_shift, up_bias, down_bias, end_gain, end_shift)
    sizes = [v.shape[0] for v in small]
    own = (out_weight, up_weight, down_weight)
    att, flat, w_group, lse, o, q, k, kt, vt, x_rows, *full = forward_all(
        x, qkv_weight, doc_ids, list(small), own, ((2, 1, True), (0, 1, False), (1, 2, False)), ring, shards, 0
    )
    down_chunks = 6 if hidden % (6 * shards * ring * 16) == 0 else 1
    layer_out, gat, mid, flat, down, up, out = mlp_all(
        att, x, out_grad[0], flat, own, full, sizes, shards, levels, down_chunks, 6
    )
    input_grad, down, up, out, qkv, flat = tail_all(
        gat, lse, w_group, mid, flat, (q, k, kt, vt, o, x_rows), (down, up, out), sizes[0],
        ring, shards, 1,
    )
    down = down.reshape(-1, width)
    if up.ndim > 2:
        up = up.reshape(12, width // shards, -1).transpose(1, 0, 2).reshape(-1, hidden)
        out = out.reshape(2, width // shards, -1).transpose(1, 0, 2).reshape(-1, width)
    if qkv.ndim > 2:
        qkv = qkv.reshape(4 * QKV_CHUNKS, GROUPS, sub, -1, 3, SLAB).transpose(0, 2, 3, 4, 1, 5)
        qkv = qkv.reshape(-1, 3 * width)
    down, up, out, qkv, input_grad, *totals = widen_all(flat, (down, up, out, qkv), input_grad, sizes)
    return (
        layer_out[None], input_grad[None], qkv, totals[0], out, totals[1], totals[2],
        totals[3], up, totals[4], down, totals[5], totals[6], totals[7],
    )


def solution(mesh):
    rows = P("shard", None)
    flat = P("shard")
    acts = P("shard", "rep", None)
    in_specs = (
        acts, rows, rows, flat, rows, flat, flat, flat, rows, flat, rows, flat, flat, flat, acts
    )
    out_specs = (acts, acts, rows, flat, rows, flat, flat, flat, rows, flat, rows, flat, flat, flat)
    return jax.shard_map(
        on_device, mesh=mesh, in_specs=in_specs, out_specs=out_specs, check_vma=False
    )
```

```python
import jax
import jax.numpy as jnp
from jax import lax
from jax.experimental import pallas as pl
from jax.experimental.pallas import tpu as pltpu
from jax.sharding import PartitionSpec as P

HEADS = 12
HEAD_DIM = 64
BLOCK = 256
GROUPS = 4
PER = HEADS // GROUPS
SLAB = PER * HEAD_DIM
EPSILON = 1e-05
FAR = 2.0**100
F32 = jnp.float32
BF16 = jnp.bfloat16
LANES = 128
NN = (((1,), (0,)), ((), ()))
NT = (((1,), (1,)), ((), ()))
TN = (((0,), (0,)), ((), ()))
VMEM_SPEC = pl.BlockSpec(memory_space=pltpu.VMEM)
VMEM_LIMIT = 67043328


def mm(left, right, dims=NN):
    return lax.dot_general(left, right, dims, preferred_element_type=F32)


ANY_SPEC = pl.BlockSpec(memory_space=pl.ANY)


def remote(src, dst, send, recv, rep, shard):
    return pltpu.make_async_remote_copy(
        src_ref=src, dst_ref=dst, send_sem=send, recv_sem=recv,
        device_id=(rep, shard), device_id_type=pl.DeviceIdType.MESH,
    )


def hello(partners):
    barrier = pltpu.get_barrier_semaphore()
    total = 0
    for rep, shard, there in partners:
        if there is True:
            pl.semaphore_signal(
                barrier, inc=1, device_id=(rep, shard), device_id_type=pl.DeviceIdType.MESH
            )
            total = total + 1
        else:

            @pl.when(there)
            def _():
                pl.semaphore_signal(
                    barrier, inc=1, device_id=(rep, shard), device_id_type=pl.DeviceIdType.MESH
                )

            total = total + there.astype(jnp.int32)
    pl.semaphore_wait(barrier, total)


class Links:
    def __init__(self, ring, shards):
        self.ring, self.shards = ring, shards
        self.r, self.s = lax.axis_index("rep"), lax.axis_index("shard")
        self.levels = ring // 4
        self.z, self.c = self.r // 4, lax.rem(self.r, 2)
        self.y = lax.rem(self.r // 2, 2)
        self.sib = self.r + 1 - 2 * self.c
        self.yn = self.r + 2 - 4 * self.y
        self.others = [lax.rem(self.s + d, shards) for d in range(1, shards)]
        self.heights = [lax.rem(self.z + d, self.levels) for d in range(1, self.levels)]
        self.line = lax.rem(self.r, 4)

    def partners(self):
        return (
            [(self.sib, self.s, True), (self.yn, self.s, True)]
            + [(self.r, t, True) for t in self.others]
            + [(h * 4 + self.line, self.s, True) for h in self.heights]
        )


def forward_kernel(ring, shards, parts, sizes, *refs):
    n_vec = len(sizes)
    x_ref, w_ref, docs_ref = refs[:3]
    vec_refs, own = refs[3 : 3 + n_vec], refs[3 + n_vec : 6 + n_vec]
    outs, rest = refs[6 + n_vec : 19 + n_vec], refs[19 + n_vec :]
    att_ref, flat_ref, wg_ref, lse_ref, o_out, q_out, k_out, kt_out, vt_out, xr_out = outs[:10]
    full = outs[10:]
    (
        xa_ref, wl_ref, low_ref, bias_ref, o_ref, q_ref, k_ref, kt_ref, vt_ref, top_ref, sum_ref,
        send, recv, wsend, wrecv, fsend, frecv, vsend, vrecv, asend, arecv, osem,
    ) = rest
    net = Links(ring, shards)
    r, s, z, y, c = net.r, net.s, net.z, net.y, net.c
    levels, members = net.levels, ring // GROUPS
    g, m = r // members, lax.rem(r, members)
    sib, yn, line, others = net.sib, net.yn, net.line, net.others
    above, below = z < levels - 1, z > 0
    hello(net.partners())

    halves = 2

    def move(b, kind, u, src=None):
        target = (r + 4, r - 4, yn, sib)[kind]
        rows = pl.ds(u * (BLOCK // halves), BLOCK // halves)
        src = xa_ref.at[b, rows] if src is None else src.at[rows]
        return remote(src, xa_ref.at[b, rows], send.at[kind, b, u], recv.at[b, u], target, s)

    for u in range(halves):
        pl.when(above)(lambda: move(r, 0, u, x_ref).start())
        pl.when(below)(lambda: move(r, 1, u, x_ref).start())
        move(r, 2, u, x_ref).start()
        move(r, 3, u, x_ref).start()
    xa_ref[r] = x_ref[...]

    width = x_ref.shape[1]
    for k in range(GROUPS):

        @pl.when(g == k)
        def _():
            wl_ref[s] = jnp.concatenate(
                [w_ref[:, t * width + k * SLAB : t * width + (k + 1) * SLAB] for t in range(3)], 1
            )

    flat_ref[s] = jnp.concatenate([v[...].astype(F32).reshape(1, -1) for v in vec_refs], axis=1)
    lists = [
        remote(flat_ref.at[s], flat_ref.at[s], vsend.at[d], vrecv.at[d], r, t)
        for d, t in enumerate(others)
    ]
    pieces = [(lambda rows: wl_ref.at[s, rows], wl_ref, w_ref.shape[0] // 2, 0, False)]
    for w, count, quad in parts:
        size = own[w].shape[0] // (4 if quad else 2) // count
        for j in range(count):
            pieces.append((lambda rows, w=w: own[w].at[rows], full[w], size, (count, j), quad))

    def span(piece, yy, cc):
        size, where, quad = piece[2:]
        count, j = where or (1, 0)
        part = (yy * 2 + cc) if quad else cc
        return pl.ds(pl.multiple_of((part * count + j) * size, size), size)

    def across(at, d):
        rows = span(pieces[at], y, c)
        return remote(
            pieces[at][0](rows), pieces[at][1].at[s, rows], wsend.at[at, d], wrecv.at[at, d],
            r, others[d],
        )

    def shifted(at, d, kind, yy, cc, target):
        rows = span(pieces[at], yy, cc)
        spot = pieces[at][1].at[others[d], rows]
        return remote(spot, spot, fsend.at[at, d, kind], frecv.at[at, d, kind], target, s)

    def relay(at):
        for d in range(shards - 1):
            across(at, d).wait_recv()
            shifted(at, d, 0, y, c, sib).start()
            if pieces[at][4]:
                shifted(at, d, 1, y, c, yn).start()

    def relay_far(at):
        for d in range(shards - 1):
            shifted(at, d, 1, 1 - y, c, yn).wait_recv()
            shifted(at, d, 2, 1 - y, c, sib).start()

    def relayed(at):
        for d in range(shards - 1):
            shifted(at, d, 0, y, 1 - c, sib).wait_recv()
            if pieces[at][4]:
                shifted(at, d, 2, 1 - y, 1 - c, sib).wait_recv()

    for copy in lists:
        copy.start()
    for at in range(len(pieces)):
        for d in range(shards - 1):
            across(at, d).start()
    relay(0)
    for copy in lists:
        copy.wait_recv()
    n0 = sizes[0]
    qv = jnp.concatenate([flat_ref[t, :, :n0] for t in range(shards)], axis=1)
    for k in range(GROUPS):

        @pl.when(g == k)
        def _():
            row = jnp.concatenate(
                [qv[:, k * SLAB : (k + 1) * SLAB], qv[:, width + k * SLAB : width + (k + 1) * SLAB]],
                axis=1,
            )
            bias_ref[...] = jnp.broadcast_to(row, (8, 2 * SLAB)).T[:, :1]

    relayed(0)
    part = width // shards
    for t in range(shards):
        wg_ref[:, t * part : (t + 1) * part] = wl_ref[t].astype(F32).T.astype(BF16)

    def level(q):
        lo, hi = z, levels - 1 - z
        turn = jnp.minimum(lo, hi)
        swing = jnp.where(lax.rem(q, 2) == 1, z - (q + 1) // 2, z + q // 2)
        rest = jnp.where(lo > hi, z - (q - turn), z + (q - turn))
        return jnp.where(q <= 2 * turn, swing, rest)

    def event(n):
        k, t = (n - 2) // 4, lax.rem(n + 2, 4)
        q = jnp.where(n < 2, 0, jnp.where(lax.rem(t, 2) == 0, k + 1, k))
        j = jnp.where(n < 2, 2 * n, t)
        q = jnp.where(n >= ring - 2, levels - 1, q)
        j = jnp.where(n >= ring - 2, 2 * (n - ring + 2) + 1, j)
        lv = level(q)
        return lv * 4 + lax.rem(y + lax.rem(j, 2), 2) * 2 + lax.rem(c + j // 2, 2), lv, j

    sub = levels // GROUPS

    def arrive(n):
        b, lv, j = event(n)

        @pl.when(n > 0)
        def _():
            for u in range(halves):
                move(b, 3, u).wait_recv()

                @pl.when(j == 0)
                def _():
                    pl.when(jnp.logical_and(lv < z, above))(lambda: move(b, 0, u).start())
                    pl.when(jnp.logical_and(lv > z, below))(lambda: move(b, 1, u).start())
                    move(b, 2, u).start()

                pl.when(j < 2)(lambda: move(b, 3, u).start())

        both = mm(wg_ref[SLAB:, :], xa_ref[b], NT)
        kt = both[:SLAB].astype(BF16)
        kt_ref[b] = kt
        vt_ref[b] = (both[SLAB:] + bias_ref[SLAB:, :]).astype(BF16)
        at = pl.multiple_of(b * BLOCK, BLOCK)
        docs = docs_ref[:, pl.ds(at, BLOCK)].astype(F32)
        blank = jnp.zeros((HEAD_DIM - 2, BLOCK), F32)
        extra = jnp.concatenate([docs * FAR - FAR, docs * (-FAR), blank], axis=0)
        for h in range(PER):
            part = kt[h * HEAD_DIM : (h + 1) * HEAD_DIM].astype(F32)
            k_ref[h, pl.ds(at, BLOCK), :] = jnp.concatenate([part, extra], axis=0).T.astype(BF16)

        @pl.when(jnp.logical_and(j == 0, lax.rem(lv, sub) == lax.rem(z, sub)))
        def _():
            i = lv // sub
            qt = (mm(wg_ref[:SLAB, :], xa_ref[b], NT) + bias_ref[:SLAB, :]).astype(BF16)
            qt = qt.astype(F32) * HEAD_DIM ** (-0.5)
            extra = jnp.concatenate([docs, 1.0 - docs, blank], axis=0)
            for h in range(PER):
                part = qt[h * HEAD_DIM : (h + 1) * HEAD_DIM]
                q_ref[i, h] = jnp.concatenate([part, extra], axis=0).astype(BF16)

    def unit(i, kb):
        keys = pl.ds(pl.multiple_of(kb * BLOCK, BLOCK), BLOCK)
        for h in range(PER):
            head = pl.ds(h * HEAD_DIM, HEAD_DIM)
            score = mm(k_ref[h, keys, :], q_ref[i, h])
            old = top_ref[i, h]
            new = jnp.maximum(old, jnp.max(score, axis=0, keepdims=True))
            probs = jnp.exp(score - new)
            shrink = jnp.exp(old - new)
            top_ref[i, h] = new
            sum_ref[i, h] = sum_ref[i, h] * shrink + jnp.sum(probs, axis=0, keepdims=True)
            o_ref[i, head, :] = o_ref[i, head, :] * shrink + mm(
                vt_ref[kb, head, :], probs.astype(BF16)
            )

    def attend(n):
        b, lv, j = event(n)
        first = jnp.logical_and(j == 0, lax.rem(lv, sub) == lax.rem(z, sub))
        known = jnp.where(n < 2, 1, jnp.minimum((n - 2) // 4 + 2, levels))

        def pair(u, carry):
            near = u < known
            seen = level(jnp.minimum(u, known - 1))
            old = event(jnp.maximum(u - known, 0))[0]
            i = jnp.where(near, seen, lv) // sub
            kb = jnp.where(near, b, old)
            query = i * members + m
            mine = jnp.where(near, lax.rem(seen, sub) == lax.rem(z, sub), old < b)
            pl.when(jnp.logical_and(mine, kb <= query))(lambda: unit(i, kb))
            return carry

        lax.fori_loop(0, known + jnp.where(first, n, 0), pair, 0)

    top_ref[...] = jnp.full(top_ref.shape, -jnp.inf, F32)
    sum_ref[...] = jnp.zeros(sum_ref.shape, F32)
    o_ref[...] = jnp.zeros(o_ref.shape, F32)
    lag = 4
    turn_on = ring - 5

    def advance(n, carry):
        pl.when(n < ring)(lambda: arrive(n))

        @pl.when(n == turn_on)
        def _():
            for at in range(len(pieces)):
                if pieces[at][4]:
                    relay(at)

        pl.when(n >= lag)(lambda: attend(n - lag))
        return carry

    lax.fori_loop(0, ring + lag, advance, 0)
    saves = [
        pltpu.make_async_copy(src, dst, osem.at[n])
        for n, (src, dst) in enumerate(
            ((k_ref, k_out), (kt_ref, kt_out), (vt_ref, vt_out), (q_ref, q_out), (o_ref, o_out))
        )
    ]
    saves += [
        pltpu.make_async_copy(xa_ref.at[i * members + m], xr_out.at[i], osem.at[5 + i])
        for i in range(GROUPS)
    ]
    for save in saves[:3] + saves[5:]:
        save.start()

    def give(i):
        return remote(low_ref.at[i], att_ref.at[g], asend.at[i], arecv.at[g], i * members + m, s)

    for i in range(GROUPS):
        for h in range(PER):
            head = pl.ds(h * HEAD_DIM, HEAD_DIM)
            out = o_ref[i, head, :] / sum_ref[i, h]
            o_ref[i, head, :] = out
            low_ref[i, head, :] = out.astype(BF16)
            lse_ref[i, h] = top_ref[i, h] + jnp.log(sum_ref[i, h])

        @pl.when(g == i)
        def _():
            att_ref[g] = low_ref[i]

        pl.when(g != i)(lambda: give(i).start())
    for save in saves[3:5]:
        save.start()
    for at in range(1, len(pieces)):
        if pieces[at][4]:
            relay_far(at)
        else:
            relay(at)
    for d in range(1, GROUPS):
        p = lax.rem(g + d, GROUPS)
        remote(low_ref.at[0], att_ref.at[p], asend.at[0], arecv.at[p], r, s).wait_recv()
    for at in range(1, len(pieces)):
        relayed(at)
    for i in range(GROUPS):
        pl.when(g != i)(lambda: give(i).wait_send())

    def sent(e, carry):
        b, lv, j = event(e)

        for u in range(halves):

            @pl.when(j == 0)
            def _():
                pl.when(jnp.logical_and(lv <= z, above))(lambda: move(b, 0, u).wait_send())
                pl.when(jnp.logical_and(lv >= z, below))(lambda: move(b, 1, u).wait_send())
                move(b, 2, u).wait_send()

            pl.when(j < 2)(lambda: move(b, 3, u).wait_send())
        return carry

    lax.fori_loop(0, ring, sent, 0)
    for copy in lists:
        copy.wait_send()
    for at in range(len(pieces)):
        for d in range(shards - 1):
            across(at, d).wait_send()
            shifted(at, d, 0, y, c, sib).wait_send()
            if pieces[at][4]:
                shifted(at, d, 1, y, c, yn).wait_send()
                shifted(at, d, 2, 1 - y, c, sib).wait_send()
    for save in saves:
        save.wait()


def forward_all(x, qkv_weight, docs, vectors, weights, parts, ring, shards, ident):
    shape = jax.ShapeDtypeStruct
    dma = pltpu.SemaphoreType.DMA
    vmem = pltpu.VMEM
    n = 1 + sum(part[1] for part in parts)
    width = x.shape[1]
    sizes = [v.shape[0] for v in vectors]
    per = max(shards - 1, 1)
    o = (GROUPS, SLAB, BLOCK)
    q = (GROUPS, PER, 2 * HEAD_DIM, BLOCK)
    k = (PER, ring * BLOCK, 2 * HEAD_DIM)
    t = (ring, SLAB, BLOCK)
    return pl.pallas_call(
        lambda *refs: forward_kernel(ring, shards, parts, sizes, *refs),
        out_shape=(
            shape(o, BF16), shape((shards, 1, sum(sizes)), F32), shape((3 * SLAB, width), BF16),
            shape((GROUPS, PER, 1, BLOCK), F32), shape(o, F32), shape(q, BF16), shape(k, BF16),
            shape(t, BF16), shape(t, BF16), shape((GROUPS,) + x.shape, BF16),
        )
        + tuple(shape((shards,) + w.shape, w.dtype) for w in weights),
        in_specs=[VMEM_SPEC] * (3 + len(vectors)) + [ANY_SPEC] * 3,
        out_specs=(VMEM_SPEC,) * 4 + (ANY_SPEC,) * 9,
        scratch_shapes=[
            vmem((ring,) + x.shape, BF16), vmem((shards, width // shards, 3 * SLAB), BF16),
            vmem(o, BF16), vmem((2 * SLAB, 1), F32), vmem(o, F32), vmem(q, BF16), vmem(k, BF16),
            vmem(t, BF16), vmem(t, BF16),
            vmem((GROUPS, PER, 1, BLOCK), F32), vmem((GROUPS, PER, 1, BLOCK), F32),
            dma((4, ring, 2)), dma((ring, 2)), dma((n, per)), dma((n, per)), dma((n, per, 3)),
            dma((n, per, 3)), dma((per,)), dma((per,)),
            dma((GROUPS,)), dma((GROUPS,)), dma((5 + GROUPS,)),
        ],
        compiler_params=pltpu.CompilerParams(
            collective_id=ident, has_side_effects=True, vmem_limit_bytes=VMEM_LIMIT
        ),
    )(x, qkv_weight, docs, *vectors, *weights)


def layer_norm(hidden, gain, shift):
    centre = hidden - jnp.mean(hidden, axis=-1, keepdims=True)
    inverse = lax.rsqrt(jnp.mean(centre * centre, axis=-1, keepdims=True) + EPSILON)
    normed = centre * inverse
    return (normed * gain + shift, normed, inverse)


def norm_back(grad_output, normed, inverse, gain):
    grad_normed = grad_output * gain
    centred = grad_normed - jnp.mean(grad_normed, axis=-1, keepdims=True)
    return inverse * (centred - normed * jnp.mean(grad_normed * normed, axis=-1, keepdims=True))


def mlp_kernel(
    shards, sizes, att_ref, x_ref, og_ref, flat_ref, *refs,
):
    own, full = refs[:3], refs[3:6]
    out_ref, gat_ref, mid_ref, small_ref, down_out, up_out, outw_out = refs[6:13]
    wo_ref, wu_ref, wd_ref, act_ref, slope_ref, gd_ref, gu_ref, go_ref, lsem, ssem = refs[13:]
    s = lax.axis_index("shard")
    width = x_ref.shape[1]
    hidden = wu_ref.shape[1]
    loads = []
    for w, ref in enumerate((wo_ref, wu_ref, wd_ref)):
        size = own[w].shape[0]
        group = []
        for d in range(shards):
            t = lax.rem(s + d, shards)
            rows = pl.ds(pl.multiple_of(t * size, size), size)
            src = own[w] if d == 0 else full[w].at[t]
            group.append(pltpu.make_async_copy(src, ref.at[rows], lsem.at[w * shards + d]))
        loads.append(group)
        for load in group:
            load.start()

    def ready(w):
        for load in loads[w]:
            load.wait()

    starts = [sum(sizes[:n]) for n in range(len(sizes))]

    def vector(n):
        return jnp.concatenate(
            [flat_ref[t, :, starts[n] : starts[n] + sizes[n]] for t in range(shards)], axis=1
        )

    def put(n, row):
        for t in range(shards):
            small_ref[t, :, starts[n] : starts[n] + sizes[n]] = row[
                :, t * sizes[n] : (t + 1) * sizes[n]
            ]

    small_ref[...] = jnp.zeros(small_ref.shape, F32)
    att = att_ref[...].reshape(width, BLOCK)
    ready(0)
    branch = mm(att, wo_ref[...], TN) + vector(1)
    gain_mid = vector(2)
    mid_out, mid_norm, mid_inv = layer_norm(x_ref[...].astype(F32) + branch, gain_mid, vector(3))
    mid_low = mid_out.astype(BF16)
    up_bias = vector(4)
    cols = 512
    ready(1)
    for at in range(0, hidden, cols):
        block = slice(at, at + cols)
        pre = mm(mid_low, wu_ref[:, block]) + up_bias[:, block]
        phi = 0.5 * (1.0 + lax.erf(pre * 0.7071067811865476))
        act_ref[:, block] = (pre * phi).astype(BF16)
        slope_ref[:, block] = phi + pre * jnp.exp(-0.5 * pre * pre) * 0.3989422804014327
    ready(2)
    ffn = mm(act_ref[...], wd_ref[...]) + vector(5)
    gain_end = vector(6)
    end_out, end_norm, end_inv = layer_norm(mid_out + ffn, gain_end, vector(7))
    out_ref[...] = end_out.astype(BF16)
    top = og_ref[...].astype(F32)

    def column(value):
        return jnp.sum(value, axis=0, keepdims=True)

    put(6, column(top * end_norm))
    put(7, column(top))
    grad_end_in = norm_back(top, end_norm, end_inv, gain_end)
    grad_ffn = grad_end_in.astype(BF16)
    put(5, column(grad_ffn.astype(F32)))
    saves = []

    def save(src, dst):
        copy = pltpu.make_async_copy(src, dst, ssem.at[len(saves)])
        copy.start()
        saves.append(copy)

    chunks = gd_ref.shape[1]
    rows = hidden // shards // chunks
    for t in range(shards):
        for k in range(chunks):
            at = t * (hidden // shards) + k * rows
            value = mm(act_ref[:, at : at + rows], grad_ffn, TN)
            gd_ref[t, k] = value.astype(BF16).reshape(gd_ref.shape[2:])
        save(gd_ref.at[t], down_out.at[t])
    grad_mid_out = grad_end_in
    ups = []
    wide = hidden // gu_ref.shape[0]
    for k in range(gu_ref.shape[0]):
        block = slice(k * wide, (k + 1) * wide)
        grad_act = mm(grad_ffn, wd_ref[block, :], NT)
        grad_pre = (grad_act * slope_ref[:, block]).astype(BF16)
        ups.append(column(grad_pre.astype(F32)))
        value = mm(mid_low, grad_pre, TN).astype(BF16)
        for half in range(2):
            gu_ref[k, half] = value[:, half * (wide // 2) : (half + 1) * (wide // 2)].reshape(
                gu_ref.shape[2:]
            )
        save(gu_ref.at[k], up_out.at[k])
        grad_mid_out = grad_mid_out + mm(grad_pre, wu_ref[:, block], NT)
    put(4, jnp.concatenate(ups, axis=1))
    put(2, column(grad_mid_out * mid_norm))
    put(3, column(grad_mid_out))
    grad_mid_in = norm_back(grad_mid_out, mid_norm, mid_inv, gain_mid)
    mid_ref[...] = grad_mid_in
    grad_branch = grad_mid_in.astype(BF16)
    put(1, column(grad_branch.astype(F32)))
    gat_ref[...] = mm(wo_ref[...], grad_branch, NT).astype(BF16).reshape(gat_ref.shape)
    value = mm(att, grad_branch).astype(BF16)
    for half in range(2):
        go_ref[0, half] = value[:, half * (width // 2) : (half + 1) * (width // 2)].reshape(
            go_ref.shape[2:]
        )
    save(go_ref, outw_out)
    for copy in saves:
        copy.wait()


def mlp_all(att, x, out_grad, flat, own, full, sizes, shards, levels, down_chunks, up_chunks):
    shape = jax.ShapeDtypeStruct
    dma = pltpu.SemaphoreType.DMA
    vmem = pltpu.VMEM
    width, hidden = own[0].shape[1], own[1].shape[1]
    gd = (shards, down_chunks, 2, 2, levels, hidden // shards // down_chunks // 4 // levels, width)
    gu = (up_chunks, 2, shards, 2, levels, width // shards // 2 // levels, hidden // up_chunks // 2)
    go = (1, 2, shards, 2, levels, width // shards // 2 // levels, width // 2)
    return pl.pallas_call(
        lambda *refs: mlp_kernel(shards, sizes, *refs),
        out_shape=(
            shape((BLOCK, width), BF16), shape((GROUPS, SLAB, BLOCK), BF16),
            shape((BLOCK, width), F32), shape(flat.shape, F32),
            shape(gd, BF16), shape(gu, BF16), shape(go, BF16),
        ),
        in_specs=[VMEM_SPEC] * 4 + [ANY_SPEC] * 6,
        out_specs=(VMEM_SPEC,) * 4 + (ANY_SPEC,) * 3,
        scratch_shapes=[
            vmem((width, width), BF16), vmem((width, hidden), BF16), vmem((hidden, width), BF16),
            vmem((BLOCK, hidden), BF16), vmem((BLOCK, hidden), F32),
            vmem(gd, BF16), vmem(gu, BF16), vmem(go, BF16),
            dma((3 * shards,)), dma((shards + up_chunks + 1,)),
        ],
        compiler_params=pltpu.CompilerParams(vmem_limit_bytes=VMEM_LIMIT),
    )(att, x, out_grad, flat, *own, *full)


def add_rows(out, terms):
    total = terms[0][...].astype(F32)
    for term in terms[1:]:
        total = total + term[...].astype(F32)
    out[...] = total.astype(out.dtype)


def reduce_steps(net, slab, out, own, near, side, mate, tall, sems, group):
    asend, arecv, bsend, brecv, csend, crecv, dsend, drecv, esend, erecv, fsend, frecv, gsend, grecv, lsem = sems
    r, s, z, y, c = net.r, net.s, net.z, net.y, net.c
    base = z // group * group
    zz = lax.rem(z, group)
    inner = [lax.rem(zz + d, group) for d in range(1, group)]
    near_copy = lambda: remote(slab(1 - c), near, asend, arecv, net.sib, s)
    own_copy = lambda: pltpu.make_async_copy(slab(c), own, lsem)
    across = lambda d: remote(
        near.at[net.others[d]], side.at[d], bsend.at[d], brecv.at[d], r, net.others[d]
    )
    over = lambda: remote(near.at[s, 1 - y], mate, csend, crecv, net.yn, s)
    along = lambda d: remote(
        near.at[s, y, inner[d]], tall.at[d], dsend.at[d], drecv.at[d],
        (base + inner[d]) * 4 + net.line, s,
    )
    one, four = out
    mine = one(c, y, z)
    levels = net.levels

    def climb(k, up):
        at = z - k if up else z + k
        piece = one(c, y, at)
        target = (z + 1 if up else z - 1) * 4 + net.line
        return remote(piece, piece, esend.at[int(up), k], erecv.at[int(up), k], target, s)

    def landed(k, up):
        at = z - k if up else z + k
        piece = one(c, y, at)
        return remote(piece, piece, esend.at[int(up), k], erecv.at[int(up), k - 1], net.r, s)

    def both_ways(k, act):
        here = (z - k >= 0, z + k < levels)
        more = (z + 1 < levels, z > 0)
        pl.when(jnp.logical_and(here[0], more[0]))(lambda: act(True))
        pl.when(jnp.logical_and(here[1], more[1]))(lambda: act(False))

    def wait_from(k):
        pl.when(z - k >= 0)(lambda: landed(k, True).wait_recv())
        pl.when(z + k < levels)(lambda: landed(k, False).wait_recv())


    def pair(at):
        return remote(one(c, y, at), one(c, y, at), fsend.at[at], frecv.at[at], net.yn, s)

    def pair_from(k):
        if k:
            pl.when(z - k >= 0)(lambda: pair(z - k).start())
            pl.when(z + k < levels)(lambda: pair(z + k).start())
        else:
            pair(z).start()

    last = lambda: remote(four(c), four(c), gsend, grecv, net.sib, s)
    n_side, n_inner = len(net.others), len(inner)

    def step0():
        near_copy().start()
        own_copy().start()

    def step1():
        near_copy().wait_recv()
        own_copy().wait()
        for t in range(net.shards):
            for half in range(2):
                add_rows(near.at[t, half], [own.at[t, half], near.at[t, half]])
        for d in range(n_side):
            across(d).start()

    def step2():
        for d in range(n_side):
            across(d).wait_recv()
        for half in range(2):
            add_rows(
                near.at[s, half], [near.at[s, half]] + [side.at[d, half] for d in range(n_side)]
            )
        over().start()

    def step3():
        over().wait_recv()
        add_rows(near.at[s, y], [near.at[s, y], mate])
        for d in range(n_inner):
            along(d).start()

    def step4():
        for d in range(n_inner):
            along(d).wait_recv()
        add_rows(mine, [near.at[s, y, zz]] + [tall.at[d] for d in range(n_inner)])
        both_ways(0, lambda up: climb(0, up).start())
        pair_from(0)

    def onward(k):
        def step():
            wait_from(k)
            both_ways(k, lambda up: climb(k, up).start())
            pair_from(k)

        return step

    def step5():
        wait_from(levels - 1)
        pair_from(levels - 1)

    def step6():
        for at in range(levels):
            piece = one(c, 1 - y, at)
            remote(piece, piece, fsend.at[at], frecv.at[at], net.yn, s).wait_recv()
        last().start()

    def step7():
        last().wait_recv()

    def drain():
        near_copy().wait_send()
        for d in range(n_side):
            across(d).wait_send()
        over().wait_send()
        for d in range(n_inner):
            along(d).wait_send()
        for k in range(levels - 1):
            both_ways(k, lambda up: climb(k, up).wait_send())
        for at in range(levels):
            pair(at).wait_send()
        last().wait_send()

    middle = [onward(k) for k in range(1, levels - 1)]
    return [step0, step1, step2, step3, step4, *middle, step5, step6, step7], drain


def reduce_scratch(shards, levels, group, rows, cols):
    dma = pltpu.SemaphoreType.DMA
    vmem = pltpu.VMEM
    many = lambda n: dma((max(n, 1),))
    buffers = [
        vmem((shards, 2, group, rows, cols), BF16),
        vmem((shards, 2, group, rows, cols), BF16),
        vmem((max(shards - 1, 1), 2, group, rows, cols), BF16),
        vmem((group, rows, cols), BF16),
        vmem((max(group - 1, 1), rows, cols), BF16),
    ]
    sems = [
        dma(()), dma(()), many(shards - 1), many(shards - 1), dma(()), dma(()),
        many(group - 1), many(group - 1), dma((2, levels)), dma((2, levels)),
        dma((levels,)), dma((levels,)), dma(()), dma(()), dma(()),
    ]
    return buffers + sems


SCRATCH = 20


def small_steps(net, src, out, near, side, mate, tall, sems):
    asend, arecv, bsend, brecv, csend, crecv, dsend, drecv = sems
    r, s, z, y, c = net.r, net.s, net.z, net.y, net.c
    near_copy = lambda: remote(src, near.at[1], asend, arecv, net.sib, s)
    across = lambda d: remote(
        near.at[0, net.others[d]], side.at[s], bsend.at[d], brecv.at[d], r, net.others[d]
    )
    over = lambda: remote(mate.at[0], mate.at[1], csend, crecv, net.yn, s)
    along = lambda d: remote(
        tall.at[z], tall.at[z], dsend.at[d], drecv.at[d], net.heights[d] * 4 + net.line, s
    )

    def step0():
        near_copy().start()

    def step1():
        near_copy().wait_recv()
        near[0] = src[...] + near[1]
        side[s] = near[0, s]
        for d in range(len(net.others)):
            across(d).start()

    def step2():
        for d in range(len(net.others)):
            across(d).wait_recv()
        total = side[0]
        for t in range(1, net.shards):
            total = total + side[t]
        mate[0] = total
        over().start()

    def step3():
        over().wait_recv()
        tall[z] = mate[0] + mate[1]
        for d in range(len(net.heights)):
            along(d).start()

    def step4():
        for d in range(len(net.heights)):
            along(d).wait_recv()
        total = tall[0]
        for t in range(1, net.levels):
            total = total + tall[t]
        out[...] = total

    def drain():
        near_copy().wait_send()
        for d in range(len(net.others)):
            across(d).wait_send()
        over().wait_send()
        for d in range(len(net.heights)):
            along(d).wait_send()

    return [step0, step1, step2, step3, step4], drain


def small_scratch(shards, levels, rows):
    dma = pltpu.SemaphoreType.DMA
    vmem = pltpu.VMEM
    return [
        vmem((2, shards, 1, rows), F32), vmem((shards, 1, rows), F32),
        vmem((2, 1, rows), F32), vmem((levels, 1, rows), F32),
        dma(()), dma(()), dma((max(shards - 1, 1),)), dma((max(shards - 1, 1),)),
        dma(()), dma(()), dma((levels - 1,)), dma((levels - 1,)),
    ]


def places(ref, chunk, core_first, levels, rows, cols):
    if len(ref.shape) != 2:
        return (
            lambda c, y, z: ref.at[chunk, c, y, z], lambda c: ref.at[chunk, c],
        )
    if core_first:

        def view(c, at, size):
            lanes = pl.ds(pl.multiple_of((chunk * 2 + c) * cols, cols), cols)
            return ref.at[pl.ds(pl.multiple_of(at, rows), size), lanes]

        return (
            lambda c, y, z: view(c, (y * levels + z) * rows, rows),
            lambda c: view(c, 0, 2 * levels * rows),
        )

    def span(at, count):
        first = (chunk * 4 * levels + at) * rows
        return ref.at[pl.ds(pl.multiple_of(first, rows), count * rows)]

    return (
        lambda c, y, z: span((c * 2 + y) * levels + z, 1),
        lambda c: span(c * 2 * levels, 2 * levels),
    )


def spread_out(jobs, offsets):
    ticks = {}
    for n, steps in enumerate(jobs):
        for t, step in enumerate(steps):
            ticks.setdefault(n + offsets[t], []).append(step)
    return [ticks.get(t, []) for t in range(max(ticks, default=-1) + 1)]


def term_jobs(net, specs, chunk_shapes, terms, outs, rest):
    jobs, drains = [], []
    for number, (which, k, core_first) in enumerate(specs):
        scratch = rest[number * SCRATCH : (number + 1) * SCRATCH]
        ref = terms[which]
        if core_first:
            slab = lambda core, ref=ref, k=k: ref.at[k, core]
        else:
            slab = lambda core, ref=ref, k=k: ref.at[:, k, core]
        spot = places(outs[which], k, core_first, net.levels, *chunk_shapes[which])
        steps, drain = reduce_steps(net, slab, spot, *scratch[:5], scratch[5:], net.levels)
        jobs.append(steps)
        drains.append(drain)
    return jobs, drains, rest[len(specs) * SCRATCH :]


def sums_kernel(ring, shards, specs, chunk_shapes, *refs):
    n = len(chunk_shapes)
    net = Links(ring, shards)
    hello(net.partners())
    jobs, drains, _ = term_jobs(net, specs, chunk_shapes, refs[:n], refs[n : 2 * n], refs[2 * n :])
    for steps in spread_out(jobs, offsets(net.levels)):
        for step in steps:
            step()
    for drain in drains:
        drain()


def tail_kernel(ring, shards, specs, chunk_shapes, n0, *refs):
    (
        go_ref, lse_ref, w_ref, mid_ref, small_ref, q_in, k_in, kt_in, vt_in, o_in, xr_in,
    ) = refs[:11]
    n_terms = len(chunk_shapes)
    terms, refs = refs[11 : 11 + n_terms], refs[11 + n_terms :]
    out_ref, outs, (qkv_ref, total_small) = refs[0], refs[1 : 1 + n_terms], refs[1 + n_terms : 3 + n_terms]
    (
        q_ref, k_ref, kt_ref, vt_ref, o_ref,
        g_ref, x_ref, v_ref, delta_ref, acc_ref, dk_ref, dv_ref, pq_ref, stage_ref, got_ref, got2_ref,
        dw_ref, dx_ref, near_ref, far_ref, db_ref, dwl_ref, row_ref, sum_ref, all_ref,
        gsend, grecv, ksend, krecv, xsend, xrecv, lsem,
    ) = refs[3 + n_terms : 35 + n_terms]
    finals, rest = outs, refs[35 + n_terms :]
    outs, rest = rest[:n_terms], rest[n_terms:]
    copies = [
        pltpu.make_async_copy(src, dst, lsem.at[6 + n])
        for n, (src, dst) in enumerate(zip(outs, finals))
    ]
    net = Links(ring, shards)
    r, s = net.r, net.s
    levels, members = net.levels, ring // GROUPS
    sub = levels // GROUPS
    g, m = r // members, lax.rem(r, members)
    peers = [lax.rem(g + d, GROUPS) for d in range(1, GROUPS)]
    mates = [lax.rem(m + d, members) for d in range(1, members)]
    partners = net.partners()
    if levels != GROUPS:
        partners = partners + [(p * members + m, s, True) for p in peers]
        partners = partners + [(g * members + t, s, True) for t in mates]
    else:
        partners = partners + [(g * members + 3 - m, s, True)]
    hello(partners)

    def give(p):
        return remote(go_ref.at[p], g_ref.at[g], gsend.at[p], grecv.at[g], p * members + m, s)

    def take(p):
        return remote(go_ref.at[p], g_ref.at[p], gsend.at[p], grecv.at[p], p * members + m, s)

    for p in peers:
        give(p).start()
    loads = [
        pltpu.make_async_copy(src, dst, lsem.at[n])
        for n, (src, dst) in enumerate(
            ((vt_in, vt_ref), (k_in, k_ref), (q_in, q_ref), (kt_in, kt_ref), (o_in, o_ref),
             (xr_in, x_ref))
        )
    ]
    for load in loads:
        load.start()
    g_ref[g] = go_ref[g]

    jobs, drains, rest = term_jobs(net, specs, chunk_shapes, terms, outs, rest)
    qkv_jobs = []
    for k in range(QKV_CHUNKS):
        steps, drain = reduce_steps(
            net, lambda core, k=k: dwl_ref.at[:, k, core], places(all_ref, k, False, levels, 0, 0),
            *rest[:5], rest[5:SCRATCH], sub
        )
        qkv_jobs.append(steps)
        drains.append(drain)
        rest = rest[SCRATCH:]
    vec_steps, drain = small_steps(net, sum_ref, total_small, *rest[:4], rest[4:])
    drains.append(drain)
    ticks = spread_out(jobs, offsets(levels))

    width = w_ref.shape[1]

    def prepare():
        dwl_ref[...] = dw_ref[...].astype(BF16).reshape(dwl_ref.shape)
        row = jnp.broadcast_to(db_ref[...], (3 * SLAB, 8)).T[:1]
        row_ref[...] = jnp.zeros(row_ref.shape, F32)
        for k in range(GROUPS):

            @pl.when(g == k)
            def _():
                row_ref[:, k * SLAB : (k + 1) * SLAB] = row[:, :SLAB]
                row_ref[:, width + k * SLAB : width + (k + 1) * SLAB] = row[:, 2 * SLAB :]

        sum_ref[...] = small_ref[...]
        for t in range(shards):
            sum_ref[t, :, :n0] = row_ref[:, t * n0 : (t + 1) * n0]

    ready = -(-(10 * members + 2 + SHIFTS[0] + 1) // PACE)
    ticks.append([copy.start for copy in copies])
    late = [[list(steps) for steps in zip(*qkv_jobs)], [[step] for step in vec_steps]]
    ticks += [[] for _ in range(ready + max(map(len, late)) - len(ticks))]
    ticks[ready].append(prepare)
    for series in late:
        for t, steps in enumerate(series):
            ticks[ready + t] += steps

    def tick(t, lo, hi):
        if hi - lo == 1:
            for step in ticks[lo]:
                step()
        else:
            mid = (lo + hi) // 2
            pl.when(t < mid)(lambda: tick(t, lo, mid))
            pl.when(t >= mid)(lambda: tick(t, mid, hi))

    for load in loads[:1]:
        load.wait()

    def turn(b, carry):
        rows = pl.ds(pl.multiple_of(b * BLOCK, BLOCK), BLOCK)
        for h in range(PER):
            v_ref[h, rows, :] = (
                vt_ref[b, h * HEAD_DIM : (h + 1) * HEAD_DIM, :].astype(F32).T.astype(BF16)
            )
        dk_ref[b] = jnp.zeros((SLAB, BLOCK), F32)
        dv_ref[b] = jnp.zeros((SLAB, BLOCK), F32)
        return carry

    lax.fori_loop(0, ring, turn, 0)
    dw_ref[...] = jnp.zeros(dw_ref.shape, F32)
    db_ref[...] = jnp.zeros(db_ref.shape, F32)
    for load in loads[1:]:
        load.wait()

    pairs = members // 2
    c, mt = net.c, m // 2
    fellows = [lax.rem(mt + d, pairs) for d in range(1, pairs)]
    pieces = 4
    size = BLOCK // pieces

    def cross():
        return lambda j: remote(
            stage_ref.at[j], got_ref.at[j], ksend.at[j, 0], krecv.at[j, 0], net.sib, s
        )

    to_core = cross()

    def share(j, d):
        t = fellows[d]
        return remote(
            got_ref.at[j, t], got2_ref.at[j, d], ksend.at[j, d + 1], krecv.at[j, d + 1],
            g * members + t * 2 + c, s,
        )

    def hop(j, u, side, target):
        rows = pl.ds(u * size, size)
        return remote(
            dx_ref.at[j, rows], far_ref.at[j, side, rows], xsend.at[j, u], xrecv.at[j, side, u],
            target, s,
        )

    def pass_dx(j, u):
        down = lambda: hop(j, u, 0, r - members)
        up = lambda: hop(j, u, 1, r + members)
        return down, up

    def begin(i):
        pl.when(g != i)(lambda: take(i).wait_recv())
        for h in range(PER):
            head = pl.ds(h * HEAD_DIM, HEAD_DIM)
            delta_ref[h] = jnp.sum(
                g_ref[i, head, :].astype(F32) * o_ref[i, head, :], axis=0, keepdims=True
            )
        acc_ref[...] = jnp.zeros(acc_ref.shape, F32)

    def unit(i, kb):
        keys = pl.ds(pl.multiple_of(kb * BLOCK, BLOCK), BLOCK)
        for h in range(PER):
            head = pl.ds(h * HEAD_DIM, HEAD_DIM)
            score = mm(k_ref[h, keys, :], q_ref[i, h])
            probs = jnp.exp(score - lse_ref[i, h])
            grad = g_ref[i, head, :]
            moved = (probs * (mm(v_ref[h, keys, :], grad) - delta_ref[h])).astype(BF16)
            acc_ref[h] += mm(kt_ref[kb, head, :], moved)
            dk_ref[kb, head, :] += mm(q_ref[i, h, :HEAD_DIM, :], moved, NT)
            dv_ref[kb, head, :] += mm(grad, probs.astype(BF16), NT)

    def end(i):
        for h in range(PER):
            pq_ref[i, pl.ds(h * HEAD_DIM, HEAD_DIM), :] = (
                acc_ref[h] * HEAD_DIM ** (-0.5)
            ).astype(BF16)
        for t in range(pairs):
            b = i * members + t * 2 + 1 - c
            stage_ref[i, t, :SLAB, :] = dk_ref[b].astype(BF16)
            stage_ref[i, t, SLAB:, :] = dv_ref[b].astype(BF16)
        to_core(i).start()

    def merge(j):
        to_core(j).wait_recv()
        for d, t in enumerate(fellows):
            b = j * members + t * 2 + c
            for half, ref in enumerate((dk_ref, dv_ref)):
                rows = pl.ds(half * SLAB, SLAB)
                got_ref[j, t, rows, :] = (ref[b] + got_ref[j, t, rows, :].astype(F32)).astype(BF16)
            share(j, d).start()

    def finish(j):
        b = j * members + m
        dk = dk_ref[b] + got_ref[j, mt, :SLAB, :].astype(F32)
        dv = dv_ref[b] + got_ref[j, mt, SLAB:, :].astype(F32)
        for d in range(pairs - 1):
            share(j, d).wait_recv()
            dk = dk + got2_ref[j, d, :SLAB, :].astype(F32)
            dv = dv + got2_ref[j, d, SLAB:, :].astype(F32)
        proj = jnp.concatenate([pq_ref[j], dk.astype(BF16), dv.astype(BF16)], axis=0)
        db_ref[...] += jnp.sum(proj.astype(F32), axis=1, keepdims=True)
        dx = mm(proj, w_ref[...], TN)
        near_ref[j] = dx
        dx_ref[j] = dx.astype(BF16)
        start_dx(j, 0)
        dw_ref[...] += mm(x_ref[j], proj.T, TN)

    def start_dx(j, depth):
        from_below = jnp.logical_and(g < j, g == depth)
        from_above = jnp.logical_and(g > j, GROUPS - 1 - g == depth)
        for u in range(pieces):
            rows = pl.ds(u * size, size)
            down, up = pass_dx(j, u)

            @pl.when(from_below)
            def _():
                if depth:
                    hop(j, u, 1, r).wait_recv()
                    dx_ref[j, rows] = (near_ref[j, rows] + far_ref[j, 1, rows].astype(F32)).astype(BF16)
                up().start()

            @pl.when(from_above)
            def _():
                if depth:
                    hop(j, u, 0, r).wait_recv()
                    dx_ref[j, rows] = (near_ref[j, rows] + far_ref[j, 0, rows].astype(F32)).astype(BF16)
                down().start()

    def own_dx():
        for side, there in ((0, g < GROUPS - 1), (1, g > 0)):

            @pl.when(there)
            def _():
                for u in range(pieces):
                    hop(g, u, side, r).wait_recv()
                near_ref[g] += far_ref[g, side].astype(F32)

    sizes = [i * members + m + 1 for i in range(GROUPS)][::-1]
    ends = [sum(sizes[: n + 1]) for n in range(GROUPS)]
    units = ends[-1]
    finishes = [members * n + 2 for n in (4, 7, 9, 10)]

    def advance(it, carry):
        past = [(it >= e).astype(jnp.int32) for e in ends]
        i = GROUPS - 1 - past[0] - past[1] - past[2]
        first = jnp.where(i == 3, 0, jnp.where(i == 2, ends[0], jnp.where(i == 1, ends[1], ends[2])))
        kb = it - first

        t = it // PACE
        if ticks:
            pl.when(jnp.logical_and(lax.rem(it, PACE) == 0, t < len(ticks)))(
                lambda: tick(t, 0, len(ticks))
            )

        @pl.when(it < units)
        def _():
            pl.when(kb == 0)(lambda: begin(i))
            unit(i, kb)

            @pl.when(kb == i * members + m)
            def _():
                end(i)

        def at_times(shift, act):
            n_due = sum((it - shift >= at).astype(jnp.int32) for at in finishes)
            n_done = sum((it - shift > at).astype(jnp.int32) for at in finishes)
            pl.when(n_due > n_done)(lambda: act(GROUPS - n_due))

        at_times(0, merge)
        at_times(SHIFTS[0], finish)
        for depth in range(1, GROUPS - 1):
            at_times(SHIFTS[depth], lambda j, depth=depth: start_dx(j, depth))
        return carry

    lax.fori_loop(0, PACE * len(ticks), advance, 0)

    for copy in copies:
        copy.wait()
    own_dx()
    out_ref[...] = (near_ref[g] + mid_ref[...]).astype(BF16)
    if len(qkv_ref.shape) == 2:
        rows = all_ref.shape[-2]
        for part in range(4 * QKV_CHUNKS):
            for z in range(levels):
                at = (part * sub + z % sub) * rows
                piece = all_ref[part // 4, part // 2 % 2, part % 2, z]
                for t in range(3):
                    lane = t * width + z // sub * SLAB
                    qkv_ref[at : at + rows, lane : lane + SLAB] = piece[
                        :, t * SLAB : (t + 1) * SLAB
                    ]
    else:
        qkv_ref[...] = all_ref[...]
    for p in peers:
        give(p).wait_send()
    for j in range(GROUPS):
        to_core(j).wait_send()
        for d in range(pairs - 1):
            share(j, d).wait_send()
        for u in range(pieces):
            pl.when(g != j)(lambda: hop(j, u, 0, r).wait_send())
    for drain in drains:
        drain()


PACE = 2
QKV_CHUNKS = 3


def offsets(levels, gaps=(2, 2, 2, 2, 2, 2, 2, 2)):
    steps = gaps[:4] + gaps[4:5] * (levels - 2) + gaps[5:]
    return [sum(steps[:t]) for t in range(len(steps) + 1)]


SHIFTS = (2, 5, 7)


def tail_all(gat, lse, w_group, mid, small, saved, terms, n0, ring, shards, ident):
    members, levels = ring // GROUPS, ring // 4
    sub = levels // GROUPS
    width = mid.shape[1]
    part = width // shards
    shape = jax.ShapeDtypeStruct
    dma = pltpu.SemaphoreType.DMA
    vmem = pltpu.VMEM
    specs, scratch, out_shape, chunk_shapes = [], [], [], []
    for i, term in enumerate(terms):
        core_first = i > 0
        chunks = term.shape[0] if core_first else term.shape[1]
        rows, cols = term.shape[-2:]
        chunk_shapes.append((rows, cols))
        if rows % 16:
            out_shape.append(shape((chunks, 2, 2, levels, rows, cols), BF16))
        elif core_first:
            out_shape.append(shape((2 * levels * rows, chunks * 2 * cols), BF16))
        else:
            out_shape.append(shape((chunks * 4 * levels * rows, cols), BF16))
        for k in range(chunks):
            specs.append((i, k, core_first))
            scratch += reduce_scratch(shards, levels, levels, rows, cols)
    term_scratch, term_shapes = scratch, out_shape
    apart = ring * BLOCK > 4096
    if apart:
        sums = pl.pallas_call(
            lambda *refs: sums_kernel(ring, shards, specs, chunk_shapes, *refs),
            out_shape=tuple(term_shapes),
            in_specs=[ANY_SPEC] * 3,
            out_specs=(VMEM_SPEC,) * 3,
            scratch_shapes=term_scratch,
            compiler_params=pltpu.CompilerParams(
                collective_id=ident + 1, has_side_effects=True, vmem_limit_bytes=VMEM_LIMIT
            ),
        )(*terms)
    specs, chunk_shapes = ([], []) if apart else (specs, chunk_shapes)
    scratch = [] if apart else list(term_scratch)
    out_shape = [] if apart else list(term_shapes)
    terms = () if apart else terms
    rows = part // (4 * QKV_CHUNKS) // sub
    buffer = (QKV_CHUNKS, 2, 2, levels, rows, 3 * SLAB)
    for _ in range(QKV_CHUNKS):
        scratch += reduce_scratch(shards, levels, sub, rows, 3 * SLAB)
    scratch += small_scratch(shards, levels, small.shape[2])
    out_shape.append(shape(buffer if rows % 16 else (part, 3 * width), BF16))
    slab = (GROUPS, SLAB, BLOCK)
    tall = (ring, SLAB, BLOCK)
    result = pl.pallas_call(
        lambda *refs: tail_kernel(ring, shards, specs, chunk_shapes, n0, *refs),
        out_shape=(shape((BLOCK, width), BF16), *out_shape, shape((1, small.shape[2]), F32)),
        in_specs=[VMEM_SPEC] * 5 + [ANY_SPEC] * (6 + len(terms)),
        out_specs=(VMEM_SPEC,) + (ANY_SPEC,) * len(terms) + (VMEM_SPEC,) * 2,
        scratch_shapes=[
            vmem((GROUPS, PER, 2 * HEAD_DIM, BLOCK), BF16),
            vmem((PER, ring * BLOCK, 2 * HEAD_DIM), BF16),
            vmem(tall, BF16), vmem(tall, BF16), vmem(slab, F32),
            vmem(slab, BF16),
            vmem((GROUPS, BLOCK, width), BF16),
            vmem((PER, ring * BLOCK, HEAD_DIM), BF16),
            vmem((PER, 1, BLOCK), F32),
            vmem((PER, HEAD_DIM, BLOCK), F32),
            vmem(tall, F32), vmem(tall, F32), vmem(slab, BF16),
            vmem((GROUPS, members // 2, 2 * SLAB, BLOCK), BF16),
            vmem((GROUPS, members // 2, 2 * SLAB, BLOCK), BF16),
            vmem((GROUPS, members // 2 - 1, 2 * SLAB, BLOCK), BF16),
            vmem((width, 3 * SLAB), F32),
            vmem((GROUPS, BLOCK, width), BF16),
            vmem((GROUPS, BLOCK, width), F32),
            vmem((GROUPS, 2, BLOCK, width), BF16),
            vmem((3 * SLAB, 1), F32),
            vmem((shards, QKV_CHUNKS, 2, 2, sub, rows, 3 * SLAB), BF16),
            vmem((1, 2 * width), F32),
            vmem(small.shape, F32),
            vmem(buffer, BF16),
            dma((GROUPS,)), dma((GROUPS,)),
            dma((GROUPS, members // 2)), dma((GROUPS, members // 2)),
            dma((GROUPS, 4)), dma((GROUPS, 2, 4)), dma((9,)),
            *(vmem(o.shape, BF16) for o in out_shape[: len(terms)]),
            *scratch,
        ],
        compiler_params=pltpu.CompilerParams(
            collective_id=ident, has_side_effects=True, vmem_limit_bytes=VMEM_LIMIT
        ),
    )(gat, lse, w_group, mid, small, *saved, *terms)
    return (result[0], *sums, *result[1:]) if apart else result


def widen_kernel(sizes, cuts, flat_ref, *refs):
    n = len(cuts)
    sources, targets, vectors = refs[:n], refs[n : 2 * n], refs[2 * n : 2 * n + len(sizes)]
    low, wide, isem, osem = refs[-2 * n - 2 : -n - 2], refs[-n - 2 : -2], refs[-2], refs[-1]
    loads, saves = [], []
    for w, parts in enumerate(cuts):
        size = sources[w].shape[0] // parts
        for j in range(parts):
            rows = pl.ds(j * size, size)
            at = len(loads)
            loads.append(pltpu.make_async_copy(sources[w].at[rows], low[w].at[rows], isem.at[at]))
            saves.append(
                (w, rows, pltpu.make_async_copy(wide[w].at[rows], targets[w].at[rows], osem.at[at]))
            )
    for load in loads:
        load.start()
    at = 0
    for ref, size in zip(vectors, sizes):
        ref[...] = flat_ref[:, at : at + size].reshape(size)
        at += size
    for load, (w, rows, save) in zip(loads, saves):
        load.wait()
        wide[w][rows] = low[w][rows].astype(wide[w].dtype)
        save.start()
    for _, _, save in saves:
        save.wait()


def widen_all(flat, arrays, same, sizes):
    shape = jax.ShapeDtypeStruct
    arrays = (*arrays, same)
    types = [F32] * (len(arrays) - 1) + [same.dtype]
    dma = pltpu.SemaphoreType.DMA
    cuts = [next(n for n in (4, 3, 2, 1) if a.shape[0] % (16 * n) == 0 or n == 1) for a in arrays]
    return pl.pallas_call(
        lambda *refs: widen_kernel(sizes, cuts, *refs),
        out_shape=tuple(shape(a.shape, t) for a, t in zip(arrays, types))
        + tuple(shape((size,), F32) for size in sizes),
        in_specs=[VMEM_SPEC] + [ANY_SPEC] * len(arrays),
        out_specs=(ANY_SPEC,) * len(arrays) + (VMEM_SPEC,) * len(sizes),
        scratch_shapes=[pltpu.VMEM(a.shape, BF16) for a in arrays]
        + [pltpu.VMEM(a.shape, t) for a, t in zip(arrays, types)]
        + [dma((sum(cuts),)), dma((sum(cuts),))],
        compiler_params=pltpu.CompilerParams(vmem_limit_bytes=VMEM_LIMIT),
    )(flat, *arrays)


def on_device(
    tokens, doc_ids, qkv_weight, qv_bias, out_weight, out_bias, mid_gain, mid_shift,
    up_weight, up_bias, down_weight, down_bias, end_gain, end_shift, out_grad,
):
    width, hidden = tokens.shape[2], up_weight.shape[1]
    ring, shards = lax.axis_size("rep"), lax.axis_size("shard")
    levels = ring // 4
    sub = levels // GROUPS
    x = tokens[0]
    small = (qv_bias, out_bias, mid_gain, mid_shift, up_bias, down_bias, end_gain, end_shift)
    sizes = [v.shape[0] for v in small]
    own = (out_weight, up_weight, down_weight)
    att, flat, w_group, lse, o, q, k, kt, vt, x_rows, *full = forward_all(
        x, qkv_weight, doc_ids, list(small), own, ((2, 1, True), (0, 1, False), (1, 2, False)), ring, shards, 0
    )
    down_chunks = 6 if hidden % (6 * shards * ring * 16) == 0 else 1
    layer_out, gat, mid, flat, down, up, out = mlp_all(
        att, x, out_grad[0], flat, own, full, sizes, shards, levels, down_chunks, 6
    )
    input_grad, down, up, out, qkv, flat = tail_all(
        gat, lse, w_group, mid, flat, (q, k, kt, vt, o, x_rows), (down, up, out), sizes[0],
        ring, shards, 1,
    )
    down = down.reshape(-1, width)
    if up.ndim > 2:
        up = up.reshape(12, width // shards, -1).transpose(1, 0, 2).reshape(-1, hidden)
        out = out.reshape(2, width // shards, -1).transpose(1, 0, 2).reshape(-1, width)
    if qkv.ndim > 2:
        qkv = qkv.reshape(4 * QKV_CHUNKS, GROUPS, sub, -1, 3, SLAB).transpose(0, 2, 3, 4, 1, 5)
        qkv = qkv.reshape(-1, 3 * width)
    down, up, out, qkv, input_grad, *totals = widen_all(flat, (down, up, out, qkv), input_grad, sizes)
    return (
        layer_out[None], input_grad[None], qkv, totals[0], out, totals[1], totals[2],
        totals[3], up, totals[4], down, totals[5], totals[6], totals[7],
    )


def solution(mesh):
    rows = P("shard", None)
    flat = P("shard")
    acts = P("shard", "rep", None)
    in_specs = (
        acts, rows, rows, flat, rows, flat, flat, flat, rows, flat, rows, flat, flat, flat, acts
    )
    out_specs = (acts, acts, rows, flat, rows, flat, flat, flat, rows, flat, rows, flat, flat, flat)
    return jax.shard_map(
        on_device, mesh=mesh, in_specs=in_specs, out_specs=out_specs, check_vma=False
    )
```

```python
import jax
import jax.numpy as jnp
from jax import lax
from jax.experimental import pallas as pl
from jax.experimental.pallas import tpu as pltpu
from jax.sharding import PartitionSpec as P

HEADS = 12
HEAD_DIM = 64
BLOCK = 256
GROUPS = 4
PER = HEADS // GROUPS
SLAB = PER * HEAD_DIM
EPSILON = 1e-05
FAR = 2.0**100
F32 = jnp.float32
BF16 = jnp.bfloat16
LANES = 128
NN = (((1,), (0,)), ((), ()))
NT = (((1,), (1,)), ((), ()))
TN = (((0,), (0,)), ((), ()))
VMEM_SPEC = pl.BlockSpec(memory_space=pltpu.VMEM)
VMEM_LIMIT = 67043328


def mm(left, right, dims=NN):
    return lax.dot_general(left, right, dims, preferred_element_type=F32)


ANY_SPEC = pl.BlockSpec(memory_space=pl.ANY)


def remote(src, dst, send, recv, rep, shard):
    return pltpu.make_async_remote_copy(
        src_ref=src, dst_ref=dst, send_sem=send, recv_sem=recv,
        device_id=(rep, shard), device_id_type=pl.DeviceIdType.MESH,
    )


def hello(partners):
    barrier = pltpu.get_barrier_semaphore()
    total = 0
    for rep, shard, there in partners:
        if there is True:
            pl.semaphore_signal(
                barrier, inc=1, device_id=(rep, shard), device_id_type=pl.DeviceIdType.MESH
            )
            total = total + 1
        else:

            @pl.when(there)
            def _():
                pl.semaphore_signal(
                    barrier, inc=1, device_id=(rep, shard), device_id_type=pl.DeviceIdType.MESH
                )

            total = total + there.astype(jnp.int32)
    pl.semaphore_wait(barrier, total)


class Links:
    def __init__(self, ring, shards):
        self.ring, self.shards = ring, shards
        self.r, self.s = lax.axis_index("rep"), lax.axis_index("shard")
        self.levels = ring // 4
        self.z, self.c = self.r // 4, lax.rem(self.r, 2)
        self.y = lax.rem(self.r // 2, 2)
        self.sib = self.r + 1 - 2 * self.c
        self.yn = self.r + 2 - 4 * self.y
        self.others = [lax.rem(self.s + d, shards) for d in range(1, shards)]
        self.heights = [lax.rem(self.z + d, self.levels) for d in range(1, self.levels)]
        self.line = lax.rem(self.r, 4)

    def partners(self):
        return (
            [(self.sib, self.s, True), (self.yn, self.s, True)]
            + [(self.r, t, True) for t in self.others]
            + [(h * 4 + self.line, self.s, True) for h in self.heights]
        )


def forward_kernel(ring, shards, parts, sizes, *refs):
    n_vec = len(sizes)
    x_ref, w_in, docs_ref = refs[:3]
    vec_refs, own = refs[3 : 3 + n_vec], refs[3 + n_vec : 6 + n_vec]
    outs, rest = refs[6 + n_vec : 19 + n_vec], refs[19 + n_vec :]
    att_ref, flat_ref, wg_ref, lse_ref, o_out, q_out, k_out, kt_out, vt_out, xr_out = outs[:10]
    full = outs[10:]
    (
        w_ref, xa_ref, wl_ref, low_ref, bias_ref, o_ref, q_ref, k_ref, kt_ref, vt_ref, top_ref, sum_ref,
        send, recv, wsend, wrecv, fsend, frecv, vsend, vrecv, asend, arecv, osem,
    ) = rest
    net = Links(ring, shards)
    r, s, z, y, c = net.r, net.s, net.z, net.y, net.c
    levels, members = net.levels, ring // GROUPS
    g, m = r // members, lax.rem(r, members)
    sib, yn, line, others = net.sib, net.yn, net.line, net.others
    above, below = z < levels - 1, z > 0
    fetch = pltpu.make_async_copy(w_in, w_ref, osem.at[5 + GROUPS])
    fetch.start()
    hello(net.partners())

    halves = 2

    def move(b, kind, u, src=None):
        target = (r + 4, r - 4, yn, sib)[kind]
        rows = pl.ds(u * (BLOCK // halves), BLOCK // halves)
        src = xa_ref.at[b, rows] if src is None else src.at[rows]
        return remote(src, xa_ref.at[b, rows], send.at[kind, b, u], recv.at[b, u], target, s)

    for u in range(halves):
        pl.when(above)(lambda: move(r, 0, u, x_ref).start())
        pl.when(below)(lambda: move(r, 1, u, x_ref).start())
        move(r, 2, u, x_ref).start()
        move(r, 3, u, x_ref).start()
    xa_ref[r] = x_ref[...]

    width = x_ref.shape[1]
    fetch.wait()
    for k in range(GROUPS):

        @pl.when(g == k)
        def _():
            wl_ref[s] = jnp.concatenate(
                [w_ref[:, t * width + k * SLAB : t * width + (k + 1) * SLAB] for t in range(3)], 1
            )

    flat_ref[s] = jnp.concatenate([v[...].astype(F32).reshape(1, -1) for v in vec_refs], axis=1)
    lists = [
        remote(flat_ref.at[s], flat_ref.at[s], vsend.at[d], vrecv.at[d], r, t)
        for d, t in enumerate(others)
    ]
    pieces = [(lambda rows: wl_ref.at[s, rows], wl_ref, w_ref.shape[0] // 2, 0, False)]
    for w, count, quad in parts:
        size = own[w].shape[0] // (4 if quad else 2) // count
        for j in range(count):
            pieces.append((lambda rows, w=w: own[w].at[rows], full[w], size, (count, j), quad))

    def span(piece, yy, cc):
        size, where, quad = piece[2:]
        count, j = where or (1, 0)
        part = (yy * 2 + cc) if quad else cc
        return pl.ds(pl.multiple_of((part * count + j) * size, size), size)

    def across(at, d):
        rows = span(pieces[at], y, c)
        return remote(
            pieces[at][0](rows), pieces[at][1].at[s, rows], wsend.at[at, d], wrecv.at[at, d],
            r, others[d],
        )

    def shifted(at, d, kind, yy, cc, target):
        rows = span(pieces[at], yy, cc)
        spot = pieces[at][1].at[others[d], rows]
        return remote(spot, spot, fsend.at[at, d, kind], frecv.at[at, d, kind], target, s)

    def relay(at):
        for d in range(shards - 1):
            across(at, d).wait_recv()
            shifted(at, d, 0, y, c, sib).start()
            if pieces[at][4]:
                shifted(at, d, 1, y, c, yn).start()

    def relay_far(at):
        for d in range(shards - 1):
            shifted(at, d, 1, 1 - y, c, yn).wait_recv()
            shifted(at, d, 2, 1 - y, c, sib).start()

    def relayed(at):
        for d in range(shards - 1):
            shifted(at, d, 0, y, 1 - c, sib).wait_recv()
            if pieces[at][4]:
                shifted(at, d, 2, 1 - y, 1 - c, sib).wait_recv()

    for copy in lists:
        copy.start()
    for at in range(len(pieces)):
        for d in range(shards - 1):
            across(at, d).start()
    relay(0)
    for copy in lists:
        copy.wait_recv()
    n0 = sizes[0]
    qv = jnp.concatenate([flat_ref[t, :, :n0] for t in range(shards)], axis=1)
    for k in range(GROUPS):

        @pl.when(g == k)
        def _():
            row = jnp.concatenate(
                [qv[:, k * SLAB : (k + 1) * SLAB], qv[:, width + k * SLAB : width + (k + 1) * SLAB]],
                axis=1,
            )
            bias_ref[...] = jnp.broadcast_to(row, (8, 2 * SLAB)).T[:, :1]

    relayed(0)
    part = width // shards
    for t in range(shards):
        wg_ref[:, t * part : (t + 1) * part] = wl_ref[t].astype(F32).T.astype(BF16)

    def level(q):
        lo, hi = z, levels - 1 - z
        turn = jnp.minimum(lo, hi)
        swing = jnp.where(lax.rem(q, 2) == 1, z - (q + 1) // 2, z + q // 2)
        rest = jnp.where(lo > hi, z - (q - turn), z + (q - turn))
        return jnp.where(q <= 2 * turn, swing, rest)

    def event(n):
        k, t = (n - 2) // 4, lax.rem(n + 2, 4)
        q = jnp.where(n < 2, 0, jnp.where(lax.rem(t, 2) == 0, k + 1, k))
        j = jnp.where(n < 2, 2 * n, t)
        q = jnp.where(n >= ring - 2, levels - 1, q)
        j = jnp.where(n >= ring - 2, 2 * (n - ring + 2) + 1, j)
        lv = level(q)
        return lv * 4 + lax.rem(y + lax.rem(j, 2), 2) * 2 + lax.rem(c + j // 2, 2), lv, j

    sub = levels // GROUPS

    def arrive(n):
        b, lv, j = event(n)

        @pl.when(n > 0)
        def _():
            for u in range(halves):
                move(b, 3, u).wait_recv()

                @pl.when(j == 0)
                def _():
                    pl.when(jnp.logical_and(lv < z, above))(lambda: move(b, 0, u).start())
                    pl.when(jnp.logical_and(lv > z, below))(lambda: move(b, 1, u).start())
                    move(b, 2, u).start()

                pl.when(j < 2)(lambda: move(b, 3, u).start())

        both = mm(wg_ref[SLAB:, :], xa_ref[b], NT)
        kt = both[:SLAB].astype(BF16)
        kt_ref[b] = kt
        vt_ref[b] = (both[SLAB:] + bias_ref[SLAB:, :]).astype(BF16)
        at = pl.multiple_of(b * BLOCK, BLOCK)
        docs = docs_ref[:, pl.ds(at, BLOCK)].astype(F32)
        blank = jnp.zeros((HEAD_DIM - 2, BLOCK), F32)
        extra = jnp.concatenate([docs * FAR - FAR, docs * (-FAR), blank], axis=0)
        for h in range(PER):
            part = kt[h * HEAD_DIM : (h + 1) * HEAD_DIM].astype(F32)
            k_ref[h, pl.ds(at, BLOCK), :] = jnp.concatenate([part, extra], axis=0).T.astype(BF16)

        @pl.when(jnp.logical_and(j == 0, lax.rem(lv, sub) == lax.rem(z, sub)))
        def _():
            i = lv // sub
            qt = (mm(wg_ref[:SLAB, :], xa_ref[b], NT) + bias_ref[:SLAB, :]).astype(BF16)
            qt = qt.astype(F32) * HEAD_DIM ** (-0.5)
            extra = jnp.concatenate([docs, 1.0 - docs, blank], axis=0)
            for h in range(PER):
                part = qt[h * HEAD_DIM : (h + 1) * HEAD_DIM]
                q_ref[i, h] = jnp.concatenate([part, extra], axis=0).astype(BF16)

    def unit(i, kb):
        keys = pl.ds(pl.multiple_of(kb * BLOCK, BLOCK), BLOCK)
        for h in range(PER):
            head = pl.ds(h * HEAD_DIM, HEAD_DIM)
            score = mm(k_ref[h, keys, :], q_ref[i, h])
            old = top_ref[i, h]
            new = jnp.maximum(old, jnp.max(score, axis=0, keepdims=True))
            probs = jnp.exp(score - new)
            shrink = jnp.exp(old - new)
            top_ref[i, h] = new
            sum_ref[i, h] = sum_ref[i, h] * shrink + jnp.sum(probs, axis=0, keepdims=True)
            o_ref[i, head, :] = o_ref[i, head, :] * shrink + mm(
                vt_ref[kb, head, :], probs.astype(BF16)
            )

    def attend(n):
        b, lv, j = event(n)
        first = jnp.logical_and(j == 0, lax.rem(lv, sub) == lax.rem(z, sub))
        known = jnp.where(n < 2, 1, jnp.minimum((n - 2) // 4 + 2, levels))

        def pair(u, carry):
            near = u < known
            seen = level(jnp.minimum(u, known - 1))
            old = event(jnp.maximum(u - known, 0))[0]
            i = jnp.where(near, seen, lv) // sub
            kb = jnp.where(near, b, old)
            query = i * members + m
            mine = jnp.where(near, lax.rem(seen, sub) == lax.rem(z, sub), old < b)
            pl.when(jnp.logical_and(mine, kb <= query))(lambda: unit(i, kb))
            return carry

        lax.fori_loop(0, known + jnp.where(first, n, 0), pair, 0)

    top_ref[...] = jnp.full(top_ref.shape, -jnp.inf, F32)
    sum_ref[...] = jnp.zeros(sum_ref.shape, F32)
    o_ref[...] = jnp.zeros(o_ref.shape, F32)
    lag = 4
    turn_on = ring - 5

    def advance(n, carry):
        pl.when(n < ring)(lambda: arrive(n))

        @pl.when(n == turn_on)
        def _():
            for at in range(len(pieces)):
                if pieces[at][4]:
                    relay(at)

        pl.when(n >= lag)(lambda: attend(n - lag))
        return carry

    lax.fori_loop(0, ring + lag, advance, 0)
    saves = [
        pltpu.make_async_copy(src, dst, osem.at[n])
        for n, (src, dst) in enumerate(
            ((k_ref, k_out), (kt_ref, kt_out), (vt_ref, vt_out), (q_ref, q_out), (o_ref, o_out))
        )
    ]
    saves += [
        pltpu.make_async_copy(xa_ref.at[i * members + m], xr_out.at[i], osem.at[5 + i])
        for i in range(GROUPS)
    ]
    for save in saves[:3] + saves[5:]:
        save.start()

    def give(i):
        return remote(low_ref.at[i], att_ref.at[g], asend.at[i], arecv.at[g], i * members + m, s)

    for i in range(GROUPS):
        for h in range(PER):
            head = pl.ds(h * HEAD_DIM, HEAD_DIM)
            out = o_ref[i, head, :] / sum_ref[i, h]
            o_ref[i, head, :] = out
            low_ref[i, head, :] = out.astype(BF16)
            lse_ref[i, h] = top_ref[i, h] + jnp.log(sum_ref[i, h])

        @pl.when(g == i)
        def _():
            att_ref[g] = low_ref[i]

        pl.when(g != i)(lambda: give(i).start())
    for save in saves[3:5]:
        save.start()
    for at in range(1, len(pieces)):
        if pieces[at][4]:
            relay_far(at)
        else:
            relay(at)
    for d in range(1, GROUPS):
        p = lax.rem(g + d, GROUPS)
        remote(low_ref.at[0], att_ref.at[p], asend.at[0], arecv.at[p], r, s).wait_recv()
    for at in range(1, len(pieces)):
        relayed(at)
    for i in range(GROUPS):
        pl.when(g != i)(lambda: give(i).wait_send())

    def sent(e, carry):
        b, lv, j = event(e)

        for u in range(halves):

            @pl.when(j == 0)
            def _():
                pl.when(jnp.logical_and(lv <= z, above))(lambda: move(b, 0, u).wait_send())
                pl.when(jnp.logical_and(lv >= z, below))(lambda: move(b, 1, u).wait_send())
                move(b, 2, u).wait_send()

            pl.when(j < 2)(lambda: move(b, 3, u).wait_send())
        return carry

    lax.fori_loop(0, ring, sent, 0)
    for copy in lists:
        copy.wait_send()
    for at in range(len(pieces)):
        for d in range(shards - 1):
            across(at, d).wait_send()
            shifted(at, d, 0, y, c, sib).wait_send()
            if pieces[at][4]:
                shifted(at, d, 1, y, c, yn).wait_send()
                shifted(at, d, 2, 1 - y, c, sib).wait_send()
    for save in saves:
        save.wait()


def forward_all(x, qkv_weight, docs, vectors, weights, parts, ring, shards, ident):
    shape = jax.ShapeDtypeStruct
    dma = pltpu.SemaphoreType.DMA
    vmem = pltpu.VMEM
    n = 1 + sum(part[1] for part in parts)
    width = x.shape[1]
    sizes = [v.shape[0] for v in vectors]
    per = max(shards - 1, 1)
    o = (GROUPS, SLAB, BLOCK)
    q = (GROUPS, PER, 2 * HEAD_DIM, BLOCK)
    k = (PER, ring * BLOCK, 2 * HEAD_DIM)
    t = (ring, SLAB, BLOCK)
    return pl.pallas_call(
        lambda *refs: forward_kernel(ring, shards, parts, sizes, *refs),
        out_shape=(
            shape(o, BF16), shape((shards, 1, sum(sizes)), F32), shape((3 * SLAB, width), BF16),
            shape((GROUPS, PER, 1, BLOCK), F32), shape(o, F32), shape(q, BF16), shape(k, BF16),
            shape(t, BF16), shape(t, BF16), shape((GROUPS,) + x.shape, BF16),
        )
        + tuple(shape((shards,) + w.shape, w.dtype) for w in weights),
        in_specs=[VMEM_SPEC, ANY_SPEC] + [VMEM_SPEC] * (1 + len(vectors)) + [ANY_SPEC] * 3,
        out_specs=(VMEM_SPEC,) * 4 + (ANY_SPEC,) * 9,
        scratch_shapes=[
            vmem(qkv_weight.shape, BF16),
            vmem((ring,) + x.shape, BF16), vmem((shards, width // shards, 3 * SLAB), BF16),
            vmem(o, BF16), vmem((2 * SLAB, 1), F32), vmem(o, F32), vmem(q, BF16), vmem(k, BF16),
            vmem(t, BF16), vmem(t, BF16),
            vmem((GROUPS, PER, 1, BLOCK), F32), vmem((GROUPS, PER, 1, BLOCK), F32),
            dma((4, ring, 2)), dma((ring, 2)), dma((n, per)), dma((n, per)), dma((n, per, 3)),
            dma((n, per, 3)), dma((per,)), dma((per,)),
            dma((GROUPS,)), dma((GROUPS,)), dma((6 + GROUPS,)),
        ],
        compiler_params=pltpu.CompilerParams(
            collective_id=ident, has_side_effects=True, vmem_limit_bytes=VMEM_LIMIT
        ),
    )(x, qkv_weight, docs, *vectors, *weights)


def layer_norm(hidden, gain, shift):
    centre = hidden - jnp.mean(hidden, axis=-1, keepdims=True)
    inverse = lax.rsqrt(jnp.mean(centre * centre, axis=-1, keepdims=True) + EPSILON)
    normed = centre * inverse
    return (normed * gain + shift, normed, inverse)


def norm_back(grad_output, normed, inverse, gain):
    grad_normed = grad_output * gain
    centred = grad_normed - jnp.mean(grad_normed, axis=-1, keepdims=True)
    return inverse * (centred - normed * jnp.mean(grad_normed * normed, axis=-1, keepdims=True))


def mlp_kernel(
    shards, sizes, att_ref, x_ref, og_ref, flat_ref, *refs,
):
    own, full = refs[:3], refs[3:6]
    out_ref, gat_ref, mid_ref, small_ref, down_out, up_out, outw_out = refs[6:13]
    wo_ref, wu_ref, wd_ref, act_ref, slope_ref, gd_ref, gu_ref, go_ref, lsem, ssem = refs[13:]
    s = lax.axis_index("shard")
    width = x_ref.shape[1]
    hidden = wu_ref.shape[1]
    loads = []
    for w, ref in enumerate((wo_ref, wu_ref, wd_ref)):
        size = own[w].shape[0]
        group = []
        for d in range(shards):
            t = lax.rem(s + d, shards)
            rows = pl.ds(pl.multiple_of(t * size, size), size)
            src = own[w] if d == 0 else full[w].at[t]
            group.append(pltpu.make_async_copy(src, ref.at[rows], lsem.at[w * shards + d]))
        loads.append(group)
        for load in group:
            load.start()

    def ready(w):
        for load in loads[w]:
            load.wait()

    starts = [sum(sizes[:n]) for n in range(len(sizes))]

    def vector(n):
        return jnp.concatenate(
            [flat_ref[t, :, starts[n] : starts[n] + sizes[n]] for t in range(shards)], axis=1
        )

    def put(n, row):
        for t in range(shards):
            small_ref[t, :, starts[n] : starts[n] + sizes[n]] = row[
                :, t * sizes[n] : (t + 1) * sizes[n]
            ]

    small_ref[...] = jnp.zeros(small_ref.shape, F32)
    att = att_ref[...].reshape(width, BLOCK)
    ready(0)
    branch = mm(att, wo_ref[...], TN) + vector(1)
    gain_mid = vector(2)
    mid_out, mid_norm, mid_inv = layer_norm(x_ref[...].astype(F32) + branch, gain_mid, vector(3))
    mid_low = mid_out.astype(BF16)
    up_bias = vector(4)
    cols = 512
    ready(1)
    for at in range(0, hidden, cols):
        block = slice(at, at + cols)
        pre = mm(mid_low, wu_ref[:, block]) + up_bias[:, block]
        phi = 0.5 * (1.0 + lax.erf(pre * 0.7071067811865476))
        act_ref[:, block] = (pre * phi).astype(BF16)
        slope_ref[:, block] = phi + pre * jnp.exp(-0.5 * pre * pre) * 0.3989422804014327
    ready(2)
    ffn = mm(act_ref[...], wd_ref[...]) + vector(5)
    gain_end = vector(6)
    end_out, end_norm, end_inv = layer_norm(mid_out + ffn, gain_end, vector(7))
    out_ref[...] = end_out.astype(BF16)
    top = og_ref[...].astype(F32)

    def column(value):
        return jnp.sum(value, axis=0, keepdims=True)

    put(6, column(top * end_norm))
    put(7, column(top))
    grad_end_in = norm_back(top, end_norm, end_inv, gain_end)
    grad_ffn = grad_end_in.astype(BF16)
    put(5, column(grad_ffn.astype(F32)))
    saves = []

    def save(src, dst):
        copy = pltpu.make_async_copy(src, dst, ssem.at[len(saves)])
        copy.start()
        saves.append(copy)

    chunks = gd_ref.shape[1]
    rows = hidden // shards // chunks
    for t in range(shards):
        for k in range(chunks):
            at = t * (hidden // shards) + k * rows
            value = mm(act_ref[:, at : at + rows], grad_ffn, TN)
            gd_ref[t, k] = value.astype(BF16).reshape(gd_ref.shape[2:])
        save(gd_ref.at[t], down_out.at[t])
    grad_mid_out = grad_end_in
    ups = []
    wide = hidden // gu_ref.shape[0]
    for k in range(gu_ref.shape[0]):
        block = slice(k * wide, (k + 1) * wide)
        grad_act = mm(grad_ffn, wd_ref[block, :], NT)
        grad_pre = (grad_act * slope_ref[:, block]).astype(BF16)
        ups.append(column(grad_pre.astype(F32)))
        value = mm(mid_low, grad_pre, TN).astype(BF16)
        for half in range(2):
            gu_ref[k, half] = value[:, half * (wide // 2) : (half + 1) * (wide // 2)].reshape(
                gu_ref.shape[2:]
            )
        save(gu_ref.at[k], up_out.at[k])
        grad_mid_out = grad_mid_out + mm(grad_pre, wu_ref[:, block], NT)
    put(4, jnp.concatenate(ups, axis=1))
    put(2, column(grad_mid_out * mid_norm))
    put(3, column(grad_mid_out))
    grad_mid_in = norm_back(grad_mid_out, mid_norm, mid_inv, gain_mid)
    mid_ref[...] = grad_mid_in
    grad_branch = grad_mid_in.astype(BF16)
    put(1, column(grad_branch.astype(F32)))
    gat_ref[...] = mm(wo_ref[...], grad_branch, NT).astype(BF16).reshape(gat_ref.shape)
    value = mm(att, grad_branch).astype(BF16)
    for half in range(2):
        go_ref[0, half] = value[:, half * (width // 2) : (half + 1) * (width // 2)].reshape(
            go_ref.shape[2:]
        )
    save(go_ref, outw_out)
    for copy in saves:
        copy.wait()


def mlp_all(att, x, out_grad, flat, own, full, sizes, shards, levels, down_chunks, up_chunks):
    shape = jax.ShapeDtypeStruct
    dma = pltpu.SemaphoreType.DMA
    vmem = pltpu.VMEM
    width, hidden = own[0].shape[1], own[1].shape[1]
    gd = (shards, down_chunks, 2, 2, levels, hidden // shards // down_chunks // 4 // levels, width)
    gu = (up_chunks, 2, shards, 2, levels, width // shards // 2 // levels, hidden // up_chunks // 2)
    go = (1, 2, shards, 2, levels, width // shards // 2 // levels, width // 2)
    return pl.pallas_call(
        lambda *refs: mlp_kernel(shards, sizes, *refs),
        out_shape=(
            shape((BLOCK, width), BF16), shape((GROUPS, SLAB, BLOCK), BF16),
            shape((BLOCK, width), F32), shape(flat.shape, F32),
            shape(gd, BF16), shape(gu, BF16), shape(go, BF16),
        ),
        in_specs=[VMEM_SPEC] * 4 + [ANY_SPEC] * 6,
        out_specs=(VMEM_SPEC,) * 4 + (ANY_SPEC,) * 3,
        scratch_shapes=[
            vmem((width, width), BF16), vmem((width, hidden), BF16), vmem((hidden, width), BF16),
            vmem((BLOCK, hidden), BF16), vmem((BLOCK, hidden), F32),
            vmem(gd, BF16), vmem(gu, BF16), vmem(go, BF16),
            dma((3 * shards,)), dma((shards + up_chunks + 1,)),
        ],
        compiler_params=pltpu.CompilerParams(vmem_limit_bytes=VMEM_LIMIT),
    )(att, x, out_grad, flat, *own, *full)


def add_rows(out, terms):
    total = terms[0][...].astype(F32)
    for term in terms[1:]:
        total = total + term[...].astype(F32)
    out[...] = total.astype(out.dtype)


def reduce_steps(net, slab, out, own, near, side, mate, tall, sems, group):
    asend, arecv, bsend, brecv, csend, crecv, dsend, drecv, esend, erecv, fsend, frecv, gsend, grecv, lsem = sems
    r, s, z, y, c = net.r, net.s, net.z, net.y, net.c
    base = z // group * group
    zz = lax.rem(z, group)
    inner = [lax.rem(zz + d, group) for d in range(1, group)]
    near_copy = lambda: remote(slab(1 - c), near, asend, arecv, net.sib, s)
    own_copy = lambda: pltpu.make_async_copy(slab(c), own, lsem)
    across = lambda d: remote(
        near.at[net.others[d]], side.at[d], bsend.at[d], brecv.at[d], r, net.others[d]
    )
    over = lambda: remote(near.at[s, 1 - y], mate, csend, crecv, net.yn, s)
    along = lambda d: remote(
        near.at[s, y, inner[d]], tall.at[d], dsend.at[d], drecv.at[d],
        (base + inner[d]) * 4 + net.line, s,
    )
    one, four = out
    mine = one(c, y, z)
    levels = net.levels

    def climb(k, up):
        at = z - k if up else z + k
        piece = one(c, y, at)
        target = (z + 1 if up else z - 1) * 4 + net.line
        return remote(piece, piece, esend.at[int(up), k], erecv.at[int(up), k], target, s)

    def landed(k, up):
        at = z - k if up else z + k
        piece = one(c, y, at)
        return remote(piece, piece, esend.at[int(up), k], erecv.at[int(up), k - 1], net.r, s)

    def both_ways(k, act):
        here = (z - k >= 0, z + k < levels)
        more = (z + 1 < levels, z > 0)
        pl.when(jnp.logical_and(here[0], more[0]))(lambda: act(True))
        pl.when(jnp.logical_and(here[1], more[1]))(lambda: act(False))

    def wait_from(k):
        pl.when(z - k >= 0)(lambda: landed(k, True).wait_recv())
        pl.when(z + k < levels)(lambda: landed(k, False).wait_recv())


    def pair(at):
        return remote(one(c, y, at), one(c, y, at), fsend.at[at], frecv.at[at], net.yn, s)

    def pair_from(k):
        if k:
            pl.when(z - k >= 0)(lambda: pair(z - k).start())
            pl.when(z + k < levels)(lambda: pair(z + k).start())
        else:
            pair(z).start()

    last = lambda: remote(four(c), four(c), gsend, grecv, net.sib, s)
    n_side, n_inner = len(net.others), len(inner)

    def step0():
        near_copy().start()
        own_copy().start()

    def step1():
        near_copy().wait_recv()
        own_copy().wait()
        for t in range(net.shards):
            for half in range(2):
                add_rows(near.at[t, half], [own.at[t, half], near.at[t, half]])
        for d in range(n_side):
            across(d).start()

    def step2():
        for d in range(n_side):
            across(d).wait_recv()
        for half in range(2):
            add_rows(
                near.at[s, half], [near.at[s, half]] + [side.at[d, half] for d in range(n_side)]
            )
        over().start()

    def step3():
        over().wait_recv()
        add_rows(near.at[s, y], [near.at[s, y], mate])
        for d in range(n_inner):
            along(d).start()

    def step4():
        for d in range(n_inner):
            along(d).wait_recv()
        add_rows(mine, [near.at[s, y, zz]] + [tall.at[d] for d in range(n_inner)])
        both_ways(0, lambda up: climb(0, up).start())
        pair_from(0)

    def onward(k):
        def step():
            wait_from(k)
            both_ways(k, lambda up: climb(k, up).start())
            pair_from(k)

        return step

    def step5():
        wait_from(levels - 1)
        pair_from(levels - 1)

    def step6():
        for at in range(levels):
            piece = one(c, 1 - y, at)
            remote(piece, piece, fsend.at[at], frecv.at[at], net.yn, s).wait_recv()
        last().start()

    def step7():
        last().wait_recv()

    def drain():
        near_copy().wait_send()
        for d in range(n_side):
            across(d).wait_send()
        over().wait_send()
        for d in range(n_inner):
            along(d).wait_send()
        for k in range(levels - 1):
            both_ways(k, lambda up: climb(k, up).wait_send())
        for at in range(levels):
            pair(at).wait_send()
        last().wait_send()

    middle = [onward(k) for k in range(1, levels - 1)]
    return [step0, step1, step2, step3, step4, *middle, step5, step6, step7], drain


def reduce_scratch(shards, levels, group, rows, cols):
    dma = pltpu.SemaphoreType.DMA
    vmem = pltpu.VMEM
    many = lambda n: dma((max(n, 1),))
    buffers = [
        vmem((shards, 2, group, rows, cols), BF16),
        vmem((shards, 2, group, rows, cols), BF16),
        vmem((max(shards - 1, 1), 2, group, rows, cols), BF16),
        vmem((group, rows, cols), BF16),
        vmem((max(group - 1, 1), rows, cols), BF16),
    ]
    sems = [
        dma(()), dma(()), many(shards - 1), many(shards - 1), dma(()), dma(()),
        many(group - 1), many(group - 1), dma((2, levels)), dma((2, levels)),
        dma((levels,)), dma((levels,)), dma(()), dma(()), dma(()),
    ]
    return buffers + sems


SCRATCH = 20


def small_steps(net, src, out, near, side, mate, tall, sems):
    asend, arecv, bsend, brecv, csend, crecv, dsend, drecv = sems
    r, s, z, y, c = net.r, net.s, net.z, net.y, net.c
    near_copy = lambda: remote(src, near.at[1], asend, arecv, net.sib, s)
    across = lambda d: remote(
        near.at[0, net.others[d]], side.at[s], bsend.at[d], brecv.at[d], r, net.others[d]
    )
    over = lambda: remote(mate.at[0], mate.at[1], csend, crecv, net.yn, s)
    along = lambda d: remote(
        tall.at[z], tall.at[z], dsend.at[d], drecv.at[d], net.heights[d] * 4 + net.line, s
    )

    def step0():
        near_copy().start()

    def step1():
        near_copy().wait_recv()
        near[0] = src[...] + near[1]
        side[s] = near[0, s]
        for d in range(len(net.others)):
            across(d).start()

    def step2():
        for d in range(len(net.others)):
            across(d).wait_recv()
        total = side[0]
        for t in range(1, net.shards):
            total = total + side[t]
        mate[0] = total
        over().start()

    def step3():
        over().wait_recv()
        tall[z] = mate[0] + mate[1]
        for d in range(len(net.heights)):
            along(d).start()

    def step4():
        for d in range(len(net.heights)):
            along(d).wait_recv()
        total = tall[0]
        for t in range(1, net.levels):
            total = total + tall[t]
        out[...] = total

    def drain():
        near_copy().wait_send()
        for d in range(len(net.others)):
            across(d).wait_send()
        over().wait_send()
        for d in range(len(net.heights)):
            along(d).wait_send()

    return [step0, step1, step2, step3, step4], drain


def small_scratch(shards, levels, rows):
    dma = pltpu.SemaphoreType.DMA
    vmem = pltpu.VMEM
    return [
        vmem((2, shards, 1, rows), F32), vmem((shards, 1, rows), F32),
        vmem((2, 1, rows), F32), vmem((levels, 1, rows), F32),
        dma(()), dma(()), dma((max(shards - 1, 1),)), dma((max(shards - 1, 1),)),
        dma(()), dma(()), dma((levels - 1,)), dma((levels - 1,)),
    ]


def places(ref, chunk, core_first, levels, rows, cols):
    if len(ref.shape) != 2:
        return (
            lambda c, y, z: ref.at[chunk, c, y, z], lambda c: ref.at[chunk, c],
        )
    if core_first:

        def view(c, at, size):
            lanes = pl.ds(pl.multiple_of((chunk * 2 + c) * cols, cols), cols)
            return ref.at[pl.ds(pl.multiple_of(at, rows), size), lanes]

        return (
            lambda c, y, z: view(c, (y * levels + z) * rows, rows),
            lambda c: view(c, 0, 2 * levels * rows),
        )

    def span(at, count):
        first = (chunk * 4 * levels + at) * rows
        return ref.at[pl.ds(pl.multiple_of(first, rows), count * rows)]

    return (
        lambda c, y, z: span((c * 2 + y) * levels + z, 1),
        lambda c: span(c * 2 * levels, 2 * levels),
    )


def spread_out(jobs, offsets):
    ticks = {}
    for n, steps in enumerate(jobs):
        for t, step in enumerate(steps):
            ticks.setdefault(n + offsets[t], []).append(step)
    return [ticks.get(t, []) for t in range(max(ticks, default=-1) + 1)]


def term_jobs(net, specs, chunk_shapes, terms, outs, rest):
    jobs, drains = [], []
    for number, (which, k, core_first) in enumerate(specs):
        scratch = rest[number * SCRATCH : (number + 1) * SCRATCH]
        ref = terms[which]
        if core_first:
            slab = lambda core, ref=ref, k=k: ref.at[k, core]
        else:
            slab = lambda core, ref=ref, k=k: ref.at[:, k, core]
        spot = places(outs[which], k, core_first, net.levels, *chunk_shapes[which])
        steps, drain = reduce_steps(net, slab, spot, *scratch[:5], scratch[5:], net.levels)
        jobs.append(steps)
        drains.append(drain)
    return jobs, drains, rest[len(specs) * SCRATCH :]


def sums_kernel(ring, shards, specs, chunk_shapes, *refs):
    n = len(chunk_shapes)
    net = Links(ring, shards)
    hello(net.partners())
    jobs, drains, _ = term_jobs(net, specs, chunk_shapes, refs[:n], refs[n : 2 * n], refs[2 * n :])
    for steps in spread_out(jobs, offsets(net.levels)):
        for step in steps:
            step()
    for drain in drains:
        drain()


def tail_kernel(ring, shards, specs, chunk_shapes, n0, *refs):
    (
        go_ref, lse_ref, w_in, mid_in, small_ref, q_in, k_in, kt_in, vt_in, o_in, xr_in,
    ) = refs[:11]
    n_terms = len(chunk_shapes)
    terms, refs = refs[11 : 11 + n_terms], refs[11 + n_terms :]
    out_ref, outs, (qkv_ref, total_small) = refs[0], refs[1 : 1 + n_terms], refs[1 + n_terms : 3 + n_terms]
    (
        w_ref, mid_ref, q_ref, k_ref, kt_ref, vt_ref, o_ref,
        g_ref, x_ref, v_ref, delta_ref, acc_ref, dk_ref, dv_ref, pq_ref, stage_ref, got_ref, got2_ref,
        dw_ref, dx_ref, near_ref, far_ref, db_ref, dwl_ref, row_ref, sum_ref, all_ref,
        gsend, grecv, ksend, krecv, xsend, xrecv, lsem,
    ) = refs[3 + n_terms : 37 + n_terms]
    finals, rest = outs, refs[37 + n_terms :]
    outs, rest = rest[:n_terms], rest[n_terms:]
    copies = [
        pltpu.make_async_copy(src, dst, lsem.at[8 + n])
        for n, (src, dst) in enumerate(zip(outs, finals))
    ]
    net = Links(ring, shards)
    r, s = net.r, net.s
    levels, members = net.levels, ring // GROUPS
    sub = levels // GROUPS
    g, m = r // members, lax.rem(r, members)
    peers = [lax.rem(g + d, GROUPS) for d in range(1, GROUPS)]
    mates = [lax.rem(m + d, members) for d in range(1, members)]
    partners = net.partners()
    if levels != GROUPS:
        partners = partners + [(p * members + m, s, True) for p in peers]
        partners = partners + [(g * members + t, s, True) for t in mates]
    else:
        partners = partners + [(g * members + 3 - m, s, True)]
    hello(partners)

    def give(p):
        return remote(go_ref.at[p], g_ref.at[g], gsend.at[p], grecv.at[g], p * members + m, s)

    def take(p):
        return remote(go_ref.at[p], g_ref.at[p], gsend.at[p], grecv.at[p], p * members + m, s)

    for p in peers:
        give(p).start()
    loads = [
        pltpu.make_async_copy(src, dst, lsem.at[n])
        for n, (src, dst) in enumerate(
            ((vt_in, vt_ref), (k_in, k_ref), (q_in, q_ref), (kt_in, kt_ref), (o_in, o_ref),
             (xr_in, x_ref), (w_in, w_ref), (mid_in, mid_ref))
        )
    ]
    for load in loads:
        load.start()
    g_ref[g] = go_ref[g]

    jobs, drains, rest = term_jobs(net, specs, chunk_shapes, terms, outs, rest)
    qkv_jobs = []
    for k in range(QKV_CHUNKS):
        steps, drain = reduce_steps(
            net, lambda core, k=k: dwl_ref.at[:, k, core], places(all_ref, k, False, levels, 0, 0),
            *rest[:5], rest[5:SCRATCH], sub
        )
        qkv_jobs.append(steps)
        drains.append(drain)
        rest = rest[SCRATCH:]
    vec_steps, drain = small_steps(net, sum_ref, total_small, *rest[:4], rest[4:])
    drains.append(drain)
    ticks = spread_out(jobs, offsets(levels))

    width = w_in.shape[1]

    def prepare():
        dwl_ref[...] = dw_ref[...].astype(BF16).reshape(dwl_ref.shape)
        row = jnp.broadcast_to(db_ref[...], (3 * SLAB, 8)).T[:1]
        row_ref[...] = jnp.zeros(row_ref.shape, F32)
        for k in range(GROUPS):

            @pl.when(g == k)
            def _():
                row_ref[:, k * SLAB : (k + 1) * SLAB] = row[:, :SLAB]
                row_ref[:, width + k * SLAB : width + (k + 1) * SLAB] = row[:, 2 * SLAB :]

        sum_ref[...] = small_ref[...]
        for t in range(shards):
            sum_ref[t, :, :n0] = row_ref[:, t * n0 : (t + 1) * n0]

    ready = -(-(10 * members + 2 + SHIFTS[0] + 1) // PACE)
    ticks.append([copy.start for copy in copies])
    late = [[list(steps) for steps in zip(*qkv_jobs)], [[step] for step in vec_steps]]
    ticks += [[] for _ in range(ready + max(map(len, late)) - len(ticks))]
    ticks[ready].append(prepare)
    for series in late:
        for t, steps in enumerate(series):
            ticks[ready + t] += steps

    def tick(t, lo, hi):
        if hi - lo == 1:
            for step in ticks[lo]:
                step()
        else:
            mid = (lo + hi) // 2
            pl.when(t < mid)(lambda: tick(t, lo, mid))
            pl.when(t >= mid)(lambda: tick(t, mid, hi))

    for load in loads[:1]:
        load.wait()

    def turn(b, carry):
        rows = pl.ds(pl.multiple_of(b * BLOCK, BLOCK), BLOCK)
        for h in range(PER):
            v_ref[h, rows, :] = (
                vt_ref[b, h * HEAD_DIM : (h + 1) * HEAD_DIM, :].astype(F32).T.astype(BF16)
            )
        dk_ref[b] = jnp.zeros((SLAB, BLOCK), F32)
        dv_ref[b] = jnp.zeros((SLAB, BLOCK), F32)
        return carry

    lax.fori_loop(0, ring, turn, 0)
    dw_ref[...] = jnp.zeros(dw_ref.shape, F32)
    db_ref[...] = jnp.zeros(db_ref.shape, F32)
    for load in loads[1:]:
        load.wait()

    pairs = members // 2
    c, mt = net.c, m // 2
    fellows = [lax.rem(mt + d, pairs) for d in range(1, pairs)]
    pieces = 4
    size = BLOCK // pieces

    def cross():
        return lambda j: remote(
            stage_ref.at[j], got_ref.at[j], ksend.at[j, 0], krecv.at[j, 0], net.sib, s
        )

    to_core = cross()

    def share(j, d):
        t = fellows[d]
        return remote(
            got_ref.at[j, t], got2_ref.at[j, d], ksend.at[j, d + 1], krecv.at[j, d + 1],
            g * members + t * 2 + c, s,
        )

    def hop(j, u, side, target):
        rows = pl.ds(u * size, size)
        return remote(
            dx_ref.at[j, rows], far_ref.at[j, side, rows], xsend.at[j, u], xrecv.at[j, side, u],
            target, s,
        )

    def pass_dx(j, u):
        down = lambda: hop(j, u, 0, r - members)
        up = lambda: hop(j, u, 1, r + members)
        return down, up

    def begin(i):
        pl.when(g != i)(lambda: take(i).wait_recv())
        for h in range(PER):
            head = pl.ds(h * HEAD_DIM, HEAD_DIM)
            delta_ref[h] = jnp.sum(
                g_ref[i, head, :].astype(F32) * o_ref[i, head, :], axis=0, keepdims=True
            )
        acc_ref[...] = jnp.zeros(acc_ref.shape, F32)

    def unit(i, kb):
        keys = pl.ds(pl.multiple_of(kb * BLOCK, BLOCK), BLOCK)
        for h in range(PER):
            head = pl.ds(h * HEAD_DIM, HEAD_DIM)
            score = mm(k_ref[h, keys, :], q_ref[i, h])
            probs = jnp.exp(score - lse_ref[i, h])
            grad = g_ref[i, head, :]
            moved = (probs * (mm(v_ref[h, keys, :], grad) - delta_ref[h])).astype(BF16)
            acc_ref[h] += mm(kt_ref[kb, head, :], moved)
            dk_ref[kb, head, :] += mm(q_ref[i, h, :HEAD_DIM, :], moved, NT)
            dv_ref[kb, head, :] += mm(grad, probs.astype(BF16), NT)

    def end(i):
        for h in range(PER):
            pq_ref[i, pl.ds(h * HEAD_DIM, HEAD_DIM), :] = (
                acc_ref[h] * HEAD_DIM ** (-0.5)
            ).astype(BF16)
        for t in range(pairs):
            b = i * members + t * 2 + 1 - c
            stage_ref[i, t, :SLAB, :] = dk_ref[b].astype(BF16)
            stage_ref[i, t, SLAB:, :] = dv_ref[b].astype(BF16)
        to_core(i).start()

    def merge(j):
        to_core(j).wait_recv()
        for d, t in enumerate(fellows):
            b = j * members + t * 2 + c
            for half, ref in enumerate((dk_ref, dv_ref)):
                rows = pl.ds(half * SLAB, SLAB)
                got_ref[j, t, rows, :] = (ref[b] + got_ref[j, t, rows, :].astype(F32)).astype(BF16)
            share(j, d).start()

    def finish(j):
        b = j * members + m
        dk = dk_ref[b] + got_ref[j, mt, :SLAB, :].astype(F32)
        dv = dv_ref[b] + got_ref[j, mt, SLAB:, :].astype(F32)
        for d in range(pairs - 1):
            share(j, d).wait_recv()
            dk = dk + got2_ref[j, d, :SLAB, :].astype(F32)
            dv = dv + got2_ref[j, d, SLAB:, :].astype(F32)
        proj = jnp.concatenate([pq_ref[j], dk.astype(BF16), dv.astype(BF16)], axis=0)
        db_ref[...] += jnp.sum(proj.astype(F32), axis=1, keepdims=True)
        dx = mm(proj, w_ref[...], TN)
        near_ref[j] = dx
        dx_ref[j] = dx.astype(BF16)
        start_dx(j, 0)
        dw_ref[...] += mm(x_ref[j], proj.T, TN)

    def start_dx(j, depth):
        from_below = jnp.logical_and(g < j, g == depth)
        from_above = jnp.logical_and(g > j, GROUPS - 1 - g == depth)
        for u in range(pieces):
            rows = pl.ds(u * size, size)
            down, up = pass_dx(j, u)

            @pl.when(from_below)
            def _():
                if depth:
                    hop(j, u, 1, r).wait_recv()
                    dx_ref[j, rows] = (near_ref[j, rows] + far_ref[j, 1, rows].astype(F32)).astype(BF16)
                up().start()

            @pl.when(from_above)
            def _():
                if depth:
                    hop(j, u, 0, r).wait_recv()
                    dx_ref[j, rows] = (near_ref[j, rows] + far_ref[j, 0, rows].astype(F32)).astype(BF16)
                down().start()

    def own_dx():
        for side, there in ((0, g < GROUPS - 1), (1, g > 0)):

            @pl.when(there)
            def _():
                for u in range(pieces):
                    hop(g, u, side, r).wait_recv()
                near_ref[g] += far_ref[g, side].astype(F32)

    sizes = [i * members + m + 1 for i in range(GROUPS)][::-1]
    ends = [sum(sizes[: n + 1]) for n in range(GROUPS)]
    units = ends[-1]
    finishes = [members * n + 2 for n in (4, 7, 9, 10)]

    def advance(it, carry):
        past = [(it >= e).astype(jnp.int32) for e in ends]
        i = GROUPS - 1 - past[0] - past[1] - past[2]
        first = jnp.where(i == 3, 0, jnp.where(i == 2, ends[0], jnp.where(i == 1, ends[1], ends[2])))
        kb = it - first

        t = it // PACE
        if ticks:
            pl.when(jnp.logical_and(lax.rem(it, PACE) == 0, t < len(ticks)))(
                lambda: tick(t, 0, len(ticks))
            )

        @pl.when(it < units)
        def _():
            pl.when(kb == 0)(lambda: begin(i))
            unit(i, kb)

            @pl.when(kb == i * members + m)
            def _():
                end(i)

        def at_times(shift, act):
            n_due = sum((it - shift >= at).astype(jnp.int32) for at in finishes)
            n_done = sum((it - shift > at).astype(jnp.int32) for at in finishes)
            pl.when(n_due > n_done)(lambda: act(GROUPS - n_due))

        at_times(0, merge)
        at_times(SHIFTS[0], finish)
        for depth in range(1, GROUPS - 1):
            at_times(SHIFTS[depth], lambda j, depth=depth: start_dx(j, depth))
        return carry

    lax.fori_loop(0, PACE * len(ticks), advance, 0)

    for copy in copies:
        copy.wait()
    own_dx()
    out_ref[...] = (near_ref[g] + mid_ref[...]).astype(BF16)
    if len(qkv_ref.shape) == 2:
        rows = all_ref.shape[-2]
        for part in range(4 * QKV_CHUNKS):
            for z in range(levels):
                at = (part * sub + z % sub) * rows
                piece = all_ref[part // 4, part // 2 % 2, part % 2, z]
                for t in range(3):
                    lane = t * width + z // sub * SLAB
                    qkv_ref[at : at + rows, lane : lane + SLAB] = piece[
                        :, t * SLAB : (t + 1) * SLAB
                    ]
    else:
        qkv_ref[...] = all_ref[...]
    for p in peers:
        give(p).wait_send()
    for j in range(GROUPS):
        to_core(j).wait_send()
        for d in range(pairs - 1):
            share(j, d).wait_send()
        for u in range(pieces):
            pl.when(g != j)(lambda: hop(j, u, 0, r).wait_send())
    for drain in drains:
        drain()


PACE = 2
QKV_CHUNKS = 3


def offsets(levels, gaps=(2, 2, 2, 2, 2, 2, 2, 2)):
    steps = gaps[:4] + gaps[4:5] * (levels - 2) + gaps[5:]
    return [sum(steps[:t]) for t in range(len(steps) + 1)]


SHIFTS = (2, 5, 7)


def tail_all(gat, lse, w_group, mid, small, saved, terms, n0, ring, shards, ident):
    members, levels = ring // GROUPS, ring // 4
    sub = levels // GROUPS
    width = mid.shape[1]
    part = width // shards
    shape = jax.ShapeDtypeStruct
    dma = pltpu.SemaphoreType.DMA
    vmem = pltpu.VMEM
    specs, scratch, out_shape, chunk_shapes = [], [], [], []
    for i, term in enumerate(terms):
        core_first = i > 0
        chunks = term.shape[0] if core_first else term.shape[1]
        rows, cols = term.shape[-2:]
        chunk_shapes.append((rows, cols))
        if rows % 16:
            out_shape.append(shape((chunks, 2, 2, levels, rows, cols), BF16))
        elif core_first:
            out_shape.append(shape((2 * levels * rows, chunks * 2 * cols), BF16))
        else:
            out_shape.append(shape((chunks * 4 * levels * rows, cols), BF16))
        for k in range(chunks):
            specs.append((i, k, core_first))
            scratch += reduce_scratch(shards, levels, levels, rows, cols)
    term_scratch, term_shapes = scratch, out_shape
    apart = ring * BLOCK > 4096
    if apart:
        sums = pl.pallas_call(
            lambda *refs: sums_kernel(ring, shards, specs, chunk_shapes, *refs),
            out_shape=tuple(term_shapes),
            in_specs=[ANY_SPEC] * 3,
            out_specs=(VMEM_SPEC,) * 3,
            scratch_shapes=term_scratch,
            compiler_params=pltpu.CompilerParams(
                collective_id=ident + 1, has_side_effects=True, vmem_limit_bytes=VMEM_LIMIT
            ),
        )(*terms)
    specs, chunk_shapes = ([], []) if apart else (specs, chunk_shapes)
    scratch = [] if apart else list(term_scratch)
    out_shape = [] if apart else list(term_shapes)
    terms = () if apart else terms
    rows = part // (4 * QKV_CHUNKS) // sub
    buffer = (QKV_CHUNKS, 2, 2, levels, rows, 3 * SLAB)
    for _ in range(QKV_CHUNKS):
        scratch += reduce_scratch(shards, levels, sub, rows, 3 * SLAB)
    scratch += small_scratch(shards, levels, small.shape[2])
    out_shape.append(shape(buffer if rows % 16 else (part, 3 * width), BF16))
    slab = (GROUPS, SLAB, BLOCK)
    tall = (ring, SLAB, BLOCK)
    result = pl.pallas_call(
        lambda *refs: tail_kernel(ring, shards, specs, chunk_shapes, n0, *refs),
        out_shape=(shape((BLOCK, width), BF16), *out_shape, shape((1, small.shape[2]), F32)),
        in_specs=[VMEM_SPEC] * 2 + [ANY_SPEC] * 2 + [VMEM_SPEC] + [ANY_SPEC] * (6 + len(terms)),
        out_specs=(VMEM_SPEC,) + (ANY_SPEC,) * len(terms) + (VMEM_SPEC,) * 2,
        scratch_shapes=[
            vmem(w_group.shape, BF16), vmem(mid.shape, F32),
            vmem((GROUPS, PER, 2 * HEAD_DIM, BLOCK), BF16),
            vmem((PER, ring * BLOCK, 2 * HEAD_DIM), BF16),
            vmem(tall, BF16), vmem(tall, BF16), vmem(slab, F32),
            vmem(slab, BF16),
            vmem((GROUPS, BLOCK, width), BF16),
            vmem((PER, ring * BLOCK, HEAD_DIM), BF16),
            vmem((PER, 1, BLOCK), F32),
            vmem((PER, HEAD_DIM, BLOCK), F32),
            vmem(tall, F32), vmem(tall, F32), vmem(slab, BF16),
            vmem((GROUPS, members // 2, 2 * SLAB, BLOCK), BF16),
            vmem((GROUPS, members // 2, 2 * SLAB, BLOCK), BF16),
            vmem((GROUPS, members // 2 - 1, 2 * SLAB, BLOCK), BF16),
            vmem((width, 3 * SLAB), F32),
            vmem((GROUPS, BLOCK, width), BF16),
            vmem((GROUPS, BLOCK, width), F32),
            vmem((GROUPS, 2, BLOCK, width), BF16),
            vmem((3 * SLAB, 1), F32),
            vmem((shards, QKV_CHUNKS, 2, 2, sub, rows, 3 * SLAB), BF16),
            vmem((1, 2 * width), F32),
            vmem(small.shape, F32),
            vmem(buffer, BF16),
            dma((GROUPS,)), dma((GROUPS,)),
            dma((GROUPS, members // 2)), dma((GROUPS, members // 2)),
            dma((GROUPS, 4)), dma((GROUPS, 2, 4)), dma((11,)),
            *(vmem(o.shape, BF16) for o in out_shape[: len(terms)]),
            *scratch,
        ],
        compiler_params=pltpu.CompilerParams(
            collective_id=ident, has_side_effects=True, vmem_limit_bytes=VMEM_LIMIT
        ),
    )(gat, lse, w_group, mid, small, *saved, *terms)
    return (result[0], *sums, *result[1:]) if apart else result


def widen_kernel(sizes, cuts, flat_ref, *refs):
    n = len(cuts)
    sources, targets, vectors = refs[:n], refs[n : 2 * n], refs[2 * n : 2 * n + len(sizes)]
    low, wide, isem, osem = refs[-2 * n - 2 : -n - 2], refs[-n - 2 : -2], refs[-2], refs[-1]
    loads, saves = [], []
    for w, parts in enumerate(cuts):
        size = sources[w].shape[0] // parts
        for j in range(parts):
            rows = pl.ds(j * size, size)
            at = len(loads)
            loads.append(pltpu.make_async_copy(sources[w].at[rows], low[w].at[rows], isem.at[at]))
            saves.append(
                (w, rows, pltpu.make_async_copy(wide[w].at[rows], targets[w].at[rows], osem.at[at]))
            )
    for load in loads:
        load.start()
    at = 0
    for ref, size in zip(vectors, sizes):
        ref[...] = flat_ref[:, at : at + size].reshape(size)
        at += size
    for load, (w, rows, save) in zip(loads, saves):
        load.wait()
        wide[w][rows] = low[w][rows].astype(wide[w].dtype)
        save.start()
    for _, _, save in saves:
        save.wait()


def widen_all(flat, arrays, same, sizes):
    shape = jax.ShapeDtypeStruct
    arrays = (*arrays, same)
    types = [F32] * (len(arrays) - 1) + [same.dtype]
    dma = pltpu.SemaphoreType.DMA
    cuts = [next(n for n in (4, 3, 2, 1) if a.shape[0] % (16 * n) == 0 or n == 1) for a in arrays]
    return pl.pallas_call(
        lambda *refs: widen_kernel(sizes, cuts, *refs),
        out_shape=tuple(shape(a.shape, t) for a, t in zip(arrays, types))
        + tuple(shape((size,), F32) for size in sizes),
        in_specs=[VMEM_SPEC] + [ANY_SPEC] * len(arrays),
        out_specs=(ANY_SPEC,) * len(arrays) + (VMEM_SPEC,) * len(sizes),
        scratch_shapes=[pltpu.VMEM(a.shape, BF16) for a in arrays]
        + [pltpu.VMEM(a.shape, t) for a, t in zip(arrays, types)]
        + [dma((sum(cuts),)), dma((sum(cuts),))],
        compiler_params=pltpu.CompilerParams(vmem_limit_bytes=VMEM_LIMIT),
    )(flat, *arrays)


def on_device(
    tokens, doc_ids, qkv_weight, qv_bias, out_weight, out_bias, mid_gain, mid_shift,
    up_weight, up_bias, down_weight, down_bias, end_gain, end_shift, out_grad,
):
    width, hidden = tokens.shape[2], up_weight.shape[1]
    ring, shards = lax.axis_size("rep"), lax.axis_size("shard")
    levels = ring // 4
    sub = levels // GROUPS
    x = tokens[0]
    small = (qv_bias, out_bias, mid_gain, mid_shift, up_bias, down_bias, end_gain, end_shift)
    sizes = [v.shape[0] for v in small]
    own = (out_weight, up_weight, down_weight)
    att, flat, w_group, lse, o, q, k, kt, vt, x_rows, *full = forward_all(
        x, qkv_weight, doc_ids, list(small), own, ((2, 1, True), (0, 1, False), (1, 2, False)), ring, shards, 0
    )
    down_chunks = 6 if hidden % (6 * shards * ring * 16) == 0 else 1
    layer_out, gat, mid, flat, down, up, out = mlp_all(
        att, x, out_grad[0], flat, own, full, sizes, shards, levels, down_chunks, 6
    )
    input_grad, down, up, out, qkv, flat = tail_all(
        gat, lse, w_group, mid, flat, (q, k, kt, vt, o, x_rows), (down, up, out), sizes[0],
        ring, shards, 1,
    )
    down = down.reshape(-1, width)
    if up.ndim > 2:
        up = up.reshape(12, width // shards, -1).transpose(1, 0, 2).reshape(-1, hidden)
        out = out.reshape(2, width // shards, -1).transpose(1, 0, 2).reshape(-1, width)
    if qkv.ndim > 2:
        qkv = qkv.reshape(4 * QKV_CHUNKS, GROUPS, sub, -1, 3, SLAB).transpose(0, 2, 3, 4, 1, 5)
        qkv = qkv.reshape(-1, 3 * width)
    down, up, out, qkv, input_grad, *totals = widen_all(flat, (down, up, out, qkv), input_grad, sizes)
    return (
        layer_out[None], input_grad[None], qkv, totals[0], out, totals[1], totals[2],
        totals[3], up, totals[4], down, totals[5], totals[6], totals[7],
    )


def solution(mesh):
    rows = P("shard", None)
    flat = P("shard")
    acts = P("shard", "rep", None)
    in_specs = (
        acts, rows, rows, flat, rows, flat, flat, flat, rows, flat, rows, flat, flat, flat, acts
    )
    out_specs = (acts, acts, rows, flat, rows, flat, flat, flat, rows, flat, rows, flat, flat, flat)
    return jax.shard_map(
        on_device, mesh=mesh, in_specs=in_specs, out_specs=out_specs, check_vma=False
    )
```
